32 devices in a mesh: row: 8 (over y, x, core), col: 4 (over z).
Axes of the slice: x: 2, y: 2, z: 4, core: 2. Of those that a mesh axis runs over, the one named last changes fastest.
Arguments:
- amplitudes: bfloat16 [100, 100, 768], P(None, None, 'col'), may hold values from -6 to 6
- integrals: bfloat16 [768, 65536], P('col', 'row'), may hold values from -0.15625 to 0.15625
- blocks: int32 [8, 2], replicated, may hold values from 0 to 49, as said below
Outputs:
- residual: bfloat16 [32, 65536], P('col', 'row')
The draws below stay inside these ranges and needn't reach their ends.
Inputs may be any that keep to these rules, and one draw needn't show every extreme that they name: `blocks`: each row is a block pair (I, J) with I <= J, all rows distinct; the pair (0, 49) is always among them.
All inputs are finite; a program needn't handle non-finite values.
Results may differ from the reference program's by a relative error of at most 0.001.
Values may be sent and summed in bfloat16 or wider, within the bound.
A program may use at most 128 MiB of HBM per device.

```python
import jax
import jax.numpy as jnp
import numpy as np
from jax import lax

OCC = 100
OB = 2
NBO = 50
K = 768
AW = 256
NBLK = 8


def draw_blocks(key, part):
    pair_table = np.array([[upper, lower] for upper in range(NBO) for lower in range(upper, NBO)], dtype=np.int32)
    corner = NBO - 1
    count_all = pair_table.shape[0]
    ordering = np.concatenate([np.array([corner]), np.arange(corner), np.arange(corner + 1, count_all)])
    pair_table = jnp.asarray(pair_table[ordering])
    remaining = jax.random.permutation(jax.random.fold_in(key, 11), count_all - 1)[:NBLK - 1] + 1
    chosen = jnp.concatenate([jnp.zeros((1,), jnp.int32), remaining.astype(jnp.int32)])
    chosen = jax.random.permutation(jax.random.fold_in(key, 12), chosen)
    return pair_table[chosen].astype(jnp.int32)


def levels(rng, shape, pieces, least, high):
    def one(dim, shards_of):
        steps = jax.random.uniform(jax.random.fold_in(jax.random.fold_in(rng, 6), dim), (shards_of,), jnp.float32, least / len(pieces), high / len(pieces))
        return jnp.repeat(jnp.exp(steps), shape[dim] // shards_of).reshape((-1,) + (1,) * (len(shape) - dim - 1))

    level = one(*pieces[0])
    for cut in pieces[1:]:
        level = level * one(*cut)
    return level


def noise(own_key, dims, deviation, bound, split=(), kind=jnp.bfloat16):
    entries = jax.random.normal(own_key, dims, jnp.float32) * deviation
    if len(split) > 0:
        entries = levels(own_key, dims, split, -0.22, 0.18) * entries
    return jnp.clip(entries, min=-bound, max=bound).astype(kind)


def setup_inputs(seed: int = 0) -> dict:
    streams_of = jax.random.split(jax.random.key(seed), 4)
    amplitudes = noise(streams_of[0], (OCC, OCC, K), 1.0, 6.0, ((2, 4),))
    integrals = noise(streams_of[1], (K, AW * AW), (2 * K) ** -0.5, 0.15625, ((0, 4), (1, 8)))
    blocks = draw_blocks(jax.random.fold_in(streams_of[3], 71), 0)
    return dict(amplitudes=amplitudes, integrals=integrals, blocks=blocks)


def pick_rows(amplitudes, blocks):
    panel_width = amplitudes.shape[2]

    def one_block(pair_index):
        first_row = pair_index[0] * OB
        second_row = pair_index[1] * OB
        anchor = jnp.zeros((), jnp.int32)
        direct_rows = lax.dynamic_slice(amplitudes, (first_row, second_row, anchor), (OB, OB, panel_width))
        swapped_rows = lax.dynamic_slice(amplitudes, (second_row, first_row, anchor), (OB, OB, panel_width))
        return direct_rows.reshape(OB * OB, panel_width), jnp.swapaxes(swapped_rows, 0, 1).reshape(OB * OB, panel_width)

    direct_rows, swapped_rows = jax.vmap(one_block)(blocks)
    return direct_rows.reshape(-1, panel_width), swapped_rows.reshape(-1, panel_width)


def reference(amplitudes, integrals, blocks):
    forward, mirrored = pick_rows(amplitudes, blocks)
    depth = integrals.shape[0]
    flipped = jnp.swapaxes(integrals.reshape(depth, AW, AW), 1, 2).reshape(depth, AW * AW)
    total = jnp.dot(forward, integrals, preferred_element_type=jnp.float32) + jnp.dot(mirrored, flipped, preferred_element_type=jnp.float32)
    return total.astype(jnp.bfloat16)
```

```python
import functools
import math

import jax
import jax.numpy as jnp
from jax import lax
from jax.experimental import pallas as pl
from jax.experimental.pallas import tpu as pltpu
from jax.sharding import PartitionSpec as P

OB = 2
LANES = 128
CODES = 256.0
SCALE = 256.0 * 127.0
TINY = 1e-30
ROWS = 8
VMEM = 67043328


def ladder_kernel(
    n_row, n_col, a_dev,
    blocks, amp_hbm, int_hbm, out_ref,
    amp, ints, lhs, prod, turned, inbox,
    main_out, rest_out, main_left, rest_left, main_right, rest_right,
    amp_sem, int_sem, x_send, x_recv, r_send, r_recv, l_send, l_recv,
):
    row = lax.axis_index("row")
    col = lax.axis_index("col")
    pairs = lhs.shape[0] // 2
    width = a_dev * n_row
    tiles = width // LANES
    per_tile = LANES // a_dev
    share = pairs // n_col
    groups = share // per_tile
    occ = amp.shape[2]
    n_parts = int_sem.shape[0]
    part = ints.shape[1] // n_parts

    barrier = pltpu.get_barrier_semaphore()

    def greet(p, carry):
        pl.semaphore_signal(barrier, inc=1, device_id={"row": lax.rem(row + p, n_row)})
        return carry

    lax.fori_loop(1, n_row, greet, 0)

    @pl.when(col > 0)
    def _():
        pl.semaphore_signal(barrier, inc=1, device_id={"col": col - 1})

    @pl.when(col < n_col - 1)
    def _():
        pl.semaphore_signal(barrier, inc=1, device_id={"col": col + 1})

    amp_copy = pltpu.make_async_copy(amp_hbm, amp, amp_sem)
    amp_copy.start()
    int_copies = []
    for i in range(n_parts):
        cut = pl.ds(i * part, part)
        copy = pltpu.make_async_copy(int_hbm.at[:, cut], ints.at[:, cut], int_sem.at[i])
        if i < n_parts // 2:
            copy.start()
        int_copies.append(copy)

    amp_copy.wait()
    for copy in int_copies[n_parts // 2:]:
        copy.start()
    spot_row = lax.broadcasted_iota(jnp.int32, (ROWS, occ), 0)
    spot_col = lax.broadcasted_iota(jnp.int32, (ROWS, occ), 1)

    def take(spots, plane):
        hit = jnp.zeros((ROWS, occ), jnp.bool_)
        for at, column in spots:
            hit = hit | ((spot_row == at) & (spot_col == column))
        chosen = jnp.where(hit, 1.0, 0.0).astype(amp.dtype)
        return lax.dot_general(
            chosen, amp[plane], (((1,), (1,)), ((), ())), preferred_element_type=jnp.float32
        )

    per_rows = ROWS // (OB * OB)

    def gather(mirrored):
        for tile in range(pairs // ROWS):
            found = jnp.zeros((ROWS, lhs.shape[1]), jnp.float32)
            for k in range(per_rows):
                upper = blocks[0, tile * per_rows + k] * OB
                lower = blocks[1, tile * per_rows + k] * OB
                base = k * OB * OB
                for m in range(OB):
                    if mirrored:
                        found += take([(base + u * OB + m, upper + u) for u in range(OB)], lower + m)
                    else:
                        found += take([(base + m * OB + v, lower + v) for v in range(OB)], upper + m)
            at = (pairs if mirrored else 0) + tile * ROWS
            lhs[at:at + ROWS, :] = found

    gather(True)

    def multiply(i, first):
        block = lhs[first:first + pairs, :].astype(jnp.bfloat16)

        def one(step, carry):
            a = i * (part // width) + step
            panel = ints[:, pl.ds(pl.multiple_of(a * width, width), width)]
            got = jnp.dot(block, panel, preferred_element_type=jnp.float32)
            for t in range(tiles):
                prod[t, pl.ds(first * a_dev + a, pairs, stride=a_dev), :] = got[:, t * LANES:(t + 1) * LANES]
            return carry

        lax.fori_loop(0, part // width, one, 0, unroll=8)

    for i in range(n_parts):
        int_copies[i].wait()
        multiply(i, pairs)

    n_near = jnp.where(col > 0, 1, 0) + jnp.where(col < n_col - 1, 1, 0)
    pl.semaphore_wait(barrier, n_row - 1 + n_near)

    to_right = n_col - 1 - col
    near = jnp.minimum(col, to_right)
    lone = (jnp.maximum(col, to_right) - near) * groups
    outward = jnp.where(to_right >= col, 1, -1)

    def unit(k):
        rest = jnp.maximum(k - lone, 0)
        distance = near - rest // (2 * groups)
        within = rest % (2 * groups)
        side = jnp.where(within % 2 == 0, -outward, outward)
        is_lone = k < lone
        is_own = distance == 0
        shift = jnp.where(is_lone, outward * (near + (lone - 1 - k) // groups + 1), side * distance)
        g = jnp.where(is_lone, k % groups, jnp.where(is_own, within, within // 2))
        return col + shift, g

    def partner(p):
        if n_row & (n_row - 1):
            return lax.rem(row + p, n_row)
        peer, bit = row, 1
        while bit < n_row:
            if p & bit:
                peer = peer + bit - 2 * bit * ((row // bit) % 2)
            bit *= 2
        return peer

    steps = sorted(range(1, n_row), key=lambda p: (-bin(p // 2).count('1'), p))

    def x_copy(d, g, p):
        peer = partner(p)
        return pltpu.make_async_remote_copy(
            src_ref=turned.at[d * groups + g, pl.ds(pl.multiple_of(peer * a_dev, a_dev), a_dev), :],
            dst_ref=inbox.at[d, g, row],
            send_sem=x_send.at[d, g, p],
            recv_sem=x_recv.at[d, g, p],
            device_id={"row": peer},
        )

    def z_copies(d, g, right):
        send, recv = (r_send, r_recv) if right else (l_send, l_recv)
        main_in, rest_in = (main_left, rest_left) if right else (main_right, rest_right)
        to = col + 1 if right else col - 1
        return [
            pltpu.make_async_remote_copy(
                src_ref=src.at[d, g], dst_ref=dst.at[d, g],
                send_sem=send.at[d, g, i], recv_sem=recv.at[d, g, i],
                device_id={"col": to},
            )
            for i, (src, dst) in enumerate(((main_out, main_in), (rest_out, rest_in)))
        ]

    def held(d, g, t):
        start = pl.multiple_of(d * (share * a_dev) + g * LANES, LANES)
        return prod.at[t, pl.ds(start, LANES)]

    half = tiles // 2

    def add_from(d, g, right):
        for copy in z_copies(d, g, right):
            copy.wait_recv()
        main_in, rest_in = (main_left, rest_left) if right else (main_right, rest_right)
        for t in range(half):
            word = rest_in[d, g, t].astype(jnp.int32).astype(jnp.float32)
            high = jnp.round(word * (1.0 / CODES))
            for place, code in ((t, high), (t + half, word - high * CODES)):
                main = main_in[d, g, place].astype(jnp.float32)
                step = jnp.maximum(jnp.abs(main), TINY) * (1.0 / SCALE)
                here = held(d, g, place)
                here[...] = here[...] + (main + code * step)

    def send_on(d, g, right):
        for t in range(half):
            codes = []
            for place in (t, t + half):
                value = held(d, g, place)[...]
                main = value.astype(jnp.bfloat16)
                main_out[d, g, place] = main
                main = main.astype(jnp.float32)
                codes.append(jnp.round((value - main) * (SCALE / jnp.maximum(jnp.abs(main), TINY))))
            word = codes[0] * CODES + codes[1]
            rest_out[d, g, t] = word.astype(jnp.int32).astype(jnp.int16)
        for copy in z_copies(d, g, right):
            copy.start()

    def turn(k, carry):
        d, g = unit(k)
        start = (pairs + d * share + g * per_tile) * a_dev
        for t in range(tiles):
            block = prod[t, pl.ds(pl.multiple_of(start, LANES), LANES), :]
            turned[d * groups + g, t * LANES:(t + 1) * LANES, :] = block.T

        for p in steps:
            x_copy(d, g, p).start()
        return carry

    lax.fori_loop(0, n_col * groups, turn, 0)

    gather(False)
    for i in range(n_parts):
        multiply(i, 0)

    piece = lax.broadcasted_iota(jnp.int32, (a_dev, LANES), 1) // a_dev

    def combine(k, carry):
        d, g = unit(k)
        inbox[d, g, row] = turned[d * groups + g, pl.ds(pl.multiple_of(row * a_dev, a_dev), a_dev), :]

        for p in steps:
            x_copy(d, g, p).wait_recv()
        for t in range(tiles):
            parts = [inbox[d, g, t * per_tile + j] for j in range(per_tile)]
            sums = []
            for q in range(per_tile):
                merged = pltpu.roll(parts[0], (-q * a_dev) % LANES, 1) if q else parts[0]
                for j in range(1, per_tile):
                    shift = ((j - q) * a_dev) % LANES
                    moved = pltpu.roll(parts[j], shift, 1) if shift else parts[j]
                    merged = jnp.where(piece == j, moved, merged)
                sums.append(merged)
            here = held(d, g, t)
            here[...] = here[...] + jnp.concatenate(sums, axis=0)

        @pl.when(d > col)
        def _():
            @pl.when(col > 0)
            def _():
                add_from(d, g, True)

            send_on(d, g, True)

        @pl.when(d < col)
        def _():
            @pl.when(col < n_col - 1)
            def _():
                add_from(d, g, False)

            send_on(d, g, False)

        return carry

    lax.fori_loop(0, n_col * groups, combine, 0)

    for g in range(groups):
        @pl.when(col > 0)
        def _(g=g):
            add_from(col, g, True)

        @pl.when(col < n_col - 1)
        def _(g=g):
            add_from(col, g, False)

    for t in range(tiles):
        for a in range(a_dev):
            value = prod[t, pl.ds(col * (share * a_dev) + a, share, stride=a_dev), :]
            at = a * width + t * LANES
            out_ref[:, at:at + LANES] = value.astype(out_ref.dtype)

    def finish(d, carry):
        for g in range(groups):
            for p in steps:
                x_copy(d, g, p).wait_send()

            @pl.when(d > col)
            def _(g=g):
                for copy in z_copies(d, g, True):
                    copy.wait_send()

            @pl.when(d < col)
            def _(g=g):
                for copy in z_copies(d, g, False):
                    copy.wait_send()

        return carry

    lax.fori_loop(0, n_col, finish, 0)


def on_device(n_row, n_col, amplitudes, integrals, blocks):
    amplitudes = jnp.swapaxes(amplitudes, 1, 2)
    blocks = blocks.T
    depth, local = integrals.shape
    width = math.isqrt(local * n_row)
    a_dev = width // n_row
    pairs = blocks.shape[1] * OB * OB
    tiles = width // LANES
    share = pairs // n_col
    groups = share * a_dev // LANES
    n_parts = 4
    f32 = jnp.float32
    dma = pltpu.SemaphoreType.DMA
    coded = [
        pltpu.VMEM((n_col, groups, tiles, LANES, LANES), jnp.bfloat16),
        pltpu.VMEM((n_col, groups, tiles // 2, LANES, LANES), jnp.int16),
    ]
    return pl.pallas_call(
        functools.partial(ladder_kernel, n_row, n_col, a_dev),
        out_shape=pltpu.VMEM((share, local), jnp.bfloat16),
        in_specs=[
            pl.BlockSpec(memory_space=pltpu.SMEM),
            pl.BlockSpec(memory_space=pl.ANY),
            pl.BlockSpec(memory_space=pl.ANY),
        ],
        out_specs=pl.BlockSpec(memory_space=pltpu.VMEM),
        scratch_shapes=[
            pltpu.VMEM(amplitudes.shape, amplitudes.dtype),
            pltpu.VMEM(integrals.shape, integrals.dtype),
            pltpu.VMEM((2 * pairs, depth), f32),
            pltpu.VMEM((tiles, 2 * pairs * a_dev, LANES), f32),
            pltpu.VMEM((n_col * groups, width, LANES), f32),
            pltpu.VMEM((n_col, groups, n_row, a_dev, LANES), f32),
            *coded, *coded, *coded,
            dma(()),
            dma((n_parts,)),
            dma((n_col, groups, n_row)),
            dma((n_col, groups, n_row)),
            dma((n_col, groups, 2)),
            dma((n_col, groups, 2)),
            dma((n_col, groups, 2)),
            dma((n_col, groups, 2)),
        ],
        compiler_params=pltpu.CompilerParams(
            collective_id=0, has_side_effects=True, vmem_limit_bytes=VMEM - 4 * share * local * 2
        ),
    )(blocks, amplitudes, integrals)


def solution(mesh):
    return jax.shard_map(
        functools.partial(on_device, mesh.shape["row"], mesh.shape["col"]),
        mesh=mesh,
        in_specs=(P(None, None, "col"), P("col", "row"), P()),
        out_specs=P("col", "row"),
        check_vma=False,
    )
```

```python
import functools
import math

import jax
import jax.numpy as jnp
from jax import lax
from jax.experimental import pallas as pl
from jax.experimental.pallas import tpu as pltpu
from jax.sharding import PartitionSpec as P

OB = 2
LANES = 128
CODE = 32700.0
TINY = 1e-30
ROWS = 8
VMEM = 67043328


def ladder_kernel(
    n_row, n_col, a_dev,
    blocks, amp_hbm, int_hbm, out_ref,
    amp, ints, lhs, prod, turned, inbox, x_top, x_tops,
    code_out, top_out, code_left, top_left, code_right, top_right,
    amp_sem, int_sem, x_send, x_recv, t_send, t_recv, r_send, r_recv, l_send, l_recv,
):
    row = lax.axis_index("row")
    col = lax.axis_index("col")
    pairs = lhs.shape[0] // 2
    width = a_dev * n_row
    tiles = width // LANES
    per_tile = LANES // a_dev
    share = pairs // n_col
    groups = share // per_tile
    occ = amp.shape[2]
    n_parts = int_sem.shape[0]
    part = ints.shape[1] // n_parts

    barrier = pltpu.get_barrier_semaphore()

    def greet(p, carry):
        pl.semaphore_signal(barrier, inc=1, device_id={"row": lax.rem(row + p, n_row)})
        return carry

    lax.fori_loop(1, n_row, greet, 0)

    @pl.when(col > 0)
    def _():
        pl.semaphore_signal(barrier, inc=1, device_id={"col": col - 1})

    @pl.when(col < n_col - 1)
    def _():
        pl.semaphore_signal(barrier, inc=1, device_id={"col": col + 1})

    amp_copy = pltpu.make_async_copy(amp_hbm, amp, amp_sem)
    amp_copy.start()
    int_copies = []
    for i in range(n_parts):
        cut = pl.ds(i * part, part)
        copy = pltpu.make_async_copy(int_hbm.at[:, cut], ints.at[:, cut], int_sem.at[i])
        if i < n_parts // 2:
            copy.start()
        int_copies.append(copy)

    amp_copy.wait()
    for copy in int_copies[n_parts // 2:]:
        copy.start()
    spot_row = lax.broadcasted_iota(jnp.int32, (ROWS, occ), 0)
    spot_col = lax.broadcasted_iota(jnp.int32, (ROWS, occ), 1)

    def take(spots, plane):
        hit = jnp.zeros((ROWS, occ), jnp.bool_)
        for at, column in spots:
            hit = hit | ((spot_row == at) & (spot_col == column))
        chosen = jnp.where(hit, 1.0, 0.0).astype(amp.dtype)
        return lax.dot_general(
            chosen, amp[plane], (((1,), (1,)), ((), ())), preferred_element_type=jnp.float32
        )

    per_rows = ROWS // (OB * OB)

    def gather(mirrored):
        for tile in range(pairs // ROWS):
            found = jnp.zeros((ROWS, lhs.shape[1]), jnp.float32)
            for k in range(per_rows):
                upper = blocks[0, tile * per_rows + k] * OB
                lower = blocks[1, tile * per_rows + k] * OB
                base = k * OB * OB
                for m in range(OB):
                    if mirrored:
                        found += take([(base + u * OB + m, upper + u) for u in range(OB)], lower + m)
                    else:
                        found += take([(base + m * OB + v, lower + v) for v in range(OB)], upper + m)
            at = (pairs if mirrored else 0) + tile * ROWS
            lhs[at:at + ROWS, :] = found

    gather(True)

    def multiply(i, first):
        block = lhs[first:first + pairs, :].astype(jnp.bfloat16)

        def one(step, carry):
            a = i * (part // width) + step
            panel = ints[:, pl.ds(pl.multiple_of(a * width, width), width)]
            got = jnp.dot(block, panel, preferred_element_type=jnp.float32)
            for t in range(tiles):
                prod[t, pl.ds(first * a_dev + a, pairs, stride=a_dev), :] = got[:, t * LANES:(t + 1) * LANES]
            return carry

        lax.fori_loop(0, part // width, one, 0, unroll=8)

    for i in range(n_parts):
        int_copies[i].wait()
        multiply(i, pairs)

    n_near = jnp.where(col > 0, 1, 0) + jnp.where(col < n_col - 1, 1, 0)
    pl.semaphore_wait(barrier, n_row - 1 + n_near)

    to_right = n_col - 1 - col
    near = jnp.minimum(col, to_right)
    lone = (jnp.maximum(col, to_right) - near) * groups
    outward = jnp.where(to_right >= col, 1, -1)

    def unit(k):
        rest = jnp.maximum(k - lone, 0)
        distance = near - rest // (2 * groups)
        within = rest % (2 * groups)
        side = jnp.where(within % 2 == 0, -outward, outward)
        is_lone = k < lone
        is_own = distance == 0
        shift = jnp.where(is_lone, outward * (near + (lone - 1 - k) // groups + 1), side * distance)
        g = jnp.where(is_lone, k % groups, jnp.where(is_own, within, within // 2))
        return col + shift, g

    def partner(p):
        if n_row & (n_row - 1):
            return lax.rem(row + p, n_row)
        peer, bit = row, 1
        while bit < n_row:
            if p & bit:
                peer = peer + bit - 2 * bit * ((row // bit) % 2)
            bit *= 2
        return peer

    steps = sorted(range(1, n_row), key=lambda p: (-bin(p // 2).count('1'), p))

    def x_copy(d, g, p):
        peer = partner(p)
        return pltpu.make_async_remote_copy(
            src_ref=turned.at[d * groups + g, pl.ds(pl.multiple_of(peer * a_dev, a_dev), a_dev), :],
            dst_ref=inbox.at[d, g, row],
            send_sem=x_send.at[d, g, p],
            recv_sem=x_recv.at[d, g, p],
            device_id={"row": peer},
        )

    def top_copy(p):
        return pltpu.make_async_remote_copy(
            src_ref=x_top,
            dst_ref=x_tops.at[row],
            send_sem=t_send.at[p],
            recv_sem=t_recv.at[p],
            device_id={"row": partner(p)},
        )

    def encode(block, top):
        return jnp.round(block * (CODE / top)).astype(jnp.int32).astype(jnp.int16)

    def decode(code, top):
        return code.astype(jnp.int32).astype(jnp.float32) * (top * (1.0 / CODE))

    def top_of(blocks):
        top = jnp.abs(blocks[0])
        for block in blocks[1:]:
            top = jnp.maximum(top, jnp.abs(block))
        return jnp.maximum(jnp.max(top, axis=0, keepdims=True), TINY)

    def z_copies(d, g, right):
        send, recv = (r_send, r_recv) if right else (l_send, l_recv)
        code_in, top_in = (code_left, top_left) if right else (code_right, top_right)
        to = col + 1 if right else col - 1
        return [
            pltpu.make_async_remote_copy(
                src_ref=src.at[d, g], dst_ref=dst.at[d, g],
                send_sem=send.at[d, g, i], recv_sem=recv.at[d, g, i],
                device_id={"col": to},
            )
            for i, (src, dst) in enumerate(((top_out, top_in), (code_out, code_in)))
        ]

    def held(d, g, t):
        start = pl.multiple_of(d * (share * a_dev) + g * LANES, LANES)
        return prod.at[t, pl.ds(start, LANES)]

    def add_from(d, g, right):
        for copy in z_copies(d, g, right):
            copy.wait_recv()
        code_in, top_in = (code_left, top_left) if right else (code_right, top_right)
        top = top_in[d, g]
        for t in range(tiles):
            here = held(d, g, t)
            here[...] = here[...] + decode(code_in[d, g, t], top)

    def send_on(d, g, right):
        top = top_of([held(d, g, t)[...] for t in range(tiles)])
        top_out[d, g] = top
        for t in range(tiles):
            code_out[d, g, t] = encode(held(d, g, t)[...], top)
        for copy in z_copies(d, g, right):
            copy.start()

    def turn(k, carry):
        start = pairs * a_dev + k * LANES
        turns = [prod[t, pl.ds(pl.multiple_of(start, LANES), LANES), :].T for t in range(tiles)]
        top = top_of(turns)
        x_top[pl.ds(k, 1), :] = top
        for t in range(tiles):
            turned[k, t * LANES:(t + 1) * LANES, :] = encode(turns[t], top)
        return carry

    lax.fori_loop(0, n_col * groups, turn, 0)
    for p in steps:
        top_copy(p).start()

    def spread(k, carry):
        d, g = unit(k)
        for p in steps:
            x_copy(d, g, p).start()
        return carry

    lax.fori_loop(0, n_col * groups, spread, 0)

    gather(False)
    for i in range(n_parts):
        multiply(i, 0)

    piece = lax.broadcasted_iota(jnp.int32, (a_dev, LANES), 1) // a_dev

    x_tops[row] = x_top[...]
    for p in steps:
        top_copy(p).wait_recv()

    def combine(k, carry):
        d, g = unit(k)
        inbox[d, g, row] = turned[d * groups + g, pl.ds(pl.multiple_of(row * a_dev, a_dev), a_dev), :]

        for p in steps:
            x_copy(d, g, p).wait_recv()
        for t in range(tiles):
            parts = []
            for j in range(per_tile):
                source = t * per_tile + j
                parts.append(decode(inbox[d, g, source], x_tops[source, pl.ds(d * groups + g, 1), :]))
            sums = []
            for q in range(per_tile):
                merged = pltpu.roll(parts[0], (-q * a_dev) % LANES, 1) if q else parts[0]
                for j in range(1, per_tile):
                    shift = ((j - q) * a_dev) % LANES
                    moved = pltpu.roll(parts[j], shift, 1) if shift else parts[j]
                    merged = jnp.where(piece == j, moved, merged)
                sums.append(merged)
            here = held(d, g, t)
            here[...] = here[...] + jnp.concatenate(sums, axis=0)

        @pl.when(d > col)
        def _():
            @pl.when(col > 0)
            def _():
                add_from(d, g, True)

            send_on(d, g, True)

        @pl.when(d < col)
        def _():
            @pl.when(col < n_col - 1)
            def _():
                add_from(d, g, False)

            send_on(d, g, False)

        return carry

    lax.fori_loop(0, n_col * groups, combine, 0)

    for g in range(groups):
        @pl.when(col > 0)
        def _(g=g):
            add_from(col, g, True)

        @pl.when(col < n_col - 1)
        def _(g=g):
            add_from(col, g, False)

    for t in range(tiles):
        for a in range(a_dev):
            value = prod[t, pl.ds(col * (share * a_dev) + a, share, stride=a_dev), :]
            at = a * width + t * LANES
            out_ref[:, at:at + LANES] = value.astype(out_ref.dtype)

    def finish(d, carry):
        for g in range(groups):
            for p in steps:
                x_copy(d, g, p).wait_send()

            @pl.when(d > col)
            def _(g=g):
                for copy in z_copies(d, g, True):
                    copy.wait_send()

            @pl.when(d < col)
            def _(g=g):
                for copy in z_copies(d, g, False):
                    copy.wait_send()

        return carry

    lax.fori_loop(0, n_col, finish, 0)
    for p in steps:
        top_copy(p).wait_send()


def on_device(n_row, n_col, amplitudes, integrals, blocks):
    amplitudes = jnp.swapaxes(amplitudes, 1, 2)
    blocks = blocks.T
    depth, local = integrals.shape
    width = math.isqrt(local * n_row)
    a_dev = width // n_row
    pairs = blocks.shape[1] * OB * OB
    tiles = width // LANES
    share = pairs // n_col
    groups = share * a_dev // LANES
    n_parts = 4
    f32 = jnp.float32
    dma = pltpu.SemaphoreType.DMA
    coded = [
        pltpu.VMEM((n_col, groups, tiles, LANES, LANES), jnp.int16),
        pltpu.VMEM((n_col, groups, 1, LANES), f32),
    ]
    return pl.pallas_call(
        functools.partial(ladder_kernel, n_row, n_col, a_dev),
        out_shape=pltpu.VMEM((share, local), jnp.bfloat16),
        in_specs=[
            pl.BlockSpec(memory_space=pltpu.SMEM),
            pl.BlockSpec(memory_space=pl.ANY),
            pl.BlockSpec(memory_space=pl.ANY),
        ],
        out_specs=pl.BlockSpec(memory_space=pltpu.VMEM),
        scratch_shapes=[
            pltpu.VMEM(amplitudes.shape, amplitudes.dtype),
            pltpu.VMEM(integrals.shape, integrals.dtype),
            pltpu.VMEM((2 * pairs, depth), f32),
            pltpu.VMEM((tiles, 2 * pairs * a_dev, LANES), f32),
            pltpu.VMEM((n_col * groups, width, LANES), jnp.int16),
            pltpu.VMEM((n_col, groups, n_row, a_dev, LANES), jnp.int16),
            pltpu.VMEM((n_col * groups, LANES), f32),
            pltpu.VMEM((n_row, n_col * groups, LANES), f32),
            *coded, *coded, *coded,
            dma(()),
            dma((n_parts,)),
            dma((n_col, groups, n_row)),
            dma((n_col, groups, n_row)),
            dma((n_row,)),
            dma((n_row,)),
            dma((n_col, groups, 2)),
            dma((n_col, groups, 2)),
            dma((n_col, groups, 2)),
            dma((n_col, groups, 2)),
        ],
        compiler_params=pltpu.CompilerParams(
            collective_id=0, has_side_effects=True, vmem_limit_bytes=VMEM - 4 * share * local * 2
        ),
    )(blocks, amplitudes, integrals)


def solution(mesh):
    return jax.shard_map(
        functools.partial(on_device, mesh.shape["row"], mesh.shape["col"]),
        mesh=mesh,
        in_specs=(P(None, None, "col"), P("col", "row"), P()),
        out_specs=P("col", "row"),
        check_vma=False,
    )
```

```python
import functools
import math

import jax
import jax.numpy as jnp
from jax import lax
from jax.experimental import pallas as pl
from jax.experimental.pallas import tpu as pltpu
from jax.sharding import PartitionSpec as P

OB = 2
LANES = 128
CODE = 32700.0
TINY = 1e-30
ROWS = 8
VMEM = 67043328


def ladder_kernel(
    n_row, n_col, a_dev,
    blocks_hbm, amp_hbm, int_hbm, out_ref,
    blocks, amp, ints, lhs, prod, turned, inbox, peaks, x_top, x_tops,
    code_out, top_out, code_in, top_in,
    block_sem, amp_sem, int_sem, x_send, x_recv, t_send, t_recv, z_send, z_recv,
):
    row = lax.axis_index("row")
    col = lax.axis_index("col")
    pairs = lhs.shape[0] // 2
    width = a_dev * n_row
    tiles = width // LANES
    per_tile = LANES // a_dev
    share = pairs // n_col
    groups = share // per_tile
    units = n_col * groups
    occ = amp.shape[2]
    n_parts = int_sem.shape[0]
    part = ints.shape[1] // n_parts

    block_copy = pltpu.make_async_copy(blocks_hbm, blocks, block_sem)
    block_copy.start()
    amp_copy = pltpu.make_async_copy(amp_hbm, amp, amp_sem)
    amp_copy.start()
    int_copies = []
    for i in range(n_parts):
        cut = pl.ds(i * part, part)
        copy = pltpu.make_async_copy(int_hbm.at[:, cut], ints.at[:, cut], int_sem.at[i])
        copy.start()
        int_copies.append(copy)

    barrier = pltpu.get_barrier_semaphore()

    def greet(p, carry):
        pl.semaphore_signal(barrier, inc=1, device_id={"row": lax.rem(row + p, n_row)})
        return carry

    lax.fori_loop(1, n_row, greet, 0)

    @pl.when(col > 0)
    def _():
        pl.semaphore_signal(barrier, inc=1, device_id={"col": col - 1})

    @pl.when(col < n_col - 1)
    def _():
        pl.semaphore_signal(barrier, inc=1, device_id={"col": col + 1})

    block_copy.wait()
    amp_copy.wait()
    spot_row = lax.broadcasted_iota(jnp.int32, (ROWS, occ), 0)
    spot_col = lax.broadcasted_iota(jnp.int32, (ROWS, occ), 1)

    def take(spots, plane):
        hit = jnp.zeros((ROWS, occ), jnp.bool_)
        for at, column in spots:
            hit = hit | ((spot_row == at) & (spot_col == column))
        chosen = jnp.where(hit, 1.0, 0.0).astype(amp.dtype)
        return lax.dot_general(
            chosen, amp[plane], (((1,), (1,)), ((), ())), preferred_element_type=jnp.float32
        )

    per_rows = ROWS // (OB * OB)

    def gather(mirrored):
        for tile in range(pairs // ROWS):
            found = jnp.zeros((ROWS, lhs.shape[1]), jnp.float32)
            for k in range(per_rows):
                upper = blocks[0, tile * per_rows + k] * OB
                lower = blocks[1, tile * per_rows + k] * OB
                base = k * OB * OB
                for m in range(OB):
                    if mirrored:
                        found += take([(base + u * OB + m, upper + u) for u in range(OB)], lower + m)
                    else:
                        found += take([(base + m * OB + v, lower + v) for v in range(OB)], upper + m)
            at = (pairs if mirrored else 0) + tile * ROWS
            lhs[at:at + ROWS, :] = found

    gather(True)

    def multiply(i, first, peak):
        block = lhs[first:first + pairs, :].astype(jnp.bfloat16)

        def one(step, peak):
            a = i * (part // width) + step
            panel = ints[:, pl.ds(pl.multiple_of(a * width, width), width)]
            got = jnp.dot(block, panel, preferred_element_type=jnp.float32)
            for t in range(tiles):
                piece = got[:, t * LANES:(t + 1) * LANES]
                prod[t, pl.ds(first * a_dev + a, pairs, stride=a_dev), :] = piece
                if peak is not None:
                    peak = jnp.maximum(peak, jnp.abs(piece))
            return peak

        return lax.fori_loop(0, part // width, one, peak, unroll=8)

    peak = jnp.full((pairs, LANES), TINY, jnp.float32)
    for i in range(n_parts):
        int_copies[i].wait()
        peak = multiply(i, pairs, peak)

    peaks[...] = jnp.broadcast_to(jnp.max(peak, axis=1, keepdims=True), peaks.shape)
    spot = lax.broadcasted_iota(jnp.int32, (units, LANES), 1) // a_dev
    table = peaks[pl.ds(0, units, stride=per_tile), :]
    for q in range(1, per_tile):
        table = jnp.where(spot == q, peaks[pl.ds(q, units, stride=per_tile), :], table)
    x_top[...] = table
    x_tops[row] = table

    n_near = jnp.where(col > 0, 1, 0) + jnp.where(col < n_col - 1, 1, 0)
    pl.semaphore_wait(barrier, n_row - 1 + n_near)

    to_right = n_col - 1 - col
    near = jnp.minimum(col, to_right)
    lone = (jnp.maximum(col, to_right) - near) * groups
    outward = jnp.where(to_right >= col, 1, -1)

    def unit(k):
        rest = jnp.maximum(k - lone, 0)
        distance = near - rest // (2 * groups)
        within = rest % (2 * groups)
        side = jnp.where(within % 2 == 0, -outward, outward)
        is_lone = k < lone
        is_own = distance == 0
        shift = jnp.where(is_lone, outward * (near + (lone - 1 - k) // groups + 1), side * distance)
        g = jnp.where(is_lone, k % groups, jnp.where(is_own, within, within // 2))
        return col + shift, g

    def partner(p):
        if n_row & (n_row - 1):
            return lax.rem(row + p, n_row)
        peer, bit = row, 1
        while bit < n_row:
            if p & bit:
                peer = peer + bit - 2 * bit * ((row // bit) % 2)
            bit *= 2
        return peer

    steps = sorted(range(1, n_row), key=lambda p: (-bin(p // 2).count('1'), p))

    def x_copy(u, p):
        peer = partner(p)
        return pltpu.make_async_remote_copy(
            src_ref=turned.at[u, pl.ds(pl.multiple_of(peer * a_dev, a_dev), a_dev), :],
            dst_ref=inbox.at[u * n_row + row],
            send_sem=x_send,
            recv_sem=x_recv.at[u],
            device_id={"row": peer},
        )

    def top_copy(p):
        return pltpu.make_async_remote_copy(
            src_ref=x_top,
            dst_ref=x_tops.at[row],
            send_sem=t_send,
            recv_sem=t_recv,
            device_id={"row": partner(p)},
        )

    def wait_for(ref, start, count, sem):
        landed = ref.at[pl.ds(start, count)]
        pltpu.make_async_copy(landed, landed, sem).wait()

    def encode(block, top):
        return jnp.round(block * (CODE / top)).astype(jnp.int32).astype(jnp.int16)

    def decode(code, top):
        return code.astype(jnp.int32).astype(jnp.float32) * (top * (1.0 / CODE))

    def top_of(blocks):
        top = jnp.abs(blocks[0])
        for block in blocks[1:]:
            top = jnp.maximum(top, jnp.abs(block))
        return jnp.maximum(jnp.max(top, axis=0, keepdims=True), TINY)

    def z_copies(d, g, to):
        u = d * groups + g
        slot = jnp.where((d == to) & (to < col), n_col, d) * groups + g
        return [
            pltpu.make_async_remote_copy(
                src_ref=src.at[u], dst_ref=dst.at[slot],
                send_sem=z_send.at[i], recv_sem=z_recv.at[i, slot],
                device_id={"col": to},
            )
            for i, (src, dst) in enumerate(((top_out, top_in), (code_out, code_in)))
        ]

    def held(d, g, t):
        start = pl.multiple_of(d * (share * a_dev) + g * LANES, LANES)
        return prod.at[t, pl.ds(start, LANES)]

    def add_from(d, g, slot):
        wait_for(top_in, slot, 1, z_recv.at[0, slot])
        wait_for(code_in, slot, 1, z_recv.at[1, slot])
        top = top_in[slot]
        for t in range(tiles):
            here = held(d, g, t)
            here[...] = here[...] + decode(code_in[slot, t], top)

    def send_on(d, g, to):
        u = d * groups + g
        top = top_of([held(d, g, t)[...] for t in range(tiles)])
        top_out[u] = top
        for t in range(tiles):
            code_out[u, t] = encode(held(d, g, t)[...], top)
        for copy in z_copies(d, g, to):
            copy.start()

    for p in steps:
        top_copy(p).start()

    def turn(k, carry):
        d, g = unit(k)
        u = d * groups + g
        start = pl.multiple_of((pairs * a_dev) + u * LANES, LANES)
        top = x_top[pl.ds(u, 1), :]
        for t in range(tiles):
            turned[u, t * LANES:(t + 1) * LANES, :] = encode(prod[t, pl.ds(start, LANES), :].T, top)
        for p in steps:
            x_copy(u, p).start()
        return carry

    lax.fori_loop(0, units, turn, 0)

    gather(False)
    for i in range(n_parts):
        multiply(i, 0, None)

    piece = lax.broadcasted_iota(jnp.int32, (a_dev, LANES), 1) // a_dev

    wait_for(x_tops, 0, n_row - 1, t_recv)

    def combine(k, carry):
        d, g = unit(k)
        u = d * groups + g
        inbox[u * n_row + row] = turned[u, pl.ds(pl.multiple_of(row * a_dev, a_dev), a_dev), :]
        wait_for(inbox, u * n_row, n_row - 1, x_recv.at[u])
        for t in range(tiles):
            parts = []
            for j in range(per_tile):
                source = t * per_tile + j
                parts.append(decode(inbox[u * n_row + source], x_tops[source, pl.ds(u, 1), :]))
            sums = []
            for q in range(per_tile):
                merged = pltpu.roll(parts[0], (-q * a_dev) % LANES, 1) if q else parts[0]
                for j in range(1, per_tile):
                    shift = ((j - q) * a_dev) % LANES
                    moved = pltpu.roll(parts[j], shift, 1) if shift else parts[j]
                    merged = jnp.where(piece == j, moved, merged)
                sums.append(merged)
            here = held(d, g, t)
            here[...] = here[...] + jnp.concatenate(sums, axis=0)

        @pl.when(d > col)
        def _():
            @pl.when(col > 0)
            def _():
                add_from(d, g, u)

            send_on(d, g, col + 1)

        @pl.when(d < col)
        def _():
            @pl.when(col < n_col - 1)
            def _():
                add_from(d, g, u)

            send_on(d, g, col - 1)

        return carry

    lax.fori_loop(0, units, combine, 0)

    for g in range(groups):
        @pl.when(col > 0)
        def _(g=g):
            add_from(col, g, col * groups + g)

        @pl.when(col < n_col - 1)
        def _(g=g):
            add_from(col, g, n_col * groups + g)

    for t in range(tiles):
        for a in range(a_dev):
            value = prod[t, pl.ds(col * (share * a_dev) + a, share, stride=a_dev), :]
            at = a * width + t * LANES
            out_ref[:, at:at + LANES] = value.astype(out_ref.dtype)

    sent = (n_col - 1) * groups
    wait_for(x_tops, 0, n_row - 1, t_send)
    wait_for(inbox, 0, units * (n_row - 1), x_send)
    if sent:
        wait_for(top_out, 0, sent, z_send.at[0])
        wait_for(code_out, 0, sent, z_send.at[1])


def on_device(n_row, n_col, amplitudes, integrals, blocks):
    amplitudes = jnp.swapaxes(amplitudes, 1, 2)
    blocks = blocks.T
    depth, local = integrals.shape
    width = math.isqrt(local * n_row)
    a_dev = width // n_row
    pairs = blocks.shape[1] * OB * OB
    tiles = width // LANES
    share = pairs // n_col
    groups = share * a_dev // LANES
    n_parts = 4
    f32 = jnp.float32
    dma = pltpu.SemaphoreType.DMA
    units = n_col * groups
    slots = units + groups
    return pl.pallas_call(
        functools.partial(ladder_kernel, n_row, n_col, a_dev),
        out_shape=pltpu.VMEM((share, local), jnp.bfloat16),
        in_specs=[
            pl.BlockSpec(memory_space=pl.ANY),
            pl.BlockSpec(memory_space=pl.ANY),
            pl.BlockSpec(memory_space=pl.ANY),
        ],
        out_specs=pl.BlockSpec(memory_space=pltpu.VMEM),
        scratch_shapes=[
            pltpu.SMEM(blocks.shape, blocks.dtype),
            pltpu.VMEM(amplitudes.shape, amplitudes.dtype),
            pltpu.VMEM(integrals.shape, integrals.dtype),
            pltpu.VMEM((2 * pairs, depth), f32),
            pltpu.VMEM((tiles, 2 * pairs * a_dev, LANES), f32),
            pltpu.VMEM((units, width, LANES), jnp.int16),
            pltpu.VMEM((units * n_row, a_dev, LANES), jnp.int16),
            pltpu.VMEM((pairs, LANES), f32),
            pltpu.VMEM((units, LANES), f32),
            pltpu.VMEM((n_row, units, LANES), f32),
            pltpu.VMEM((units, tiles, LANES, LANES), jnp.int16),
            pltpu.VMEM((units, 1, LANES), f32),
            pltpu.VMEM((slots, tiles, LANES, LANES), jnp.int16),
            pltpu.VMEM((slots, 1, LANES), f32),
            dma(()),
            dma(()),
            dma((n_parts,)),
            dma(()),
            dma((units,)),
            dma(()),
            dma(()),
            dma((2,)),
            dma((2, slots)),
        ],
        compiler_params=pltpu.CompilerParams(
            collective_id=0, has_side_effects=True, vmem_limit_bytes=VMEM - 4 * share * local * 2
        ),
    )(blocks, amplitudes, integrals)


def solution(mesh):
    return jax.shard_map(
        functools.partial(on_device, mesh.shape["row"], mesh.shape["col"]),
        mesh=mesh,
        in_specs=(P(None, None, "col"), P("col", "row"), P()),
        out_specs=P("col", "row"),
        check_vma=False,
    )
```

```python
import functools
import math

import jax
import jax.numpy as jnp
from jax import lax
from jax.experimental import pallas as pl
from jax.experimental.pallas import tpu as pltpu
from jax.sharding import PartitionSpec as P

OB = 2
LANES = 128
CODE = 32700.0
TINY = 1e-30
ROWS = 8
VMEM = 67043328


def ladder_kernel(
    n_row, n_col, a_dev,
    blocks_hbm, amp_hbm, int_hbm, out_ref,
    blocks, amp, ints, lhs, prod, turned, inbox, peaks, x_top, x_tops,
    code_out, top_out, code_in, top_in,
    block_sem, amp_sem, int_sem, x_send, x_recv, t_send, t_recv, z_send, z_recv,
):
    row = lax.axis_index("row")
    col = lax.axis_index("col")
    pairs = lhs.shape[0] // 2
    width = a_dev * n_row
    tiles = width // LANES
    per_tile = LANES // a_dev
    share = pairs // n_col
    groups = share // per_tile
    units = n_col * groups
    occ = amp.shape[2]
    n_parts = int_sem.shape[0]
    part = ints.shape[1] // n_parts

    block_copy = pltpu.make_async_copy(blocks_hbm, blocks, block_sem)
    block_copy.start()
    amp_copy = pltpu.make_async_copy(amp_hbm, amp, amp_sem)
    amp_copy.start()
    int_copies = []
    for i in range(n_parts):
        cut = pl.ds(i * part, part)
        copy = pltpu.make_async_copy(int_hbm.at[:, cut], ints.at[:, cut], int_sem.at[i])
        copy.start()
        int_copies.append(copy)

    barrier = pltpu.get_barrier_semaphore()

    def greet(p, carry):
        pl.semaphore_signal(barrier, inc=1, device_id={"row": lax.rem(row + p, n_row)})
        return carry

    lax.fori_loop(1, n_row, greet, 0)

    @pl.when(col > 0)
    def _():
        pl.semaphore_signal(barrier, inc=1, device_id={"col": col - 1})

    @pl.when(col < n_col - 1)
    def _():
        pl.semaphore_signal(barrier, inc=1, device_id={"col": col + 1})

    block_copy.wait()
    amp_copy.wait()
    spot_row = lax.broadcasted_iota(jnp.int32, (ROWS, occ), 0)
    spot_col = lax.broadcasted_iota(jnp.int32, (ROWS, occ), 1)

    def take(spots, plane):
        hit = jnp.zeros((ROWS, occ), jnp.bool_)
        for at, column in spots:
            hit = hit | ((spot_row == at) & (spot_col == column))
        chosen = jnp.where(hit, 1.0, 0.0).astype(amp.dtype)
        return lax.dot_general(
            chosen, amp[plane], (((1,), (1,)), ((), ())), preferred_element_type=jnp.float32
        )

    per_rows = ROWS // (OB * OB)

    def gather(mirrored):
        for tile in range(pairs // ROWS):
            found = jnp.zeros((ROWS, lhs.shape[1]), jnp.float32)
            for k in range(per_rows):
                upper = blocks[0, tile * per_rows + k] * OB
                lower = blocks[1, tile * per_rows + k] * OB
                base = k * OB * OB
                for m in range(OB):
                    if mirrored:
                        found += take([(base + u * OB + m, upper + u) for u in range(OB)], lower + m)
                    else:
                        found += take([(base + m * OB + v, lower + v) for v in range(OB)], upper + m)
            at = (pairs if mirrored else 0) + tile * ROWS
            lhs[at:at + ROWS, :] = found

    gather(True)

    def multiply(i, first, peak):
        block = lhs[first:first + pairs, :].astype(jnp.bfloat16)

        def one(step, peak):
            a = i * (part // width) + step
            panel = ints[:, pl.ds(pl.multiple_of(a * width, width), width)]
            got = jnp.dot(block, panel, preferred_element_type=jnp.float32)
            for t in range(tiles):
                piece = got[:, t * LANES:(t + 1) * LANES]
                prod[t, pl.ds(first * a_dev + a, pairs, stride=a_dev), :] = piece
                if peak is not None:
                    peak = jnp.maximum(peak, jnp.abs(piece))
            return peak

        return lax.fori_loop(0, part // width, one, peak, unroll=8)

    peak = jnp.full((pairs, LANES), TINY, jnp.float32)
    for i in range(n_parts):
        int_copies[i].wait()
        peak = multiply(i, pairs, peak)

    peaks[...] = jnp.broadcast_to(jnp.max(peak, axis=1, keepdims=True), peaks.shape)
    spot = lax.broadcasted_iota(jnp.int32, (units, LANES), 1) // a_dev
    table = peaks[pl.ds(0, units, stride=per_tile), :]
    for q in range(1, per_tile):
        table = jnp.where(spot == q, peaks[pl.ds(q, units, stride=per_tile), :], table)
    x_top[...] = table
    x_tops[row] = table

    n_near = jnp.where(col > 0, 1, 0) + jnp.where(col < n_col - 1, 1, 0)
    pl.semaphore_wait(barrier, n_row - 1 + n_near)

    to_right = n_col - 1 - col
    near = jnp.minimum(col, to_right)
    lone = (jnp.maximum(col, to_right) - near) * groups
    outward = jnp.where(to_right >= col, 1, -1)

    def unit(k):
        rest = jnp.maximum(k - lone, 0)
        distance = near - rest // (2 * groups)
        within = rest % (2 * groups)
        side = jnp.where(within % 2 == 0, -outward, outward)
        is_lone = k < lone
        is_own = distance == 0
        shift = jnp.where(is_lone, outward * (near + (lone - 1 - k) // groups + 1), side * distance)
        g = jnp.where(is_lone, k % groups, jnp.where(is_own, within, within // 2))
        up = to_right * groups
        d = jnp.where(k < up, n_col - 1 - k // groups, (k - up) // groups)
        first_up = to_right > col
        return jnp.where(first_up, d, col + shift), jnp.where(first_up, k % groups, g)

    def partner(p):
        if n_row & (n_row - 1):
            return lax.rem(row + p, n_row)
        peer, bit = row, 1
        while bit < n_row:
            if p & bit:
                peer = peer + bit - 2 * bit * ((row // bit) % 2)
            bit *= 2
        return peer

    steps = sorted(range(1, n_row), key=lambda p: (-bin(p // 2).count('1'), p))

    def x_copy(u, p):
        peer = partner(p)
        return pltpu.make_async_remote_copy(
            src_ref=turned.at[u, pl.ds(pl.multiple_of(peer * a_dev, a_dev), a_dev), :],
            dst_ref=inbox.at[u * n_row + row],
            send_sem=x_send,
            recv_sem=x_recv.at[u],
            device_id={"row": peer},
        )

    def top_copy(p):
        return pltpu.make_async_remote_copy(
            src_ref=x_top,
            dst_ref=x_tops.at[row],
            send_sem=t_send,
            recv_sem=t_recv,
            device_id={"row": partner(p)},
        )

    def wait_for(ref, start, count, sem):
        landed = ref.at[pl.ds(start, count)]
        pltpu.make_async_copy(landed, landed, sem).wait()

    def encode(block, top):
        return jnp.round(block * (CODE / top)).astype(jnp.int32).astype(jnp.int16)

    def decode(code, top):
        return code.astype(jnp.int32).astype(jnp.float32) * (top * (1.0 / CODE))

    def top_of(blocks):
        top = jnp.abs(blocks[0])
        for block in blocks[1:]:
            top = jnp.maximum(top, jnp.abs(block))
        return jnp.maximum(jnp.max(top, axis=0, keepdims=True), TINY)

    def z_copies(d, g, t, to):
        u = d * groups + g
        slot = jnp.where((d == to) & (to < col), n_col, d) * groups + g
        return [
            pltpu.make_async_remote_copy(
                src_ref=src.at[u * tiles + t], dst_ref=dst.at[slot * tiles + t],
                send_sem=z_send.at[i], recv_sem=z_recv.at[i, slot * tiles + t],
                device_id={"col": to},
            )
            for i, (src, dst) in enumerate(((top_out, top_in), (code_out, code_in)))
        ]

    def held(d, g, t):
        start = pl.multiple_of(d * (share * a_dev) + g * LANES, LANES)
        return prod.at[t, pl.ds(start, LANES)]

    def add_from(d, g, t, slot):
        at = slot * tiles + t
        wait_for(top_in, at, 1, z_recv.at[0, at])
        wait_for(code_in, at, 1, z_recv.at[1, at])
        here = held(d, g, t)
        here[...] = here[...] + decode(code_in[at], top_in[at])

    def send_on(d, g, t, to):
        at = (d * groups + g) * tiles + t
        block = held(d, g, t)[...]
        top = top_of([block])
        top_out[at] = top
        code_out[at] = encode(block, top)
        for copy in z_copies(d, g, t, to):
            copy.start()

    for p in steps:
        top_copy(p).start()

    def turn(k, carry):
        d, g = unit(k)
        u = d * groups + g
        start = pl.multiple_of((pairs * a_dev) + u * LANES, LANES)
        top = x_top[pl.ds(u, 1), :]
        for t in range(tiles):
            turned[u, t * LANES:(t + 1) * LANES, :] = encode(prod[t, pl.ds(start, LANES), :].T, top)
        for p in steps:
            x_copy(u, p).start()
        return carry

    lax.fori_loop(0, units, turn, 0)

    gather(False)
    for i in range(n_parts):
        multiply(i, 0, None)

    piece = lax.broadcasted_iota(jnp.int32, (a_dev, LANES), 1) // a_dev

    wait_for(x_tops, 0, n_row - 1, t_recv)

    def combine(k, carry):
        d, g = unit(k)
        u = d * groups + g
        inbox[u * n_row + row] = turned[u, pl.ds(pl.multiple_of(row * a_dev, a_dev), a_dev), :]
        wait_for(inbox, u * n_row, n_row - 1, x_recv.at[u])
        for t in range(tiles):
            parts = []
            for j in range(per_tile):
                source = t * per_tile + j
                parts.append(decode(inbox[u * n_row + source], x_tops[source, pl.ds(u, 1), :]))
            sums = []
            for q in range(per_tile):
                merged = pltpu.roll(parts[0], (-q * a_dev) % LANES, 1) if q else parts[0]
                for j in range(1, per_tile):
                    shift = ((j - q) * a_dev) % LANES
                    moved = pltpu.roll(parts[j], shift, 1) if shift else parts[j]
                    merged = jnp.where(piece == j, moved, merged)
                sums.append(merged)
            here = held(d, g, t)
            here[...] = here[...] + jnp.concatenate(sums, axis=0)

        @pl.when(d > col)
        def _():
            for t in range(tiles):
                @pl.when(col > 0)
                def _(t=t):
                    add_from(d, g, t, u)

                send_on(d, g, t, col + 1)

        @pl.when(d < col)
        def _():
            for t in range(tiles):
                @pl.when(col < n_col - 1)
                def _(t=t):
                    add_from(d, g, t, u)

                send_on(d, g, t, col - 1)

        return carry

    lax.fori_loop(0, units, combine, 0)

    for g in range(groups):
        for t in range(tiles):
            @pl.when(col > 0)
            def _(g=g, t=t):
                add_from(col, g, t, col * groups + g)

            @pl.when(col < n_col - 1)
            def _(g=g, t=t):
                add_from(col, g, t, n_col * groups + g)

    for t in range(tiles):
        for a in range(a_dev):
            value = prod[t, pl.ds(col * (share * a_dev) + a, share, stride=a_dev), :]
            at = a * width + t * LANES
            out_ref[:, at:at + LANES] = value.astype(out_ref.dtype)

    sent = (n_col - 1) * groups * tiles
    wait_for(x_tops, 0, n_row - 1, t_send)
    wait_for(inbox, 0, units * (n_row - 1), x_send)
    if sent:
        wait_for(top_out, 0, sent, z_send.at[0])
        wait_for(code_out, 0, sent, z_send.at[1])


def on_device(n_row, n_col, amplitudes, integrals, blocks):
    amplitudes = jnp.swapaxes(amplitudes, 1, 2)
    blocks = blocks.T
    depth, local = integrals.shape
    width = math.isqrt(local * n_row)
    a_dev = width // n_row
    pairs = blocks.shape[1] * OB * OB
    tiles = width // LANES
    share = pairs // n_col
    groups = share * a_dev // LANES
    n_parts = 4
    f32 = jnp.float32
    dma = pltpu.SemaphoreType.DMA
    units = n_col * groups
    slots = (units + groups) * tiles
    return pl.pallas_call(
        functools.partial(ladder_kernel, n_row, n_col, a_dev),
        out_shape=pltpu.VMEM((share, local), jnp.bfloat16),
        in_specs=[
            pl.BlockSpec(memory_space=pl.ANY),
            pl.BlockSpec(memory_space=pl.ANY),
            pl.BlockSpec(memory_space=pl.ANY),
        ],
        out_specs=pl.BlockSpec(memory_space=pltpu.VMEM),
        scratch_shapes=[
            pltpu.SMEM(blocks.shape, blocks.dtype),
            pltpu.VMEM(amplitudes.shape, amplitudes.dtype),
            pltpu.VMEM(integrals.shape, integrals.dtype),
            pltpu.VMEM((2 * pairs, depth), f32),
            pltpu.VMEM((tiles, 2 * pairs * a_dev, LANES), f32),
            pltpu.VMEM((units, width, LANES), jnp.int16),
            pltpu.VMEM((units * n_row, a_dev, LANES), jnp.int16),
            pltpu.VMEM((pairs, LANES), f32),
            pltpu.VMEM((units, LANES), f32),
            pltpu.VMEM((n_row, units, LANES), f32),
            pltpu.VMEM((units * tiles, LANES, LANES), jnp.int16),
            pltpu.VMEM((units * tiles, 1, LANES), f32),
            pltpu.VMEM((slots, LANES, LANES), jnp.int16),
            pltpu.VMEM((slots, 1, LANES), f32),
            dma(()),
            dma(()),
            dma((n_parts,)),
            dma(()),
            dma((units,)),
            dma(()),
            dma(()),
            dma((2,)),
            dma((2, slots)),
        ],
        compiler_params=pltpu.CompilerParams(
            collective_id=0, has_side_effects=True, vmem_limit_bytes=VMEM - 4 * share * local * 2
        ),
    )(blocks, amplitudes, integrals)


def solution(mesh):
    return jax.shard_map(
        functools.partial(on_device, mesh.shape["row"], mesh.shape["col"]),
        mesh=mesh,
        in_specs=(P(None, None, "col"), P("col", "row"), P()),
        out_specs=P("col", "row"),
        check_vma=False,
    )
```

```python
import functools
import math

import jax
import jax.numpy as jnp
from jax import lax
from jax.experimental import pallas as pl
from jax.experimental.pallas import tpu as pltpu
from jax.sharding import PartitionSpec as P

OB = 2
LANES = 128
CODE = 32700.0
TINY = 1e-30
ROWS = 8
VMEM = 67043328


def ladder_kernel(
    n_row, n_col, a_dev,
    blocks_hbm, amp_hbm, int_hbm, out_ref,
    blocks, amp, ints, lhs, prod, turned, inbox, peaks, x_top, x_tops,
    code_out, top_out, code_in, top_in,
    block_sem, amp_sem, int_sem, x_send, x_recv, t_send, t_recv, z_send, z_recv,
):
    row = lax.axis_index("row")
    col = lax.axis_index("col")
    pairs = lhs.shape[0] // 2
    width = a_dev * n_row
    tiles = width // LANES
    per_tile = LANES // a_dev
    share = pairs // n_col
    groups = share // per_tile
    units = n_col * groups
    occ = amp.shape[2]
    n_parts = int_sem.shape[0]
    part = ints.shape[1] // n_parts

    block_copy = pltpu.make_async_copy(blocks_hbm, blocks, block_sem)
    block_copy.start()
    amp_copy = pltpu.make_async_copy(amp_hbm, amp, amp_sem)
    amp_copy.start()
    int_copies = []
    for i in range(n_parts):
        cut = pl.ds(i * part, part)
        copy = pltpu.make_async_copy(int_hbm.at[:, cut], ints.at[:, cut], int_sem.at[i])
        copy.start()
        int_copies.append(copy)

    barrier = pltpu.get_barrier_semaphore()

    def greet(p, carry):
        pl.semaphore_signal(barrier, inc=1, device_id={"row": lax.rem(row + p, n_row)})
        return carry

    lax.fori_loop(1, n_row, greet, 0)

    def greet_col(p, carry):
        pl.semaphore_signal(barrier, inc=1, device_id={"col": lax.rem(col + p, n_col)})
        return carry

    lax.fori_loop(1, n_col, greet_col, 0)

    block_copy.wait()
    amp_copy.wait()
    spot_row = lax.broadcasted_iota(jnp.int32, (ROWS, occ), 0)
    spot_col = lax.broadcasted_iota(jnp.int32, (ROWS, occ), 1)

    def take(spots, plane):
        hit = jnp.zeros((ROWS, occ), jnp.bool_)
        for at, column in spots:
            hit = hit | ((spot_row == at) & (spot_col == column))
        chosen = jnp.where(hit, 1.0, 0.0).astype(amp.dtype)
        return lax.dot_general(
            chosen, amp[plane], (((1,), (1,)), ((), ())), preferred_element_type=jnp.float32
        )

    per_rows = ROWS // (OB * OB)

    def gather(mirrored):
        for tile in range(pairs // ROWS):
            found = jnp.zeros((ROWS, lhs.shape[1]), jnp.float32)
            for k in range(per_rows):
                upper = blocks[0, tile * per_rows + k] * OB
                lower = blocks[1, tile * per_rows + k] * OB
                base = k * OB * OB
                for m in range(OB):
                    if mirrored:
                        found += take([(base + u * OB + m, upper + u) for u in range(OB)], lower + m)
                    else:
                        found += take([(base + m * OB + v, lower + v) for v in range(OB)], upper + m)
            at = (pairs if mirrored else 0) + tile * ROWS
            lhs[at:at + ROWS, :] = found

    gather(True)

    def multiply(i, first, peak):
        block = lhs[first:first + pairs, :].astype(jnp.bfloat16)

        def one(step, peak):
            a = i * (part // width) + step
            panel = ints[:, pl.ds(pl.multiple_of(a * width, width), width)]
            got = jnp.dot(block, panel, preferred_element_type=jnp.float32)
            for t in range(tiles):
                piece = got[:, t * LANES:(t + 1) * LANES]
                prod[t, pl.ds(first * a_dev + a, pairs, stride=a_dev), :] = piece
                if peak is not None:
                    peak = jnp.maximum(peak, jnp.abs(piece))
            return peak

        return lax.fori_loop(0, part // width, one, peak, unroll=8)

    peak = jnp.full((pairs, LANES), TINY, jnp.float32)
    for i in range(n_parts):
        int_copies[i].wait()
        peak = multiply(i, pairs, peak)

    peaks[...] = jnp.broadcast_to(jnp.max(peak, axis=1, keepdims=True), peaks.shape)
    spot = lax.broadcasted_iota(jnp.int32, (units, LANES), 1) // a_dev
    table = peaks[pl.ds(0, units, stride=per_tile), :]
    for q in range(1, per_tile):
        table = jnp.where(spot == q, peaks[pl.ds(q, units, stride=per_tile), :], table)
    x_top[...] = table
    x_tops[row] = table

    pl.semaphore_wait(barrier, n_row + n_col - 2)

    last = n_col - 1
    lower = col < last - col
    from_end = jnp.where(lower, col, last - col)

    def unit(k):
        b = k // groups
        n = last - 1 - from_end
        inner = jnp.where(b < n + 2, n_col - b, b - 1 - n)
        inner = jnp.where(b == 0, last, jnp.where(b == 1, 0, inner))
        d = jnp.where(from_end == 0, last - b, inner)
        return jnp.where(lower, d, last - d), k % groups

    def partner(p):
        if n_row & (n_row - 1):
            return lax.rem(row + p, n_row)
        peer, bit = row, 1
        while bit < n_row:
            if p & bit:
                peer = peer + bit - 2 * bit * ((row // bit) % 2)
            bit *= 2
        return peer

    steps = sorted(range(1, n_row), key=lambda p: (-bin(p // 2).count('1'), p))

    def x_copy(u, p):
        peer = partner(p)
        return pltpu.make_async_remote_copy(
            src_ref=turned.at[u, pl.ds(pl.multiple_of(peer * a_dev, a_dev), a_dev), :],
            dst_ref=inbox.at[u * n_row + row],
            send_sem=x_send,
            recv_sem=x_recv.at[u],
            device_id={"row": peer},
        )

    def top_copy(p):
        return pltpu.make_async_remote_copy(
            src_ref=x_top,
            dst_ref=x_tops.at[row],
            send_sem=t_send,
            recv_sem=t_recv,
            device_id={"row": partner(p)},
        )

    def wait_for(ref, start, count, sem):
        landed = ref.at[pl.ds(start, count)]
        pltpu.make_async_copy(landed, landed, sem).wait()

    def encode(block, top):
        return jnp.round(block * (CODE / top)).astype(jnp.int32).astype(jnp.int16)

    def decode(code, top):
        return code.astype(jnp.int32).astype(jnp.float32) * (top * (1.0 / CODE))

    def top_of(blocks):
        top = jnp.abs(blocks[0])
        for block in blocks[1:]:
            top = jnp.maximum(top, jnp.abs(block))
        return jnp.maximum(jnp.max(top, axis=0, keepdims=True), TINY)

    def relay_slot(d, g):
        return ((d - 1) * groups + g) * tiles

    def own_slot(source, d, g):
        return ((last - 1 + jnp.where(source < d, source, source - 1)) * groups + g) * tiles

    def z_copies(d, g, t):
        u = d * groups + g
        to = jnp.where(d > col, col + 1, col - 1)
        to = jnp.where((d == 0) | (d == last), d, to)
        slot = jnp.where(to == d, own_slot(col, d, g), relay_slot(d, g)) + t
        return [
            pltpu.make_async_remote_copy(
                src_ref=src.at[u * tiles + t], dst_ref=dst.at[slot],
                send_sem=z_send.at[i], recv_sem=z_recv.at[i, slot],
                device_id={"col": to},
            )
            for i, (src, dst) in enumerate(((top_out, top_in), (code_out, code_in)))
        ]

    def held(d, g, t):
        start = pl.multiple_of(d * (share * a_dev) + g * LANES, LANES)
        return prod.at[t, pl.ds(start, LANES)]

    def add_from(d, g, t, slot):
        at = slot + t
        wait_for(top_in, at, 1, z_recv.at[0, at])
        wait_for(code_in, at, 1, z_recv.at[1, at])
        here = held(d, g, t)
        here[...] = here[...] + decode(code_in[at], top_in[at])

    def send_on(d, g, t):
        at = (d * groups + g) * tiles + t
        block = held(d, g, t)[...]
        top = top_of([block])
        top_out[at] = top
        code_out[at] = encode(block, top)
        for copy in z_copies(d, g, t):
            copy.start()

    for p in steps:
        top_copy(p).start()

    def turn(k, carry):
        d, g = unit(k)
        u = d * groups + g
        start = pl.multiple_of((pairs * a_dev) + u * LANES, LANES)
        top = x_top[pl.ds(u, 1), :]
        for t in range(tiles):
            turned[u, t * LANES:(t + 1) * LANES, :] = encode(prod[t, pl.ds(start, LANES), :].T, top)
        for p in steps:
            x_copy(u, p).start()
        return carry

    lax.fori_loop(0, units, turn, 0)

    gather(False)
    for i in range(n_parts):
        multiply(i, 0, None)

    piece = lax.broadcasted_iota(jnp.int32, (a_dev, LANES), 1) // a_dev

    wait_for(x_tops, 0, n_row - 1, t_recv)

    def combine(k, carry):
        d, g = unit(k)
        u = d * groups + g
        inbox[u * n_row + row] = turned[u, pl.ds(pl.multiple_of(row * a_dev, a_dev), a_dev), :]
        wait_for(inbox, u * n_row, n_row - 1, x_recv.at[u])
        for t in range(tiles):
            parts = []
            for j in range(per_tile):
                source = t * per_tile + j
                parts.append(decode(inbox[u * n_row + source], x_tops[source, pl.ds(u, 1), :]))
            sums = []
            for q in range(per_tile):
                merged = pltpu.roll(parts[0], (-q * a_dev) % LANES, 1) if q else parts[0]
                for j in range(1, per_tile):
                    shift = ((j - q) * a_dev) % LANES
                    moved = pltpu.roll(parts[j], shift, 1) if shift else parts[j]
                    merged = jnp.where(piece == j, moved, merged)
                sums.append(merged)
            here = held(d, g, t)
            here[...] = here[...] + jnp.concatenate(sums, axis=0)

        begins = jnp.where(d > col, col == 0, col == last) | (d == 0) | (d == last)

        @pl.when(d != col)
        def _():
            for t in range(tiles):
                @pl.when(jnp.logical_not(begins))
                def _(t=t):
                    add_from(d, g, t, relay_slot(d, g))

                send_on(d, g, t)

        return carry

    lax.fori_loop(0, units, combine, 0)

    at_end = (col == 0) | (col == last)

    def collect(j, carry):
        beside = jnp.where(j == 0, col - 1, col + 1)
        across = jnp.where(col == 0, j + 1, last - 1 - j)
        source = jnp.where(at_end, across, beside)
        for g in range(groups):
            for t in range(tiles):
                add_from(col, g, t, own_slot(source, col, g))
        return carry

    lax.fori_loop(0, jnp.where(at_end, last, 2), collect, 0)

    for t in range(tiles):
        for a in range(a_dev):
            value = prod[t, pl.ds(col * (share * a_dev) + a, share, stride=a_dev), :]
            at = a * width + t * LANES
            out_ref[:, at:at + LANES] = value.astype(out_ref.dtype)

    sent = (n_col - 1) * groups * tiles
    wait_for(x_tops, 0, n_row - 1, t_send)
    wait_for(inbox, 0, units * (n_row - 1), x_send)
    if sent:
        wait_for(top_out, 0, sent, z_send.at[0])
        wait_for(code_out, 0, sent, z_send.at[1])


def on_device(n_row, n_col, amplitudes, integrals, blocks):
    amplitudes = jnp.swapaxes(amplitudes, 1, 2)
    blocks = blocks.T
    depth, local = integrals.shape
    width = math.isqrt(local * n_row)
    a_dev = width // n_row
    pairs = blocks.shape[1] * OB * OB
    tiles = width // LANES
    share = pairs // n_col
    groups = share * a_dev // LANES
    n_parts = 4
    f32 = jnp.float32
    dma = pltpu.SemaphoreType.DMA
    units = n_col * groups
    slots = (2 * n_col - 3) * groups * tiles
    return pl.pallas_call(
        functools.partial(ladder_kernel, n_row, n_col, a_dev),
        out_shape=pltpu.VMEM((share, local), jnp.bfloat16),
        in_specs=[
            pl.BlockSpec(memory_space=pl.ANY),
            pl.BlockSpec(memory_space=pl.ANY),
            pl.BlockSpec(memory_space=pl.ANY),
        ],
        out_specs=pl.BlockSpec(memory_space=pltpu.VMEM),
        scratch_shapes=[
            pltpu.SMEM(blocks.shape, blocks.dtype),
            pltpu.VMEM(amplitudes.shape, amplitudes.dtype),
            pltpu.VMEM(integrals.shape, integrals.dtype),
            pltpu.VMEM((2 * pairs, depth), f32),
            pltpu.VMEM((tiles, 2 * pairs * a_dev, LANES), f32),
            pltpu.VMEM((units, width, LANES), jnp.int16),
            pltpu.VMEM((units * n_row, a_dev, LANES), jnp.int16),
            pltpu.VMEM((pairs, LANES), f32),
            pltpu.VMEM((units, LANES), f32),
            pltpu.VMEM((n_row, units, LANES), f32),
            pltpu.VMEM((units * tiles, LANES, LANES), jnp.int16),
            pltpu.VMEM((units * tiles, 1, LANES), f32),
            pltpu.VMEM((slots, LANES, LANES), jnp.int16),
            pltpu.VMEM((slots, 1, LANES), f32),
            dma(()),
            dma(()),
            dma((n_parts,)),
            dma(()),
            dma((units,)),
            dma(()),
            dma(()),
            dma((2,)),
            dma((2, slots)),
        ],
        compiler_params=pltpu.CompilerParams(
            collective_id=0, has_side_effects=True, vmem_limit_bytes=VMEM - 4 * share * local * 2
        ),
    )(blocks, amplitudes, integrals)


def solution(mesh):
    return jax.shard_map(
        functools.partial(on_device, mesh.shape["row"], mesh.shape["col"]),
        mesh=mesh,
        in_specs=(P(None, None, "col"), P("col", "row"), P()),
        out_specs=P("col", "row"),
        check_vma=False,
    )
```

```python
import functools
import math

import jax
import jax.numpy as jnp
from jax import lax
from jax.experimental import pallas as pl
from jax.experimental.pallas import tpu as pltpu
from jax.sharding import PartitionSpec as P

OB = 2
LANES = 128
CODE = 32700.0
TINY = 1e-30
ROWS = 8
VMEM = 67043328


def ladder_kernel(
    n_row, n_col, a_dev,
    blocks_hbm, amp_hbm, int_hbm, out_ref,
    blocks, amp, ints, lhs, prod, turned, inbox, peaks, x_top, x_tops,
    code_out, top_out, code_in, top_in,
    block_sem, amp_sem, int_sem, x_send, x_recv, t_send, t_recv, z_send, z_recv,
):
    row = lax.axis_index("row")
    col = lax.axis_index("col")
    pairs = lhs.shape[0] // 2
    width = a_dev * n_row
    tiles = width // LANES
    per_tile = LANES // a_dev
    share = pairs // n_col
    groups = share // per_tile
    units = n_col * groups
    occ = amp.shape[2]
    n_parts = int_sem.shape[0]
    part = ints.shape[1] // n_parts

    block_copy = pltpu.make_async_copy(blocks_hbm, blocks, block_sem)
    block_copy.start()
    amp_copy = pltpu.make_async_copy(amp_hbm, amp, amp_sem)
    amp_copy.start()
    int_copies = []
    for i in range(n_parts):
        cut = pl.ds(i * part, part)
        copy = pltpu.make_async_copy(int_hbm.at[:, cut], ints.at[:, cut], int_sem.at[i])
        copy.start()
        int_copies.append(copy)

    barrier = pltpu.get_barrier_semaphore()

    def greet(p, carry):
        pl.semaphore_signal(barrier, inc=1, device_id={"row": lax.rem(row + p, n_row)})
        return carry

    lax.fori_loop(1, n_row, greet, 0)

    def greet_col(p, carry):
        pl.semaphore_signal(barrier, inc=1, device_id={"col": lax.rem(col + p, n_col)})
        return carry

    lax.fori_loop(1, n_col, greet_col, 0)

    block_copy.wait()
    amp_copy.wait()
    spot_row = lax.broadcasted_iota(jnp.int32, (ROWS, occ), 0)
    spot_col = lax.broadcasted_iota(jnp.int32, (ROWS, occ), 1)

    def take(spots, plane):
        hit = jnp.zeros((ROWS, occ), jnp.bool_)
        for at, column in spots:
            hit = hit | ((spot_row == at) & (spot_col == column))
        chosen = jnp.where(hit, 1.0, 0.0).astype(amp.dtype)
        return lax.dot_general(
            chosen, amp[plane], (((1,), (1,)), ((), ())), preferred_element_type=jnp.float32
        )

    per_rows = ROWS // (OB * OB)

    def gather(mirrored):
        for tile in range(pairs // ROWS):
            found = jnp.zeros((ROWS, lhs.shape[1]), jnp.float32)
            for k in range(per_rows):
                upper = blocks[0, tile * per_rows + k] * OB
                lower = blocks[1, tile * per_rows + k] * OB
                base = k * OB * OB
                for m in range(OB):
                    if mirrored:
                        found += take([(base + u * OB + m, upper + u) for u in range(OB)], lower + m)
                    else:
                        found += take([(base + m * OB + v, lower + v) for v in range(OB)], upper + m)
            at = (pairs if mirrored else 0) + tile * ROWS
            lhs[at:at + ROWS, :] = found

    gather(True)

    def multiply(i, first, peak):
        block = lhs[first:first + pairs, :].astype(jnp.bfloat16)

        def one(step, peak):
            a = i * (part // width) + step
            panel = ints[:, pl.ds(pl.multiple_of(a * width, width), width)]
            got = jnp.dot(block, panel, preferred_element_type=jnp.float32)
            for t in range(tiles):
                piece = got[:, t * LANES:(t + 1) * LANES]
                prod[t, pl.ds(first * a_dev + a, pairs, stride=a_dev), :] = piece
                if peak is not None:
                    peak = jnp.maximum(peak, jnp.abs(piece))
            return peak

        return lax.fori_loop(0, part // width, one, peak, unroll=8)

    peak = jnp.full((pairs, LANES), TINY, jnp.float32)
    for i in range(n_parts):
        int_copies[i].wait()
        peak = multiply(i, pairs, peak)

    peaks[...] = jnp.broadcast_to(jnp.max(peak, axis=1, keepdims=True), peaks.shape)
    spot = lax.broadcasted_iota(jnp.int32, (units, LANES), 1) // a_dev
    table = peaks[pl.ds(0, units, stride=per_tile), :]
    for q in range(1, per_tile):
        table = jnp.where(spot == q, peaks[pl.ds(q, units, stride=per_tile), :], table)
    x_top[...] = table
    x_tops[row] = table

    pl.semaphore_wait(barrier, n_row + n_col - 2)

    last = n_col - 1
    lower = col < last - col
    from_end = jnp.where(lower, col, last - col)

    def unit(k):
        b = k // groups
        n = last - 1 - from_end
        inner = jnp.where(b < n + 2, n_col - b, b - 1 - n)
        inner = jnp.where(b < 2, jnp.where(lower == (b == 0), 0, last), inner)
        d = jnp.where(from_end == 0, last - b, inner)
        return jnp.where(lower, d, last - d), k % groups

    def partner(p):
        if n_row & (n_row - 1):
            return lax.rem(row + p, n_row)
        peer, bit = row, 1
        while bit < n_row:
            if p & bit:
                peer = peer + bit - 2 * bit * ((row // bit) % 2)
            bit *= 2
        return peer

    steps = sorted(range(1, n_row), key=lambda p: (-bin(p // 2).count('1'), p))

    def x_copy(u, p):
        peer = partner(p)
        return pltpu.make_async_remote_copy(
            src_ref=turned.at[u, pl.ds(pl.multiple_of(peer * a_dev, a_dev), a_dev), :],
            dst_ref=inbox.at[u * n_row + row],
            send_sem=x_send,
            recv_sem=x_recv.at[u],
            device_id={"row": peer},
        )

    def top_copy(p):
        return pltpu.make_async_remote_copy(
            src_ref=x_top,
            dst_ref=x_tops.at[row],
            send_sem=t_send,
            recv_sem=t_recv,
            device_id={"row": partner(p)},
        )

    def wait_for(ref, start, count, sem):
        landed = ref.at[pl.ds(start, count)]
        pltpu.make_async_copy(landed, landed, sem).wait()

    def encode(block, top):
        return jnp.round(block * (CODE / top)).astype(jnp.int32).astype(jnp.int16)

    def decode(code, top):
        return code.astype(jnp.int32).astype(jnp.float32) * (top * (1.0 / CODE))

    def top_of(blocks):
        top = jnp.abs(blocks[0])
        for block in blocks[1:]:
            top = jnp.maximum(top, jnp.abs(block))
        return jnp.maximum(jnp.max(top, axis=0, keepdims=True), TINY)

    def relay_slot(d, g):
        return ((d - 1) * groups + g) * tiles

    def own_slot(source, d, g):
        return ((last - 1 + jnp.where(source < d, source, source - 1)) * groups + g) * tiles

    def z_copies(d, g, t):
        u = d * groups + g
        to = jnp.where(d > col, col + 1, col - 1)
        to = jnp.where((d == 0) | (d == last), d, to)
        slot = jnp.where(to == d, own_slot(col, d, g), relay_slot(d, g)) + t
        return [
            pltpu.make_async_remote_copy(
                src_ref=src.at[u * tiles + t], dst_ref=dst.at[slot],
                send_sem=z_send.at[i], recv_sem=z_recv.at[i, slot],
                device_id={"col": to},
            )
            for i, (src, dst) in enumerate(((top_out, top_in), (code_out, code_in)))
        ]

    def held(d, g, t):
        start = pl.multiple_of(d * (share * a_dev) + g * LANES, LANES)
        return prod.at[t, pl.ds(start, LANES)]

    def add_from(d, g, t, slot):
        at = slot + t
        wait_for(top_in, at, 1, z_recv.at[0, at])
        wait_for(code_in, at, 1, z_recv.at[1, at])
        here = held(d, g, t)
        here[...] = here[...] + decode(code_in[at], top_in[at])

    def send_on(d, g, t):
        at = (d * groups + g) * tiles + t
        block = held(d, g, t)[...]
        top = top_of([block])
        top_out[at] = top
        code_out[at] = encode(block, top)
        for copy in z_copies(d, g, t):
            copy.start()

    for p in steps:
        top_copy(p).start()

    def turn(k, carry):
        d, g = unit(k)
        u = d * groups + g
        start = pl.multiple_of((pairs * a_dev) + u * LANES, LANES)
        top = x_top[pl.ds(u, 1), :]
        for t in range(tiles):
            turned[u, t * LANES:(t + 1) * LANES, :] = encode(prod[t, pl.ds(start, LANES), :].T, top)
        for p in steps:
            x_copy(u, p).start()
        return carry

    lax.fori_loop(0, units, turn, 0)

    gather(False)
    for i in range(n_parts):
        multiply(i, 0, None)

    piece = lax.broadcasted_iota(jnp.int32, (a_dev, LANES), 1) // a_dev

    wait_for(x_tops, 0, n_row - 1, t_recv)

    def combine(k, carry):
        d, g = unit(k)
        u = d * groups + g
        inbox[u * n_row + row] = turned[u, pl.ds(pl.multiple_of(row * a_dev, a_dev), a_dev), :]
        wait_for(inbox, u * n_row, n_row - 1, x_recv.at[u])
        for t in range(tiles):
            parts = []
            for j in range(per_tile):
                source = t * per_tile + j
                parts.append(decode(inbox[u * n_row + source], x_tops[source, pl.ds(u, 1), :]))
            sums = []
            for q in range(per_tile):
                merged = pltpu.roll(parts[0], (-q * a_dev) % LANES, 1) if q else parts[0]
                for j in range(1, per_tile):
                    shift = ((j - q) * a_dev) % LANES
                    moved = pltpu.roll(parts[j], shift, 1) if shift else parts[j]
                    merged = jnp.where(piece == j, moved, merged)
                sums.append(merged)
            here = held(d, g, t)
            here[...] = here[...] + jnp.concatenate(sums, axis=0)

        begins = jnp.where(d > col, col == 0, col == last) | (d == 0) | (d == last)

        @pl.when(d != col)
        def _():
            for t in range(tiles):
                @pl.when(jnp.logical_not(begins))
                def _(t=t):
                    add_from(d, g, t, relay_slot(d, g))

                send_on(d, g, t)

        return carry

    lax.fori_loop(0, units, combine, 0)

    at_end = (col == 0) | (col == last)

    def collect(j, carry):
        beside = jnp.where(j == 0, col - 1, col + 1)
        across = jnp.where(col == 0, j + 1, last - 1 - j)
        source = jnp.where(at_end, across, beside)
        for g in range(groups):
            for t in range(tiles):
                add_from(col, g, t, own_slot(source, col, g))
        return carry

    lax.fori_loop(0, jnp.where(at_end, last, 2), collect, 0)

    for t in range(tiles):
        for a in range(a_dev):
            value = prod[t, pl.ds(col * (share * a_dev) + a, share, stride=a_dev), :]
            at = a * width + t * LANES
            out_ref[:, at:at + LANES] = value.astype(out_ref.dtype)

    sent = (n_col - 1) * groups * tiles
    wait_for(x_tops, 0, n_row - 1, t_send)
    wait_for(inbox, 0, units * (n_row - 1), x_send)
    if sent:
        wait_for(top_out, 0, sent, z_send.at[0])
        wait_for(code_out, 0, sent, z_send.at[1])


def on_device(n_row, n_col, amplitudes, integrals, blocks):
    amplitudes = jnp.swapaxes(amplitudes, 1, 2)
    blocks = blocks.T
    depth, local = integrals.shape
    width = math.isqrt(local * n_row)
    a_dev = width // n_row
    pairs = blocks.shape[1] * OB * OB
    tiles = width // LANES
    share = pairs // n_col
    groups = share * a_dev // LANES
    n_parts = 4
    f32 = jnp.float32
    dma = pltpu.SemaphoreType.DMA
    units = n_col * groups
    slots = (2 * n_col - 3) * groups * tiles
    return pl.pallas_call(
        functools.partial(ladder_kernel, n_row, n_col, a_dev),
        out_shape=pltpu.VMEM((share, local), jnp.bfloat16),
        in_specs=[
            pl.BlockSpec(memory_space=pl.ANY),
            pl.BlockSpec(memory_space=pl.ANY),
            pl.BlockSpec(memory_space=pl.ANY),
        ],
        out_specs=pl.BlockSpec(memory_space=pltpu.VMEM),
        scratch_shapes=[
            pltpu.SMEM(blocks.shape, blocks.dtype),
            pltpu.VMEM(amplitudes.shape, amplitudes.dtype),
            pltpu.VMEM(integrals.shape, integrals.dtype),
            pltpu.VMEM((2 * pairs, depth), f32),
            pltpu.VMEM((tiles, 2 * pairs * a_dev, LANES), f32),
            pltpu.VMEM((units, width, LANES), jnp.int16),
            pltpu.VMEM((units * n_row, a_dev, LANES), jnp.int16),
            pltpu.VMEM((pairs, LANES), f32),
            pltpu.VMEM((units, LANES), f32),
            pltpu.VMEM((n_row, units, LANES), f32),
            pltpu.VMEM((units * tiles, LANES, LANES), jnp.int16),
            pltpu.VMEM((units * tiles, 1, LANES), f32),
            pltpu.VMEM((slots, LANES, LANES), jnp.int16),
            pltpu.VMEM((slots, 1, LANES), f32),
            dma(()),
            dma(()),
            dma((n_parts,)),
            dma(()),
            dma((units,)),
            dma(()),
            dma(()),
            dma((2,)),
            dma((2, slots)),
        ],
        compiler_params=pltpu.CompilerParams(
            collective_id=0, has_side_effects=True, vmem_limit_bytes=VMEM - 4 * share * local * 2
        ),
    )(blocks, amplitudes, integrals)


def solution(mesh):
    return jax.shard_map(
        functools.partial(on_device, mesh.shape["row"], mesh.shape["col"]),
        mesh=mesh,
        in_specs=(P(None, None, "col"), P("col", "row"), P()),
        out_specs=P("col", "row"),
        check_vma=False,
    )
```

```python
import functools
import math

import jax
import jax.numpy as jnp
from jax import lax
from jax.experimental import pallas as pl
from jax.experimental.pallas import tpu as pltpu
from jax.sharding import PartitionSpec as P

OB = 2
LANES = 128
CODE = 32700.0
TINY = 1e-30
ROWS = 8
VMEM = 67043328


def ladder_kernel(
    n_row, n_col, a_dev,
    blocks_hbm, amp_hbm, int_hbm, out_ref,
    blocks, amp, ints, lhs, prod, turned, inbox, peaks, x_top, x_tops,
    code_out, top_out, code_in, top_in,
    block_sem, amp_sem, int_sem, x_send, x_recv, t_send, t_recv, z_send, z_recv,
):
    row = lax.axis_index("row")
    col = lax.axis_index("col")
    pairs = lhs.shape[0] // 2
    width = a_dev * n_row
    tiles = width // LANES
    per_tile = LANES // a_dev
    share = pairs // n_col
    groups = share // per_tile
    units = n_col * groups
    occ = amp.shape[2]
    n_parts = int_sem.shape[0]
    part = ints.shape[1] // n_parts

    block_copy = pltpu.make_async_copy(blocks_hbm, blocks, block_sem)
    block_copy.start()
    amp_copies = []
    n_cuts = amp_sem.shape[0]
    planes = amp.shape[0] // n_cuts
    for i in range(n_cuts):
        cut = pl.ds(i * planes, planes if i < n_cuts - 1 else amp.shape[0] - i * planes)
        amp_copies.append(pltpu.make_async_copy(amp_hbm.at[cut], amp.at[cut], amp_sem.at[i]))
        amp_copies[i].start()
    int_copies = []
    for i in range(n_parts):
        cut = pl.ds(i * part, part)
        copy = pltpu.make_async_copy(int_hbm.at[:, cut], ints.at[:, cut], int_sem.at[i])
        int_copies.append(copy)

    barrier = pltpu.get_barrier_semaphore()

    def greet(p, carry):
        pl.semaphore_signal(barrier, inc=1, device_id={"row": lax.rem(row + p, n_row)})
        return carry

    lax.fori_loop(1, n_row, greet, 0)

    def greet_col(p, carry):
        pl.semaphore_signal(barrier, inc=1, device_id={"col": lax.rem(col + p, n_col)})
        return carry

    lax.fori_loop(1, n_col, greet_col, 0)

    amp_copies[0].wait()
    for copy in int_copies:
        copy.start()
    block_copy.wait()
    for copy in amp_copies[1:]:
        copy.wait()
    spot_row = lax.broadcasted_iota(jnp.int32, (ROWS, occ), 0)
    spot_col = lax.broadcasted_iota(jnp.int32, (ROWS, occ), 1)

    def take(spots, plane):
        hit = jnp.zeros((ROWS, occ), jnp.bool_)
        for at, column in spots:
            hit = hit | ((spot_row == at) & (spot_col == column))
        chosen = jnp.where(hit, 1.0, 0.0).astype(amp.dtype)
        return lax.dot_general(
            chosen, amp[plane], (((1,), (1,)), ((), ())), preferred_element_type=jnp.float32
        )

    per_rows = ROWS // (OB * OB)

    def gather(mirrored):
        for tile in range(pairs // ROWS):
            found = jnp.zeros((ROWS, lhs.shape[1]), jnp.float32)
            for k in range(per_rows):
                upper = blocks[0, tile * per_rows + k] * OB
                lower = blocks[1, tile * per_rows + k] * OB
                base = k * OB * OB
                for m in range(OB):
                    if mirrored:
                        found += take([(base + u * OB + m, upper + u) for u in range(OB)], lower + m)
                    else:
                        found += take([(base + m * OB + v, lower + v) for v in range(OB)], upper + m)
            at = (pairs if mirrored else 0) + tile * ROWS
            lhs[at:at + ROWS, :] = found

    gather(True)

    def multiply(i, first, peak):
        block = lhs[first:first + pairs, :].astype(jnp.bfloat16)

        def one(step, peak):
            a = i * (part // width) + step
            panel = ints[:, pl.ds(pl.multiple_of(a * width, width), width)]
            got = jnp.dot(block, panel, preferred_element_type=jnp.float32)
            for t in range(tiles):
                piece = got[:, t * LANES:(t + 1) * LANES]
                prod[t, pl.ds(first * a_dev + a, pairs, stride=a_dev), :] = piece
                if peak is not None:
                    peak = jnp.maximum(peak, jnp.abs(piece))
            return peak

        return lax.fori_loop(0, part // width, one, peak, unroll=8)

    peak = jnp.full((pairs, LANES), TINY, jnp.float32)
    for i in range(n_parts):
        int_copies[i].wait()
        peak = multiply(i, pairs, peak)

    peaks[...] = jnp.broadcast_to(jnp.max(peak, axis=1, keepdims=True), peaks.shape)
    spot = lax.broadcasted_iota(jnp.int32, (units, LANES), 1) // a_dev
    table = peaks[pl.ds(0, units, stride=per_tile), :]
    for q in range(1, per_tile):
        table = jnp.where(spot == q, peaks[pl.ds(q, units, stride=per_tile), :], table)
    x_top[...] = table
    x_tops[row] = table

    pl.semaphore_wait(barrier, n_row + n_col - 2)

    last = n_col - 1
    lower = col < last - col
    from_end = jnp.where(lower, col, last - col)

    def unit(k):
        b = k // groups
        n = last - 1 - from_end
        inner = jnp.where(b < n + 2, n_col - b, b - 1 - n)
        inner = jnp.where(b < 2, jnp.where(lower == (b == 0), 0, last), inner)
        d = jnp.where(from_end == 0, last - b, inner)
        return jnp.where(lower, d, last - d), k % groups

    def partner(p):
        if n_row & (n_row - 1):
            return lax.rem(row + p, n_row)
        peer, bit = row, 1
        while bit < n_row:
            if p & bit:
                peer = peer + bit - 2 * bit * ((row // bit) % 2)
            bit *= 2
        return peer

    steps = sorted(range(1, n_row), key=lambda p: (-bin(p // 2).count('1'), p))

    def x_copy(u, p):
        peer = partner(p)
        return pltpu.make_async_remote_copy(
            src_ref=turned.at[u, pl.ds(pl.multiple_of(peer * a_dev, a_dev), a_dev), :],
            dst_ref=inbox.at[u * n_row + row],
            send_sem=x_send,
            recv_sem=x_recv.at[u],
            device_id={"row": peer},
        )

    def top_copy(p):
        return pltpu.make_async_remote_copy(
            src_ref=x_top,
            dst_ref=x_tops.at[row],
            send_sem=t_send,
            recv_sem=t_recv,
            device_id={"row": partner(p)},
        )

    def wait_for(ref, start, count, sem):
        landed = ref.at[pl.ds(start, count)]
        pltpu.make_async_copy(landed, landed, sem).wait()

    def encode(block, top):
        return jnp.round(block * (CODE / top)).astype(jnp.int32).astype(jnp.int16)

    def decode(code, top):
        return code.astype(jnp.int32).astype(jnp.float32) * (top * (1.0 / CODE))

    def top_of(blocks):
        top = jnp.abs(blocks[0])
        for block in blocks[1:]:
            top = jnp.maximum(top, jnp.abs(block))
        return jnp.maximum(jnp.max(top, axis=0, keepdims=True), TINY)

    def relay_slot(d, g):
        return ((d - 1) * groups + g) * tiles

    def own_slot(source, d, g):
        return ((last - 1 + jnp.where(source < d, source, source - 1)) * groups + g) * tiles

    def z_copies(d, g, t):
        u = d * groups + g
        to = jnp.where(d > col, col + 1, col - 1)
        to = jnp.where((d == 0) | (d == last), d, to)
        slot = jnp.where(to == d, own_slot(col, d, g), relay_slot(d, g)) + t
        return [
            pltpu.make_async_remote_copy(
                src_ref=src.at[u * tiles + t], dst_ref=dst.at[slot],
                send_sem=z_send.at[i], recv_sem=z_recv.at[i, slot],
                device_id={"col": to},
            )
            for i, (src, dst) in enumerate(((top_out, top_in), (code_out, code_in)))
        ]

    def held(d, g, t):
        start = pl.multiple_of(d * (share * a_dev) + g * LANES, LANES)
        return prod.at[t, pl.ds(start, LANES)]

    def add_from(d, g, t, slot):
        at = slot + t
        wait_for(top_in, at, 1, z_recv.at[0, at])
        wait_for(code_in, at, 1, z_recv.at[1, at])
        here = held(d, g, t)
        here[...] = here[...] + decode(code_in[at], top_in[at])

    def send_on(d, g, t):
        at = (d * groups + g) * tiles + t
        block = held(d, g, t)[...]
        top = top_of([block])
        top_out[at] = top
        code_out[at] = encode(block, top)
        for copy in z_copies(d, g, t):
            copy.start()

    for p in steps:
        top_copy(p).start()

    def turn(k, carry):
        d, g = unit(k)
        u = d * groups + g
        start = pl.multiple_of((pairs * a_dev) + u * LANES, LANES)
        top = x_top[pl.ds(u, 1), :]
        for t in range(tiles):
            turned[u, t * LANES:(t + 1) * LANES, :] = encode(prod[t, pl.ds(start, LANES), :].T, top)
        for p in steps:
            x_copy(u, p).start()
        return carry

    lax.fori_loop(0, units, turn, 0, unroll=2)

    gather(False)
    for i in range(n_parts):
        multiply(i, 0, None)

    piece = lax.broadcasted_iota(jnp.int32, (a_dev, LANES), 1) // a_dev

    wait_for(x_tops, 0, n_row - 1, t_recv)

    def combine(k, carry):
        d, g = unit(k)
        u = d * groups + g
        inbox[u * n_row + row] = turned[u, pl.ds(pl.multiple_of(row * a_dev, a_dev), a_dev), :]
        wait_for(inbox, u * n_row, n_row - 1, x_recv.at[u])
        for t in range(tiles):
            parts = []
            for j in range(per_tile):
                source = t * per_tile + j
                parts.append(decode(inbox[u * n_row + source], x_tops[source, pl.ds(u, 1), :]))
            sums = []
            for q in range(per_tile):
                merged = pltpu.roll(parts[0], (-q * a_dev) % LANES, 1) if q else parts[0]
                for j in range(1, per_tile):
                    shift = ((j - q) * a_dev) % LANES
                    moved = pltpu.roll(parts[j], shift, 1) if shift else parts[j]
                    merged = jnp.where(piece == j, moved, merged)
                sums.append(merged)
            here = held(d, g, t)
            here[...] = here[...] + jnp.concatenate(sums, axis=0)

        begins = jnp.where(d > col, col == 0, col == last) | (d == 0) | (d == last)

        @pl.when(d != col)
        def _():
            for t in range(tiles):
                @pl.when(jnp.logical_not(begins))
                def _(t=t):
                    add_from(d, g, t, relay_slot(d, g))

                send_on(d, g, t)

        return carry

    lax.fori_loop(0, units, combine, 0)

    at_end = (col == 0) | (col == last)

    def collect(j, carry):
        beside = jnp.where(j == 0, col - 1, col + 1)
        across = jnp.where(col == 0, j + 1, last - 1 - j)
        source = jnp.where(at_end, across, beside)
        for g in range(groups):
            for t in range(tiles):
                add_from(col, g, t, own_slot(source, col, g))
        return carry

    lax.fori_loop(0, jnp.where(at_end, last, 2), collect, 0)

    for t in range(tiles):
        for a in range(a_dev):
            value = prod[t, pl.ds(col * (share * a_dev) + a, share, stride=a_dev), :]
            at = a * width + t * LANES
            out_ref[:, at:at + LANES] = value.astype(out_ref.dtype)

    sent = (n_col - 1) * groups * tiles
    wait_for(x_tops, 0, n_row - 1, t_send)
    wait_for(inbox, 0, units * (n_row - 1), x_send)
    if sent:
        wait_for(top_out, 0, sent, z_send.at[0])
        wait_for(code_out, 0, sent, z_send.at[1])


def on_device(n_row, n_col, amplitudes, integrals, blocks):
    amplitudes = jnp.swapaxes(amplitudes, 1, 2)
    blocks = blocks.T
    depth, local = integrals.shape
    width = math.isqrt(local * n_row)
    a_dev = width // n_row
    pairs = blocks.shape[1] * OB * OB
    tiles = width // LANES
    share = pairs // n_col
    groups = share * a_dev // LANES
    n_parts = 4
    f32 = jnp.float32
    dma = pltpu.SemaphoreType.DMA
    units = n_col * groups
    slots = (2 * n_col - 3) * groups * tiles
    return pl.pallas_call(
        functools.partial(ladder_kernel, n_row, n_col, a_dev),
        out_shape=pltpu.VMEM((share, local), jnp.bfloat16),
        in_specs=[
            pl.BlockSpec(memory_space=pl.ANY),
            pl.BlockSpec(memory_space=pl.ANY),
            pl.BlockSpec(memory_space=pl.ANY),
        ],
        out_specs=pl.BlockSpec(memory_space=pltpu.VMEM),
        scratch_shapes=[
            pltpu.SMEM(blocks.shape, blocks.dtype),
            pltpu.VMEM(amplitudes.shape, amplitudes.dtype),
            pltpu.VMEM(integrals.shape, integrals.dtype),
            pltpu.VMEM((2 * pairs, depth), f32),
            pltpu.VMEM((tiles, 2 * pairs * a_dev, LANES), f32),
            pltpu.VMEM((units, width, LANES), jnp.int16),
            pltpu.VMEM((units * n_row, a_dev, LANES), jnp.int16),
            pltpu.VMEM((pairs, LANES), f32),
            pltpu.VMEM((units, LANES), f32),
            pltpu.VMEM((n_row, units, LANES), f32),
            pltpu.VMEM((units * tiles, LANES, LANES), jnp.int16),
            pltpu.VMEM((units * tiles, 1, LANES), f32),
            pltpu.VMEM((slots, LANES, LANES), jnp.int16),
            pltpu.VMEM((slots, 1, LANES), f32),
            dma(()),
            dma((4,)),
            dma((n_parts,)),
            dma(()),
            dma((units,)),
            dma(()),
            dma(()),
            dma((2,)),
            dma((2, slots)),
        ],
        compiler_params=pltpu.CompilerParams(
            collective_id=0, has_side_effects=True, vmem_limit_bytes=VMEM - 4 * share * local * 2
        ),
    )(blocks, amplitudes, integrals)


def solution(mesh):
    return jax.shard_map(
        functools.partial(on_device, mesh.shape["row"], mesh.shape["col"]),
        mesh=mesh,
        in_specs=(P(None, None, "col"), P("col", "row"), P()),
        out_specs=P("col", "row"),
        check_vma=False,
    )
```

```python
import functools
import math

import jax
import jax.numpy as jnp
from jax import lax
from jax.experimental import pallas as pl
from jax.experimental.pallas import tpu as pltpu
from jax.sharding import PartitionSpec as P

OB = 2
LANES = 128
CODE = 32700.0
TINY = 1e-30
ROWS = 8
VMEM = 67043328


def ladder_kernel(
    n_row, n_col, a_dev,
    blocks_hbm, amp_hbm, int_hbm, out_ref,
    blocks, amp, ints, lhs, prod, turned, inbox, peaks, x_top, x_tops,
    code_out, top_out, code_in, top_in,
    block_sem, amp_sem, int_sem, x_send, x_recv, t_send, t_recv, z_send, z_recv,
):
    row = lax.axis_index("row")
    col = lax.axis_index("col")
    pairs = lhs.shape[0] // 2
    width = a_dev * n_row
    tiles = width // LANES
    per_tile = LANES // a_dev
    share = pairs // n_col
    groups = share // per_tile
    units = n_col * groups
    occ = amp.shape[2]
    n_parts = int_sem.shape[0]
    part = ints.shape[1] // n_parts

    block_copy = pltpu.make_async_copy(blocks_hbm, blocks, block_sem)
    block_copy.start()
    amp_copies = []
    n_cuts = amp_sem.shape[0]
    planes = amp.shape[0] // n_cuts
    for i in range(n_cuts):
        cut = pl.ds(i * planes, planes if i < n_cuts - 1 else amp.shape[0] - i * planes)
        amp_copies.append(pltpu.make_async_copy(amp_hbm.at[cut], amp.at[cut], amp_sem.at[i]))
        amp_copies[i].start()
    int_copies = []
    for i in range(n_parts):
        cut = pl.ds(i * part, part)
        copy = pltpu.make_async_copy(int_hbm.at[:, cut], ints.at[:, cut], int_sem.at[i])
        int_copies.append(copy)

    barrier = pltpu.get_barrier_semaphore()

    def greet(p, carry):
        pl.semaphore_signal(barrier, inc=1, device_id={"row": lax.rem(row + p, n_row)})
        return carry

    lax.fori_loop(1, n_row, greet, 0)

    def greet_col(p, carry):
        pl.semaphore_signal(barrier, inc=1, device_id={"col": lax.rem(col + p, n_col)})
        return carry

    lax.fori_loop(1, n_col, greet_col, 0)

    amp_copies[0].wait()
    for copy in int_copies:
        copy.start()
    block_copy.wait()
    for copy in amp_copies[1:]:
        copy.wait()
    spot_row = lax.broadcasted_iota(jnp.int32, (ROWS, occ), 0)
    spot_col = lax.broadcasted_iota(jnp.int32, (ROWS, occ), 1)

    def take(spots, plane):
        hit = jnp.zeros((ROWS, occ), jnp.bool_)
        for at, column in spots:
            hit = hit | ((spot_row == at) & (spot_col == column))
        chosen = jnp.where(hit, 1.0, 0.0).astype(amp.dtype)
        return lax.dot_general(
            chosen, amp[plane], (((1,), (1,)), ((), ())), preferred_element_type=jnp.float32
        )

    per_rows = ROWS // (OB * OB)

    def gather(mirrored):
        for tile in range(pairs // ROWS):
            found = jnp.zeros((ROWS, lhs.shape[1]), jnp.float32)
            for k in range(per_rows):
                upper = blocks[0, tile * per_rows + k] * OB
                lower = blocks[1, tile * per_rows + k] * OB
                base = k * OB * OB
                for m in range(OB):
                    if mirrored:
                        found += take([(base + u * OB + m, upper + u) for u in range(OB)], lower + m)
                    else:
                        found += take([(base + m * OB + v, lower + v) for v in range(OB)], upper + m)
            at = (pairs if mirrored else 0) + tile * ROWS
            lhs[at:at + ROWS, :] = found

    gather(True)

    def multiply(i, first, peak):
        block = lhs[first:first + pairs, :].astype(jnp.bfloat16)

        def one(step, peak):
            a = i * (part // width) + step
            panel = ints[:, pl.ds(pl.multiple_of(a * width, width), width)]
            got = jnp.dot(block, panel, preferred_element_type=jnp.float32)
            for t in range(tiles):
                piece = got[:, t * LANES:(t + 1) * LANES]
                prod[t, pl.ds(first * a_dev + a, pairs, stride=a_dev), :] = piece
                if peak is not None:
                    peak = jnp.maximum(peak, jnp.abs(piece))
            return peak

        return lax.fori_loop(0, part // width, one, peak, unroll=8)

    peak = jnp.full((pairs, LANES), TINY, jnp.float32)
    for i in range(n_parts):
        int_copies[i].wait()
        peak = multiply(i, pairs, peak)

    peaks[...] = jnp.broadcast_to(jnp.max(peak, axis=1, keepdims=True), peaks.shape)
    spot = lax.broadcasted_iota(jnp.int32, (units, LANES), 1) // a_dev
    table = peaks[pl.ds(0, units, stride=per_tile), :]
    for q in range(1, per_tile):
        table = jnp.where(spot == q, peaks[pl.ds(q, units, stride=per_tile), :], table)
    x_top[...] = table
    x_tops[row] = table

    pl.semaphore_wait(barrier, n_row + n_col - 2)

    last = n_col - 1
    lower = col < last - col
    from_end = jnp.where(lower, col, last - col)

    def unit(k):
        b = k // groups
        n = last - 1 - from_end
        inner = jnp.where(b < n + 2, n_col - b, b - 1 - n)
        inner = jnp.where(b == 0, 0, jnp.where(b == 1, last, inner))
        d = jnp.where(from_end == 0, last - b, inner)
        return jnp.where(lower, d, last - d), k % groups

    def partner(p):
        if n_row & (n_row - 1):
            return lax.rem(row + p, n_row)
        peer, bit = row, 1
        while bit < n_row:
            if p & bit:
                peer = peer + bit - 2 * bit * ((row // bit) % 2)
            bit *= 2
        return peer

    steps = sorted(range(1, n_row), key=lambda p: (-bin(p // 2).count('1'), p))

    def x_copy(u, p):
        peer = partner(p)
        return pltpu.make_async_remote_copy(
            src_ref=turned.at[u, pl.ds(pl.multiple_of(peer * a_dev, a_dev), a_dev), :],
            dst_ref=inbox.at[u * n_row + row],
            send_sem=x_send,
            recv_sem=x_recv.at[u],
            device_id={"row": peer},
        )

    def top_copy(p):
        return pltpu.make_async_remote_copy(
            src_ref=x_top,
            dst_ref=x_tops.at[row],
            send_sem=t_send,
            recv_sem=t_recv,
            device_id={"row": partner(p)},
        )

    def wait_for(ref, start, count, sem):
        landed = ref.at[pl.ds(start, count)]
        pltpu.make_async_copy(landed, landed, sem).wait()

    def encode(block, top):
        return jnp.round(block * (CODE / top)).astype(jnp.int32).astype(jnp.int16)

    def decode(code, top):
        return code.astype(jnp.int32).astype(jnp.float32) * (top * (1.0 / CODE))

    def top_of(blocks):
        top = jnp.abs(blocks[0])
        for block in blocks[1:]:
            top = jnp.maximum(top, jnp.abs(block))
        return jnp.maximum(jnp.max(top, axis=0, keepdims=True), TINY)

    def relay_slot(at, d, g):
        return (jnp.where(d < at, d, d - 1) * groups + g) * tiles

    def own_slot(source, d, g):
        at_end = (d == 0) | (d == last)
        which = jnp.where(at_end, source - 1, jnp.where(source < d, 0, 1))
        return ((last + which) * groups + g) * tiles

    def z_copies(d, g, t):
        u = d * groups + g
        straight = ((d == 0) & (col < last)) | ((d == last) & (col > 0))
        to = jnp.where(straight, d, jnp.where(d > col, col + 1, col - 1))
        slot = jnp.where(to == d, own_slot(col, d, g), relay_slot(to, d, g)) + t
        return [
            pltpu.make_async_remote_copy(
                src_ref=src.at[u * tiles + t], dst_ref=dst.at[slot],
                send_sem=z_send.at[i], recv_sem=z_recv.at[i, slot],
                device_id={"col": to},
            )
            for i, (src, dst) in enumerate(((top_out, top_in), (code_out, code_in)))
        ]

    def held(d, g, t):
        start = pl.multiple_of(d * (share * a_dev) + g * LANES, LANES)
        return prod.at[t, pl.ds(start, LANES)]

    def add_from(d, g, t, slot):
        at = slot + t
        wait_for(top_in, at, 1, z_recv.at[0, at])
        wait_for(code_in, at, 1, z_recv.at[1, at])
        here = held(d, g, t)
        here[...] = here[...] + decode(code_in[at], top_in[at])

    def send_on(d, g, t):
        at = (d * groups + g) * tiles + t
        block = held(d, g, t)[...]
        top = top_of([block])
        top_out[at] = top
        code_out[at] = encode(block, top)
        for copy in z_copies(d, g, t):
            copy.start()

    for p in steps:
        top_copy(p).start()

    def turn(k, carry):
        d, g = unit(k)
        u = d * groups + g
        start = pl.multiple_of((pairs * a_dev) + u * LANES, LANES)
        top = x_top[pl.ds(u, 1), :]
        for t in range(tiles):
            turned[u, t * LANES:(t + 1) * LANES, :] = encode(prod[t, pl.ds(start, LANES), :].T, top)
        for p in steps:
            x_copy(u, p).start()
        return carry

    lax.fori_loop(0, units, turn, 0, unroll=2)

    gather(False)
    for i in range(n_parts):
        multiply(i, 0, None)

    piece = lax.broadcasted_iota(jnp.int32, (a_dev, LANES), 1) // a_dev

    wait_for(x_tops, 0, n_row - 1, t_recv)

    def combine(k, carry):
        d, g = unit(k)
        u = d * groups + g
        inbox[u * n_row + row] = turned[u, pl.ds(pl.multiple_of(row * a_dev, a_dev), a_dev), :]
        wait_for(inbox, u * n_row, n_row - 1, x_recv.at[u])
        for t in range(tiles):
            parts = []
            for j in range(per_tile):
                source = t * per_tile + j
                parts.append(decode(inbox[u * n_row + source], x_tops[source, pl.ds(u, 1), :]))
            sums = []
            for q in range(per_tile):
                merged = pltpu.roll(parts[0], (-q * a_dev) % LANES, 1) if q else parts[0]
                for j in range(1, per_tile):
                    shift = ((j - q) * a_dev) % LANES
                    moved = pltpu.roll(parts[j], shift, 1) if shift else parts[j]
                    merged = jnp.where(piece == j, moved, merged)
                sums.append(merged)
            here = held(d, g, t)
            here[...] = here[...] + jnp.concatenate(sums, axis=0)

        first = jnp.where(d > col, 0, last)
        at_end = (d == 0) | (d == last)
        passes = (col != first) & (jnp.logical_not(at_end) | (jnp.abs(col - first) == 1))

        @pl.when(d != col)
        def _():
            for t in range(tiles):
                @pl.when(passes)
                def _(t=t):
                    add_from(d, g, t, relay_slot(col, d, g))

                send_on(d, g, t)

        return carry

    lax.fori_loop(0, units, combine, 0)

    at_end = (col == 0) | (col == last)

    def collect(j, carry):
        beside = jnp.where(j == 0, col - 1, col + 1)
        across = jnp.where(col == 0, j + 1, last - 1 - j)
        source = jnp.where(at_end, across, beside)
        for g in range(groups):
            for t in range(tiles):
                add_from(col, g, t, own_slot(source, col, g))
        return carry

    lax.fori_loop(0, jnp.where(at_end, last - 1, 2), collect, 0)

    for t in range(tiles):
        for a in range(a_dev):
            value = prod[t, pl.ds(col * (share * a_dev) + a, share, stride=a_dev), :]
            at = a * width + t * LANES
            out_ref[:, at:at + LANES] = value.astype(out_ref.dtype)

    sent = (n_col - 1) * groups * tiles
    wait_for(x_tops, 0, n_row - 1, t_send)
    wait_for(inbox, 0, units * (n_row - 1), x_send)
    if sent:
        wait_for(top_out, 0, sent, z_send.at[0])
        wait_for(code_out, 0, sent, z_send.at[1])


def on_device(n_row, n_col, amplitudes, integrals, blocks):
    amplitudes = jnp.swapaxes(amplitudes, 1, 2)
    blocks = blocks.T
    depth, local = integrals.shape
    width = math.isqrt(local * n_row)
    a_dev = width // n_row
    pairs = blocks.shape[1] * OB * OB
    tiles = width // LANES
    share = pairs // n_col
    groups = share * a_dev // LANES
    n_parts = 4
    f32 = jnp.float32
    dma = pltpu.SemaphoreType.DMA
    units = n_col * groups
    slots = (2 * n_col - 3) * groups * tiles
    return pl.pallas_call(
        functools.partial(ladder_kernel, n_row, n_col, a_dev),
        out_shape=pltpu.VMEM((share, local), jnp.bfloat16),
        in_specs=[
            pl.BlockSpec(memory_space=pl.ANY),
            pl.BlockSpec(memory_space=pl.ANY),
            pl.BlockSpec(memory_space=pl.ANY),
        ],
        out_specs=pl.BlockSpec(memory_space=pltpu.VMEM),
        scratch_shapes=[
            pltpu.SMEM(blocks.shape, blocks.dtype),
            pltpu.VMEM(amplitudes.shape, amplitudes.dtype),
            pltpu.VMEM(integrals.shape, integrals.dtype),
            pltpu.VMEM((2 * pairs, depth), f32),
            pltpu.VMEM((tiles, 2 * pairs * a_dev, LANES), f32),
            pltpu.VMEM((units, width, LANES), jnp.int16),
            pltpu.VMEM((units * n_row, a_dev, LANES), jnp.int16),
            pltpu.VMEM((pairs, LANES), f32),
            pltpu.VMEM((units, LANES), f32),
            pltpu.VMEM((n_row, units, LANES), f32),
            pltpu.VMEM((units * tiles, LANES, LANES), jnp.int16),
            pltpu.VMEM((units * tiles, 1, LANES), f32),
            pltpu.VMEM((slots, LANES, LANES), jnp.int16),
            pltpu.VMEM((slots, 1, LANES), f32),
            dma(()),
            dma((4,)),
            dma((n_parts,)),
            dma(()),
            dma((units,)),
            dma(()),
            dma(()),
            dma((2,)),
            dma((2, slots)),
        ],
        compiler_params=pltpu.CompilerParams(
            collective_id=0, has_side_effects=True, vmem_limit_bytes=VMEM - 4 * share * local * 2
        ),
    )(blocks, amplitudes, integrals)


def solution(mesh):
    return jax.shard_map(
        functools.partial(on_device, mesh.shape["row"], mesh.shape["col"]),
        mesh=mesh,
        in_specs=(P(None, None, "col"), P("col", "row"), P()),
        out_specs=P("col", "row"),
        check_vma=False,
    )
```

```python
import functools
import math

import jax
import jax.numpy as jnp
from jax import lax
from jax.experimental import pallas as pl
from jax.experimental.pallas import tpu as pltpu
from jax.sharding import PartitionSpec as P

OB = 2
LANES = 128
CODE = 32700.0
TINY = 1e-30
ROWS = 8
VMEM = 67043328


def ladder_kernel(
    n_row, n_col, a_dev,
    blocks_hbm, amp_hbm, int_hbm, out_ref,
    blocks, amp, ints, lhs, prod, turned, inbox, peaks, x_top, x_tops,
    code_out, top_out, code_in, top_in,
    block_sem, amp_sem, int_sem, x_send, x_recv, t_send, t_recv, z_send, z_recv,
):
    row = lax.axis_index("row")
    col = lax.axis_index("col")
    pairs = lhs.shape[0] // 2
    width = a_dev * n_row
    tiles = width // LANES
    per_tile = LANES // a_dev
    share = pairs // n_col
    groups = share // per_tile
    units = n_col * groups
    occ = amp.shape[2]
    n_parts = int_sem.shape[0]
    part = ints.shape[1] // n_parts

    block_copy = pltpu.make_async_copy(blocks_hbm, blocks, block_sem)
    block_copy.start()
    amp_copies = []
    n_cuts = amp_sem.shape[0]
    planes = amp.shape[0] // n_cuts
    for i in range(n_cuts):
        cut = pl.ds(i * planes, planes if i < n_cuts - 1 else amp.shape[0] - i * planes)
        amp_copies.append(pltpu.make_async_copy(amp_hbm.at[cut], amp.at[cut], amp_sem.at[i]))
        amp_copies[i].start()
    int_copies = []
    for i in range(n_parts):
        cut = pl.ds(i * part, part)
        copy = pltpu.make_async_copy(int_hbm.at[:, cut], ints.at[:, cut], int_sem.at[i])
        int_copies.append(copy)

    barrier = pltpu.get_barrier_semaphore()

    def greet(p, carry):
        pl.semaphore_signal(barrier, inc=1, device_id={"row": lax.rem(row + p, n_row)})
        return carry

    lax.fori_loop(1, n_row, greet, 0)

    def greet_col(p, carry):
        pl.semaphore_signal(barrier, inc=1, device_id={"col": lax.rem(col + p, n_col)})
        return carry

    lax.fori_loop(1, n_col, greet_col, 0)

    amp_copies[0].wait()
    for copy in int_copies:
        copy.start()
    block_copy.wait()
    for copy in amp_copies[1:]:
        copy.wait()
    spot_row = lax.broadcasted_iota(jnp.int32, (ROWS, occ), 0)
    spot_col = lax.broadcasted_iota(jnp.int32, (ROWS, occ), 1)

    def take(spots, plane):
        hit = jnp.zeros((ROWS, occ), jnp.bool_)
        for at, column in spots:
            hit = hit | ((spot_row == at) & (spot_col == column))
        chosen = jnp.where(hit, 1.0, 0.0).astype(amp.dtype)
        return lax.dot_general(
            chosen, amp[plane], (((1,), (1,)), ((), ())), preferred_element_type=jnp.float32
        )

    per_rows = ROWS // (OB * OB)

    def gather(mirrored):
        for tile in range(pairs // ROWS):
            found = jnp.zeros((ROWS, lhs.shape[1]), jnp.float32)
            for k in range(per_rows):
                upper = blocks[0, tile * per_rows + k] * OB
                lower = blocks[1, tile * per_rows + k] * OB
                base = k * OB * OB
                for m in range(OB):
                    if mirrored:
                        found += take([(base + u * OB + m, upper + u) for u in range(OB)], lower + m)
                    else:
                        found += take([(base + m * OB + v, lower + v) for v in range(OB)], upper + m)
            at = (pairs if mirrored else 0) + tile * ROWS
            lhs[at:at + ROWS, :] = found

    gather(True)

    def multiply(i, first, peak):
        block = lhs[first:first + pairs, :].astype(jnp.bfloat16)

        def one(step, peak):
            a = i * (part // width) + step
            panel = ints[:, pl.ds(pl.multiple_of(a * width, width), width)]
            got = jnp.dot(block, panel, preferred_element_type=jnp.float32)
            for t in range(tiles):
                piece = got[:, t * LANES:(t + 1) * LANES]
                prod[t, pl.ds(first * a_dev + a, pairs, stride=a_dev), :] = piece
                if peak is not None:
                    peak = jnp.maximum(peak, jnp.abs(piece))
            return peak

        return lax.fori_loop(0, part // width, one, peak, unroll=8)

    peak = jnp.full((pairs, LANES), TINY, jnp.float32)
    for i in range(n_parts):
        int_copies[i].wait()
        peak = multiply(i, pairs, peak)

    peaks[...] = jnp.broadcast_to(jnp.max(peak, axis=1, keepdims=True), peaks.shape)
    spot = lax.broadcasted_iota(jnp.int32, (units, LANES), 1) // a_dev
    table = peaks[pl.ds(0, units, stride=per_tile), :]
    for q in range(1, per_tile):
        table = jnp.where(spot == q, peaks[pl.ds(q, units, stride=per_tile), :], table)
    x_top[...] = table
    x_tops[row] = table

    pl.semaphore_wait(barrier, n_row + n_col - 2)

    last = n_col - 1
    lower = col < last - col
    from_end = jnp.where(lower, col, last - col)

    def unit(k):
        b = k // groups
        n = last - 1 - from_end
        inner = jnp.where(b < n + 2, n_col - b, b - 1 - n)
        inner = jnp.where(b == 0, 0, jnp.where(b == 1, last, inner))
        d = jnp.where(from_end == 0, last - b, inner)
        return jnp.where(lower, d, last - d), k % groups

    def partner(p):
        if n_row & (n_row - 1):
            return lax.rem(row + p, n_row)
        peer, bit = row, 1
        while bit < n_row:
            if p & bit:
                peer = peer + bit - 2 * bit * ((row // bit) % 2)
            bit *= 2
        return peer

    near = sorted(range(2, min(per_tile, n_row)), key=lambda p: (-bin(p // 2).count('1'), p))
    far = sorted(range(per_tile, n_row), key=lambda p: (-bin(p // 2).count('1'), p))
    steps = near + far + [1]
    own_tile = row // per_tile

    def x_copy(u, p):
        peer = partner(p)
        return pltpu.make_async_remote_copy(
            src_ref=turned.at[u, pl.ds(pl.multiple_of(peer * a_dev, a_dev), a_dev), :],
            dst_ref=inbox.at[u * n_row + row],
            send_sem=x_send,
            recv_sem=x_recv.at[u * tiles + own_tile],
            device_id={"row": peer},
        )

    def top_copy(p):
        return pltpu.make_async_remote_copy(
            src_ref=x_top,
            dst_ref=x_tops.at[row],
            send_sem=t_send,
            recv_sem=t_recv.at[own_tile],
            device_id={"row": partner(p)},
        )

    def wait_for(ref, start, count, sem):
        landed = ref.at[pl.ds(start, count)]
        pltpu.make_async_copy(landed, landed, sem).wait()

    def encode(block, top):
        return jnp.round(block * (CODE / top)).astype(jnp.int32).astype(jnp.int16)

    def decode(code, top):
        return code.astype(jnp.int32).astype(jnp.float32) * (top * (1.0 / CODE))

    def top_of(blocks):
        top = jnp.abs(blocks[0])
        for block in blocks[1:]:
            top = jnp.maximum(top, jnp.abs(block))
        return jnp.maximum(jnp.max(top, axis=0, keepdims=True), TINY)

    def relay_slot(at, d, g):
        return (jnp.where(d < at, d, d - 1) * groups + g) * tiles

    def own_slot(source, d, g):
        at_end = (d == 0) | (d == last)
        which = jnp.where(at_end, source - 1, jnp.where(source < d, 0, 1))
        return ((last + which) * groups + g) * tiles

    def z_copies(d, g, t):
        u = d * groups + g
        straight = ((d == 0) & (col < last)) | ((d == last) & (col > 0))
        to = jnp.where(straight, d, jnp.where(d > col, col + 1, col - 1))
        slot = jnp.where(to == d, own_slot(col, d, g), relay_slot(to, d, g)) + t
        return [
            pltpu.make_async_remote_copy(
                src_ref=src.at[u * tiles + t], dst_ref=dst.at[slot],
                send_sem=z_send, recv_sem=z_recv.at[slot],
                device_id={"col": to},
            )
            for src, dst in ((top_out, top_in), (code_out, code_in))
        ]

    def held(d, g, t):
        start = pl.multiple_of(d * (share * a_dev) + g * LANES, LANES)
        return prod.at[t, pl.ds(start, LANES)]

    message = LANES // 2 + 1

    def add_from(d, g, t, slot):
        at = slot + t
        wait_for(prod.at[0], 0, message, z_recv.at[at])
        here = held(d, g, t)
        here[...] = here[...] + decode(code_in[at], top_in[at])

    def send_on(d, g, t):
        at = (d * groups + g) * tiles + t
        block = held(d, g, t)[...]
        top = top_of([block])
        top_out[at] = top
        code_out[at] = encode(block, top)
        for copy in z_copies(d, g, t):
            copy.start()

    for p in steps:
        top_copy(p).start()

    def turn(k, carry):
        d, g = unit(k)
        u = d * groups + g
        start = pl.multiple_of((pairs * a_dev) + u * LANES, LANES)
        for t in range(tiles):
            codes = [
                encode(
                    prod[t, pl.ds(pl.multiple_of(start + q * a_dev, a_dev), a_dev), :],
                    peaks[pl.ds(u * per_tile + q, 1), :],
                )
                for q in range(per_tile)
            ]
            turned[u, t * LANES:(t + 1) * LANES, :] = jnp.concatenate(codes, axis=0).T
        for p in steps:
            x_copy(u, p).start()
        return carry

    lax.fori_loop(0, units, turn, 0, unroll=2)

    gather(False)
    for i in range(n_parts):
        multiply(i, 0, None)

    piece = lax.broadcasted_iota(jnp.int32, (a_dev, LANES), 1) // a_dev

    def combine(k, carry):
        d, g = unit(k)
        u = d * groups + g
        inbox[u * n_row + row] = turned[u, pl.ds(pl.multiple_of(row * a_dev, a_dev), a_dev), :]
        first = jnp.where(d > col, 0, last)
        at_end = (d == 0) | (d == last)
        passes = (col != first) & (jnp.logical_not(at_end) | (jnp.abs(col - first) == 1))
        for i in range(tiles):
            t = lax.rem(own_tile + i, tiles)
            count = per_tile if i else per_tile - 1

            @pl.when(k == 0)
            def _(t=t, count=count):
                wait_for(x_tops, 0, count, t_recv.at[t])

            wait_for(inbox, u * n_row, count, x_recv.at[u * tiles + t])
            parts = []
            for j in range(per_tile):
                source = t * per_tile + j
                parts.append(decode(inbox[u * n_row + source], x_tops[source, pl.ds(u, 1), :]))
            sums = []
            for q in range(per_tile):
                merged = pltpu.roll(parts[0], (-q * a_dev) % LANES, 1) if q else parts[0]
                for j in range(1, per_tile):
                    shift = ((j - q) * a_dev) % LANES
                    moved = pltpu.roll(parts[j], shift, 1) if shift else parts[j]
                    merged = jnp.where(piece == j, moved, merged)
                sums.append(merged)
            here = held(d, g, t)
            here[...] = here[...] + jnp.concatenate(sums, axis=0)

            @pl.when(d != col)
            def _(t=t):
                @pl.when(passes)
                def _():
                    add_from(d, g, t, relay_slot(col, d, g))

                send_on(d, g, t)

        return carry

    lax.fori_loop(0, units, combine, 0)

    at_end = (col == 0) | (col == last)

    def collect(j, carry):
        beside = jnp.where(j == 0, col - 1, col + 1)
        across = jnp.where(col == 0, j + 1, last - 1 - j)
        source = jnp.where(at_end, across, beside)
        for g in range(groups):
            for i in range(tiles):
                t = lax.rem(own_tile + i, tiles)
                add_from(col, g, t, own_slot(source, col, g))
        return carry

    lax.fori_loop(0, jnp.where(at_end, last - 1, 2), collect, 0)

    for t in range(tiles):
        for a in range(a_dev):
            value = prod[t, pl.ds(col * (share * a_dev) + a, share, stride=a_dev), :]
            at = a * width + t * LANES
            out_ref[:, at:at + LANES] = value.astype(out_ref.dtype)

    sent = (n_col - 1) * groups * tiles
    wait_for(x_tops, 0, n_row - 1, t_send)
    wait_for(inbox, 0, units * (n_row - 1), x_send)
    wait_for(prod.at[0], 0, sent * message, z_send)


def on_device(n_row, n_col, amplitudes, integrals, blocks):
    amplitudes = jnp.swapaxes(amplitudes, 1, 2)
    blocks = blocks.T
    depth, local = integrals.shape
    width = math.isqrt(local * n_row)
    a_dev = width // n_row
    pairs = blocks.shape[1] * OB * OB
    tiles = width // LANES
    share = pairs // n_col
    groups = share * a_dev // LANES
    n_parts = 4
    f32 = jnp.float32
    dma = pltpu.SemaphoreType.DMA
    units = n_col * groups
    slots = (2 * n_col - 3) * groups * tiles
    return pl.pallas_call(
        functools.partial(ladder_kernel, n_row, n_col, a_dev),
        out_shape=pltpu.VMEM((share, local), jnp.bfloat16),
        in_specs=[
            pl.BlockSpec(memory_space=pl.ANY),
            pl.BlockSpec(memory_space=pl.ANY),
            pl.BlockSpec(memory_space=pl.ANY),
        ],
        out_specs=pl.BlockSpec(memory_space=pltpu.VMEM),
        scratch_shapes=[
            pltpu.SMEM(blocks.shape, blocks.dtype),
            pltpu.VMEM(amplitudes.shape, amplitudes.dtype),
            pltpu.VMEM(integrals.shape, integrals.dtype),
            pltpu.VMEM((2 * pairs, depth), f32),
            pltpu.VMEM((tiles, 2 * pairs * a_dev, LANES), f32),
            pltpu.VMEM((units, width, LANES), jnp.int16),
            pltpu.VMEM((units * n_row, a_dev, LANES), jnp.int16),
            pltpu.VMEM((pairs, LANES), f32),
            pltpu.VMEM((units, LANES), f32),
            pltpu.VMEM((n_row, units, LANES), f32),
            pltpu.VMEM((units * tiles, LANES, LANES), jnp.int16),
            pltpu.VMEM((units * tiles, 1, LANES), f32),
            pltpu.VMEM((slots, LANES, LANES), jnp.int16),
            pltpu.VMEM((slots, 1, LANES), f32),
            dma(()),
            dma((4,)),
            dma((n_parts,)),
            dma(()),
            dma((units * tiles,)),
            dma(()),
            dma((tiles,)),
            dma(()),
            dma((slots,)),
        ],
        compiler_params=pltpu.CompilerParams(
            collective_id=0, has_side_effects=True, vmem_limit_bytes=VMEM - 4 * share * local * 2
        ),
    )(blocks, amplitudes, integrals)


def solution(mesh):
    return jax.shard_map(
        functools.partial(on_device, mesh.shape["row"], mesh.shape["col"]),
        mesh=mesh,
        in_specs=(P(None, None, "col"), P("col", "row"), P()),
        out_specs=P("col", "row"),
        check_vma=False,
    )
```

```python
import functools
import math

import jax
import jax.numpy as jnp
from jax import lax
from jax.experimental import pallas as pl
from jax.experimental.pallas import tpu as pltpu
from jax.sharding import PartitionSpec as P

OB = 2
LANES = 128
CODE = 32700.0
TINY = 1e-30
ROWS = 8
VMEM = 67043328


def ladder_kernel(
    n_row, n_col, a_dev,
    blocks_hbm, amp_hbm, int_hbm, out_ref,
    blocks, amp, ints, lhs, prod, turned, inbox, peaks, x_top, x_tops,
    code_out, top_out, code_in, top_in,
    block_sem, amp_sem, int_sem, x_send, x_recv, t_send, t_recv, z_send, z_recv,
):
    row = lax.axis_index("row")
    col = lax.axis_index("col")
    pairs = lhs.shape[0] // 2
    width = a_dev * n_row
    tiles = width // LANES
    per_tile = LANES // a_dev
    share = pairs // n_col
    groups = share // per_tile
    units = n_col * groups
    occ = amp.shape[2]
    n_parts = int_sem.shape[0]
    part = ints.shape[1] // n_parts

    block_copy = pltpu.make_async_copy(blocks_hbm, blocks, block_sem)
    block_copy.start()
    amp_copies = []
    n_cuts = amp_sem.shape[0]
    planes = amp.shape[0] // n_cuts
    for i in range(n_cuts):
        cut = pl.ds(i * planes, planes if i < n_cuts - 1 else amp.shape[0] - i * planes)
        amp_copies.append(pltpu.make_async_copy(amp_hbm.at[cut], amp.at[cut], amp_sem.at[i]))
        amp_copies[i].start()
    int_copies = []
    for i in range(n_parts):
        cut = pl.ds(i * part, part)
        copy = pltpu.make_async_copy(int_hbm.at[:, cut], ints.at[:, cut], int_sem.at[i])
        int_copies.append(copy)

    barrier = pltpu.get_barrier_semaphore()

    def greet(p, carry):
        pl.semaphore_signal(barrier, inc=1, device_id={"row": lax.rem(row + p, n_row)})
        return carry

    lax.fori_loop(1, n_row, greet, 0)

    def greet_col(p, carry):
        pl.semaphore_signal(barrier, inc=1, device_id={"col": lax.rem(col + p, n_col)})
        return carry

    lax.fori_loop(1, n_col, greet_col, 0)

    amp_copies[0].wait()
    for copy in int_copies:
        copy.start()
    block_copy.wait()
    for copy in amp_copies[1:]:
        copy.wait()
    spot_row = lax.broadcasted_iota(jnp.int32, (ROWS, occ), 0)
    spot_col = lax.broadcasted_iota(jnp.int32, (ROWS, occ), 1)

    def take(spots, plane):
        hit = jnp.zeros((ROWS, occ), jnp.bool_)
        for at, column in spots:
            hit = hit | ((spot_row == at) & (spot_col == column))
        chosen = jnp.where(hit, 1.0, 0.0).astype(amp.dtype)
        return lax.dot_general(
            chosen, amp[plane], (((1,), (1,)), ((), ())), preferred_element_type=jnp.float32
        )

    per_rows = ROWS // (OB * OB)

    def gather(mirrored):
        for tile in range(pairs // ROWS):
            found = jnp.zeros((ROWS, lhs.shape[1]), jnp.float32)
            for k in range(per_rows):
                upper = blocks[0, tile * per_rows + k] * OB
                lower = blocks[1, tile * per_rows + k] * OB
                base = k * OB * OB
                for m in range(OB):
                    if mirrored:
                        found += take([(base + u * OB + m, upper + u) for u in range(OB)], lower + m)
                    else:
                        found += take([(base + m * OB + v, lower + v) for v in range(OB)], upper + m)
            at = (pairs if mirrored else 0) + tile * ROWS
            lhs[at:at + ROWS, :] = found

    gather(True)

    def multiply(i, first, peak):
        block = lhs[first:first + pairs, :].astype(jnp.bfloat16)

        def one(step, peak):
            a = i * (part // width) + step
            panel = ints[:, pl.ds(pl.multiple_of(a * width, width), width)]
            got = jnp.dot(block, panel, preferred_element_type=jnp.float32)
            for t in range(tiles):
                piece = got[:, t * LANES:(t + 1) * LANES]
                prod[t, pl.ds(first * a_dev + a, pairs, stride=a_dev), :] = piece
                if peak is not None:
                    peak = jnp.maximum(peak, jnp.abs(piece))
            return peak

        return lax.fori_loop(0, part // width, one, peak, unroll=16)

    peak = jnp.full((pairs, LANES), TINY, jnp.float32)
    for i in range(n_parts):
        int_copies[i].wait()
        peak = multiply(i, pairs, peak)

    peaks[...] = jnp.broadcast_to(jnp.max(peak, axis=1, keepdims=True), peaks.shape)
    spot = lax.broadcasted_iota(jnp.int32, (units, LANES), 1) // a_dev
    table = peaks[pl.ds(0, units, stride=per_tile), :]
    for q in range(1, per_tile):
        table = jnp.where(spot == q, peaks[pl.ds(q, units, stride=per_tile), :], table)
    x_top[...] = table
    x_tops[row] = table

    pl.semaphore_wait(barrier, n_row + n_col - 2)

    last = n_col - 1
    lower = col < last - col
    from_end = jnp.where(lower, col, last - col)

    def unit(k):
        b = k // groups
        n = last - 1 - from_end
        inner = jnp.where(b < n + 2, n_col - b, b - 1 - n)
        inner = jnp.where(b == 0, 0, jnp.where(b == 1, last, inner))
        d = jnp.where(from_end == 0, last - b, inner)
        return jnp.where(lower, d, last - d), k % groups

    def partner(p):
        if n_row & (n_row - 1):
            return lax.rem(row + p, n_row)
        peer, bit = row, 1
        while bit < n_row:
            if p & bit:
                peer = peer + bit - 2 * bit * ((row // bit) % 2)
            bit *= 2
        return peer

    near = sorted(range(2, min(per_tile, n_row)), key=lambda p: (-bin(p // 2).count('1'), p))
    far = sorted(range(per_tile, n_row), key=lambda p: (-bin(p // 2).count('1'), p))
    own_tile = row // per_tile

    def x_copy(u, p):
        peer = partner(p)
        return pltpu.make_async_remote_copy(
            src_ref=turned.at[u, pl.ds(pl.multiple_of(peer * a_dev, a_dev), a_dev), :],
            dst_ref=inbox.at[u * n_row + row],
            send_sem=x_send,
            recv_sem=x_recv.at[u * tiles + own_tile],
            device_id={"row": peer},
        )

    def top_copy(p):
        return pltpu.make_async_remote_copy(
            src_ref=x_top,
            dst_ref=x_tops.at[row],
            send_sem=t_send,
            recv_sem=t_recv.at[own_tile],
            device_id={"row": partner(p)},
        )

    def wait_for(ref, start, count, sem):
        landed = ref.at[pl.ds(start, count)]
        pltpu.make_async_copy(landed, landed, sem).wait()

    def encode(block, top):
        return jnp.round(block * (CODE / top)).astype(jnp.int32).astype(jnp.int16)

    def decode(code, top):
        return code.astype(jnp.int32).astype(jnp.float32) * (top * (1.0 / CODE))

    def top_of(blocks):
        top = jnp.abs(blocks[0])
        for block in blocks[1:]:
            top = jnp.maximum(top, jnp.abs(block))
        return jnp.maximum(jnp.max(top, axis=0, keepdims=True), TINY)

    def relay_slot(at, d, g):
        return (jnp.where(d < at, d, d - 1) * groups + g) * tiles

    def own_slot(source, d, g):
        at_end = (d == 0) | (d == last)
        which = jnp.where(at_end, source - 1, jnp.where(source < d, 0, 1))
        return ((last + which) * groups + g) * tiles

    def z_copies(d, g, t):
        u = d * groups + g
        straight = ((d == 0) & (col < last)) | ((d == last) & (col > 0))
        to = jnp.where(straight, d, jnp.where(d > col, col + 1, col - 1))
        slot = jnp.where(to == d, own_slot(col, d, g), relay_slot(to, d, g)) + t
        return [
            pltpu.make_async_remote_copy(
                src_ref=src.at[u * tiles + t], dst_ref=dst.at[slot],
                send_sem=z_send, recv_sem=z_recv.at[slot],
                device_id={"col": to},
            )
            for src, dst in ((top_out, top_in), (code_out, code_in))
        ]

    def held(d, g, t):
        start = pl.multiple_of(d * (share * a_dev) + g * LANES, LANES)
        return prod.at[t, pl.ds(start, LANES)]

    message = LANES // 2 + 1

    def add_from(d, g, t, slot):
        at = slot + t
        wait_for(prod.at[0], 0, message, z_recv.at[at])
        here = held(d, g, t)
        here[...] = here[...] + decode(code_in[at], top_in[at])

    def send_on(d, g, t):
        at = (d * groups + g) * tiles + t
        block = held(d, g, t)[...]
        top = top_of([block])
        top_out[at] = top
        code_out[at] = encode(block, top)
        for copy in z_copies(d, g, t):
            copy.start()

    for p in near:
        top_copy(p).start()

    def turn(k, carry):
        d, g = unit(k)
        u = d * groups + g
        start = pl.multiple_of((pairs * a_dev) + u * LANES, LANES)
        for t in range(tiles):
            codes = [
                encode(
                    prod[t, pl.ds(pl.multiple_of(start + q * a_dev, a_dev), a_dev), :],
                    peaks[pl.ds(u * per_tile + q, 1), :],
                )
                for q in range(per_tile)
            ]
            turned[u, t * LANES:(t + 1) * LANES, :] = jnp.concatenate(codes, axis=0).T
        for p in near:
            x_copy(u, p).start()

        @pl.when(k == 0)
        def _():
            for p in far + [1]:
                top_copy(p).start()

        for p in far + [1]:
            x_copy(u, p).start()
        return carry

    lax.fori_loop(0, units, turn, 0, unroll=2)

    gather(False)
    for i in range(n_parts):
        multiply(i, 0, None)

    piece = lax.broadcasted_iota(jnp.int32, (a_dev, LANES), 1) // a_dev

    def combine(k, carry):
        d, g = unit(k)
        u = d * groups + g
        inbox[u * n_row + row] = turned[u, pl.ds(pl.multiple_of(row * a_dev, a_dev), a_dev), :]
        first = jnp.where(d > col, 0, last)
        at_end = (d == 0) | (d == last)
        passes = (col != first) & (jnp.logical_not(at_end) | (jnp.abs(col - first) == 1))
        for i in range(tiles):
            t = lax.rem(own_tile + i, tiles)
            count = per_tile if i else per_tile - 1

            @pl.when(k == 0)
            def _(t=t, count=count):
                wait_for(x_tops, 0, count, t_recv.at[t])

            wait_for(inbox, u * n_row, count, x_recv.at[u * tiles + t])
            parts = []
            for j in range(per_tile):
                source = t * per_tile + j
                parts.append(decode(inbox[u * n_row + source], x_tops[source, pl.ds(u, 1), :]))
            sums = []
            for q in range(per_tile):
                merged = pltpu.roll(parts[0], (-q * a_dev) % LANES, 1) if q else parts[0]
                for j in range(1, per_tile):
                    shift = ((j - q) * a_dev) % LANES
                    moved = pltpu.roll(parts[j], shift, 1) if shift else parts[j]
                    merged = jnp.where(piece == j, moved, merged)
                sums.append(merged)
            here = held(d, g, t)
            here[...] = here[...] + jnp.concatenate(sums, axis=0)

            @pl.when(d != col)
            def _(t=t):
                @pl.when(passes)
                def _():
                    add_from(d, g, t, relay_slot(col, d, g))

                send_on(d, g, t)

        return carry

    lax.fori_loop(0, units, combine, 0)

    at_end = (col == 0) | (col == last)
    sources = jnp.where(at_end, last - 1, 2)

    def source_of(j):
        beside = jnp.where(j == 0, col - 1, col + 1)
        across = jnp.where(col == 0, j + 1, last - 1 - j)
        return jnp.where(at_end, across, beside)

    def collect(j, g):
        for i in range(tiles):
            t = lax.rem(own_tile + i, tiles)
            add_from(col, g, t, own_slot(source_of(j), col, g))

    def collect_all(j, carry):
        for g in range(groups):
            collect(j, g)
        return carry

    lax.fori_loop(0, sources - 1, collect_all, 0)
    for g in range(groups - 1):
        collect(sources - 1, g)
    for i in range(tiles):
        t = lax.rem(own_tile + i, tiles)
        add_from(col, groups - 1, t, own_slot(source_of(sources - 1), col, groups - 1))
        for a in range(a_dev):
            value = prod[t, pl.ds(col * (share * a_dev) + a, share, stride=a_dev), :]
            at = pl.multiple_of(a * width + t * LANES, LANES)
            out_ref[:, pl.ds(at, LANES)] = value.astype(out_ref.dtype)

    sent = (n_col - 1) * groups * tiles
    wait_for(x_tops, 0, n_row - 1, t_send)
    wait_for(inbox, 0, units * (n_row - 1), x_send)
    wait_for(prod.at[0], 0, sent * message, z_send)


def on_device(n_row, n_col, amplitudes, integrals, blocks):
    amplitudes = jnp.swapaxes(amplitudes, 1, 2)
    blocks = blocks.T
    depth, local = integrals.shape
    width = math.isqrt(local * n_row)
    a_dev = width // n_row
    pairs = blocks.shape[1] * OB * OB
    tiles = width // LANES
    share = pairs // n_col
    groups = share * a_dev // LANES
    n_parts = 2
    f32 = jnp.float32
    dma = pltpu.SemaphoreType.DMA
    units = n_col * groups
    slots = (2 * n_col - 3) * groups * tiles
    return pl.pallas_call(
        functools.partial(ladder_kernel, n_row, n_col, a_dev),
        out_shape=pltpu.VMEM((share, local), jnp.bfloat16),
        in_specs=[
            pl.BlockSpec(memory_space=pl.ANY),
            pl.BlockSpec(memory_space=pl.ANY),
            pl.BlockSpec(memory_space=pl.ANY),
        ],
        out_specs=pl.BlockSpec(memory_space=pltpu.VMEM),
        scratch_shapes=[
            pltpu.SMEM(blocks.shape, blocks.dtype),
            pltpu.VMEM(amplitudes.shape, amplitudes.dtype),
            pltpu.VMEM(integrals.shape, integrals.dtype),
            pltpu.VMEM((2 * pairs, depth), f32),
            pltpu.VMEM((tiles, 2 * pairs * a_dev, LANES), f32),
            pltpu.VMEM((units, width, LANES), jnp.int16),
            pltpu.VMEM((units * n_row, a_dev, LANES), jnp.int16),
            pltpu.VMEM((pairs, LANES), f32),
            pltpu.VMEM((units, LANES), f32),
            pltpu.VMEM((n_row, units, LANES), f32),
            pltpu.VMEM((units * tiles, LANES, LANES), jnp.int16),
            pltpu.VMEM((units * tiles, 1, LANES), f32),
            pltpu.VMEM((slots, LANES, LANES), jnp.int16),
            pltpu.VMEM((slots, 1, LANES), f32),
            dma(()),
            dma((4,)),
            dma((n_parts,)),
            dma(()),
            dma((units * tiles,)),
            dma(()),
            dma((tiles,)),
            dma(()),
            dma((slots,)),
        ],
        compiler_params=pltpu.CompilerParams(
            collective_id=0, has_side_effects=True, vmem_limit_bytes=VMEM - 4 * share * local * 2
        ),
    )(blocks, amplitudes, integrals)


def solution(mesh):
    return jax.shard_map(
        functools.partial(on_device, mesh.shape["row"], mesh.shape["col"]),
        mesh=mesh,
        in_specs=(P(None, None, "col"), P("col", "row"), P()),
        out_specs=P("col", "row"),
        check_vma=False,
    )
```

```python
import functools
import math

import jax
import jax.numpy as jnp
from jax import lax
from jax.experimental import pallas as pl
from jax.experimental.pallas import tpu as pltpu
from jax.sharding import PartitionSpec as P

OB = 2
LANES = 128
CODE = 32700.0
TINY = 1e-30
PACKED = 4
ROWS = 8
VMEM = 67043328


def ladder_kernel(
    n_row, n_col, a_dev,
    blocks_hbm, amp_hbm, int_hbm, out_ref,
    blocks, amp, ints, lhs, prod, turned, inbox, peaks, x_top, x_tops, x_wide,
    code_out, top_out, code_in, top_in,
    block_sem, amp_sem, int_sem, x_send, x_recv, t_send, t_recv, z_send, z_recv,
):
    row = lax.axis_index("row")
    col = lax.axis_index("col")
    pairs = lhs.shape[0] // 2
    width = a_dev * n_row
    tiles = width // LANES
    per_tile = LANES // a_dev
    share = pairs // n_col
    groups = share // per_tile
    units = n_col * groups
    occ = amp.shape[2]
    n_parts = int_sem.shape[0]
    part = ints.shape[1] // n_parts

    block_copy = pltpu.make_async_copy(blocks_hbm, blocks, block_sem)
    block_copy.start()
    amp_copies = []
    n_cuts = amp_sem.shape[0]
    planes = amp.shape[0] // n_cuts
    for i in range(n_cuts):
        cut = pl.ds(i * planes, planes if i < n_cuts - 1 else amp.shape[0] - i * planes)
        amp_copies.append(pltpu.make_async_copy(amp_hbm.at[cut], amp.at[cut], amp_sem.at[i]))
        amp_copies[i].start()
    int_copies = []
    for i in range(n_parts):
        cut = pl.ds(i * part, part)
        copy = pltpu.make_async_copy(int_hbm.at[:, cut], ints.at[:, cut], int_sem.at[i])
        int_copies.append(copy)

    barrier = pltpu.get_barrier_semaphore()

    def greet(p, carry):
        pl.semaphore_signal(barrier, inc=1, device_id={"row": lax.rem(row + p, n_row)})
        return carry

    lax.fori_loop(1, n_row, greet, 0)

    def greet_col(p, carry):
        pl.semaphore_signal(barrier, inc=1, device_id={"col": lax.rem(col + p, n_col)})
        return carry

    lax.fori_loop(1, n_col, greet_col, 0)

    amp_copies[0].wait()
    for copy in int_copies:
        copy.start()
    block_copy.wait()
    for copy in amp_copies[1:]:
        copy.wait()
    spot_row = lax.broadcasted_iota(jnp.int32, (ROWS, occ), 0)
    spot_col = lax.broadcasted_iota(jnp.int32, (ROWS, occ), 1)

    def take(spots, plane):
        hit = jnp.zeros((ROWS, occ), jnp.bool_)
        for at, column in spots:
            hit = hit | ((spot_row == at) & (spot_col == column))
        chosen = jnp.where(hit, 1.0, 0.0).astype(amp.dtype)
        return lax.dot_general(
            chosen, amp[plane], (((1,), (1,)), ((), ())), preferred_element_type=jnp.float32
        )

    per_rows = ROWS // (OB * OB)

    def gather(mirrored):
        for tile in range(pairs // ROWS):
            found = jnp.zeros((ROWS, lhs.shape[1]), jnp.float32)
            for k in range(per_rows):
                upper = blocks[0, tile * per_rows + k] * OB
                lower = blocks[1, tile * per_rows + k] * OB
                base = k * OB * OB
                for m in range(OB):
                    if mirrored:
                        found += take([(base + u * OB + m, upper + u) for u in range(OB)], lower + m)
                    else:
                        found += take([(base + m * OB + v, lower + v) for v in range(OB)], upper + m)
            at = (pairs if mirrored else 0) + tile * ROWS
            lhs[at:at + ROWS, :] = found

    gather(True)

    def multiply(i, first, peak):
        block = lhs[first:first + pairs, :].astype(jnp.bfloat16)

        def one(step, peak):
            a = i * (part // width) + step
            panel = ints[:, pl.ds(pl.multiple_of(a * width, width), width)]
            got = jnp.dot(block, panel, preferred_element_type=jnp.float32)
            for t in range(tiles):
                piece = got[:, t * LANES:(t + 1) * LANES]
                prod[t, pl.ds(first * a_dev + a, pairs, stride=a_dev), :] = piece
                if peak is not None:
                    peak = jnp.maximum(peak, jnp.abs(piece))
            return peak

        return lax.fori_loop(0, part // width, one, peak, unroll=16)

    peak = jnp.full((pairs, LANES), TINY, jnp.float32)
    for i in range(n_parts):
        int_copies[i].wait()
        peak = multiply(i, pairs, peak)

    peaks[...] = jnp.broadcast_to(jnp.max(peak, axis=1, keepdims=True), peaks.shape)
    n_rows = x_top.shape[0]
    packed = units // n_rows
    wide = a_dev // packed
    spot = lax.broadcasted_iota(jnp.int32, (n_rows, LANES), 1) // wide
    table = peaks[pl.ds(0, n_rows, stride=packed * per_tile), :]
    for m in range(packed):
        for q in range(per_tile):
            some = peaks[pl.ds(m * per_tile + q, n_rows, stride=packed * per_tile), :]
            table = jnp.where(spot == q * packed + m, some, table)
    x_top[...] = table
    x_tops[row] = table

    pl.semaphore_wait(barrier, n_row + n_col - 2)

    last = n_col - 1
    lower = col < last - col
    from_end = jnp.where(lower, col, last - col)

    def unit(k):
        b = k // groups
        n = last - 1 - from_end
        inner = jnp.where(b < n + 2, n_col - b, b - 1 - n)
        inner = jnp.where(b == 0, 0, jnp.where(b == 1, last, inner))
        d = jnp.where(from_end == 0, last - b, inner)
        return jnp.where(lower, d, last - d), k % groups

    def partner(p):
        if n_row & (n_row - 1):
            return lax.rem(row + p, n_row)
        peer, bit = row, 1
        while bit < n_row:
            if p & bit:
                peer = peer + bit - 2 * bit * ((row // bit) % 2)
            bit *= 2
        return peer

    near = sorted(range(2, min(per_tile, n_row)), key=lambda p: (-bin(p // 2).count('1'), p))
    far = sorted(range(per_tile, n_row), key=lambda p: (-bin(p // 2).count('1'), p))
    own_tile = row // per_tile

    def x_copy(u, p):
        peer = partner(p)
        return pltpu.make_async_remote_copy(
            src_ref=turned.at[u, pl.ds(pl.multiple_of(peer * a_dev, a_dev), a_dev), :],
            dst_ref=inbox.at[u * n_row + row],
            send_sem=x_send,
            recv_sem=x_recv.at[u * tiles + own_tile],
            device_id={"row": peer},
        )

    def top_copy(p):
        return pltpu.make_async_remote_copy(
            src_ref=x_top,
            dst_ref=x_tops.at[row],
            send_sem=t_send,
            recv_sem=t_recv.at[own_tile],
            device_id={"row": partner(p)},
        )

    def wait_for(ref, start, count, sem):
        landed = ref.at[pl.ds(start, count)]
        pltpu.make_async_copy(landed, landed, sem).wait()

    def encode(block, top):
        return jnp.round(block * (CODE / top)).astype(jnp.int32).astype(jnp.int16)

    def decode(code, top):
        return code.astype(jnp.int32).astype(jnp.float32) * (top * (1.0 / CODE))

    def top_of(blocks):
        top = jnp.abs(blocks[0])
        for block in blocks[1:]:
            top = jnp.maximum(top, jnp.abs(block))
        return jnp.maximum(jnp.max(top, axis=0, keepdims=True), TINY)

    def relay_slot(at, d, g):
        return (jnp.where(d < at, d, d - 1) * groups + g) * tiles

    def own_slot(source, d, g):
        at_end = (d == 0) | (d == last)
        which = jnp.where(at_end, source - 1, jnp.where(source < d, 0, 1))
        return ((last + which) * groups + g) * tiles

    def z_copies(d, g, t):
        u = d * groups + g
        straight = ((d == 0) & (col < last)) | ((d == last) & (col > 0))
        to = jnp.where(straight, d, jnp.where(d > col, col + 1, col - 1))
        slot = jnp.where(to == d, own_slot(col, d, g), relay_slot(to, d, g)) + t
        return [
            pltpu.make_async_remote_copy(
                src_ref=src.at[u * tiles + t], dst_ref=dst.at[slot],
                send_sem=z_send, recv_sem=z_recv.at[slot],
                device_id={"col": to},
            )
            for src, dst in ((top_out, top_in), (code_out, code_in))
        ]

    def held(d, g, t):
        start = pl.multiple_of(d * (share * a_dev) + g * LANES, LANES)
        return prod.at[t, pl.ds(start, LANES)]

    message = LANES // 2 + 1

    def add_from(d, g, t, slot):
        at = slot + t
        wait_for(prod.at[0], 0, message, z_recv.at[at])
        here = held(d, g, t)
        here[...] = here[...] + decode(code_in[at], top_in[at])

    def send_on(d, g, t):
        at = (d * groups + g) * tiles + t
        block = held(d, g, t)[...]
        top = top_of([block])
        top_out[at] = top
        code_out[at] = encode(block, top)
        for copy in z_copies(d, g, t):
            copy.start()

    for p in near:
        top_copy(p).start()

    def turn(k, carry):
        d, g = unit(k)
        u = d * groups + g
        start = pl.multiple_of((pairs * a_dev) + u * LANES, LANES)
        for t in range(tiles):
            codes = [
                encode(
                    prod[t, pl.ds(pl.multiple_of(start + q * a_dev, a_dev), a_dev), :],
                    peaks[pl.ds(u * per_tile + q, 1), :],
                )
                for q in range(per_tile)
            ]
            turned[u, t * LANES:(t + 1) * LANES, :] = jnp.concatenate(codes, axis=0).T
        for p in near:
            x_copy(u, p).start()

        @pl.when(k == 0)
        def _():
            for p in far + [1]:
                top_copy(p).start()

        for p in far + [1]:
            x_copy(u, p).start()
        return carry

    lax.fori_loop(0, units, turn, 0, unroll=2)

    gather(False)
    for i in range(n_parts):
        multiply(i, 0, None)

    piece = lax.broadcasted_iota(jnp.int32, (a_dev, LANES), 1) // a_dev

    def combine(k, carry):
        d, g = unit(k)
        u = d * groups + g
        inbox[u * n_row + row] = turned[u, pl.ds(pl.multiple_of(row * a_dev, a_dev), a_dev), :]
        first = jnp.where(d > col, 0, last)
        at_end = (d == 0) | (d == last)
        passes = (col != first) & (jnp.logical_not(at_end) | (jnp.abs(col - first) == 1))
        for i in range(tiles):
            t = lax.rem(own_tile + i, tiles)
            count = per_tile if i else per_tile - 1

            @pl.when(k == 0)
            def _(t=t, count=count):
                wait_for(x_tops, 0, count, t_recv.at[t])
                rows = jnp.concatenate([x_tops[t * per_tile + j] for j in range(per_tile)], axis=0)
                place = lax.broadcasted_iota(jnp.int32, rows.shape, 1) // wide % packed
                for m in range(packed):
                    only = jnp.where(place == m, rows, 0.0)
                    spread = only
                    for v in range(packed):
                        if v != m:
                            spread = spread + pltpu.roll(only, ((v - m) * wide) % LANES, 1)
                    x_wide[t, m] = spread

            wait_for(inbox, u * n_row, count, x_recv.at[u * tiles + t])
            parts = []
            for j in range(per_tile):
                source = t * per_tile + j
                parts.append(decode(inbox[u * n_row + source], x_wide[t, lax.rem(u, packed), pl.ds(j * n_rows + u // packed, 1), :]))
            sums = []
            for q in range(per_tile):
                merged = pltpu.roll(parts[0], (-q * a_dev) % LANES, 1) if q else parts[0]
                for j in range(1, per_tile):
                    shift = ((j - q) * a_dev) % LANES
                    moved = pltpu.roll(parts[j], shift, 1) if shift else parts[j]
                    merged = jnp.where(piece == j, moved, merged)
                sums.append(merged)
            here = held(d, g, t)
            here[...] = here[...] + jnp.concatenate(sums, axis=0)

            @pl.when(d != col)
            def _(t=t):
                @pl.when(passes)
                def _():
                    add_from(d, g, t, relay_slot(col, d, g))

                send_on(d, g, t)

        return carry

    lax.fori_loop(0, units, combine, 0)

    at_end = (col == 0) | (col == last)
    sources = jnp.where(at_end, last - 1, 2)

    def source_of(j):
        beside = jnp.where(j == 0, col - 1, col + 1)
        across = jnp.where(col == 0, j + 1, last - 1 - j)
        return jnp.where(at_end, across, beside)

    def collect(j, g):
        for i in range(tiles):
            t = lax.rem(own_tile + i, tiles)
            add_from(col, g, t, own_slot(source_of(j), col, g))

    def collect_all(j, carry):
        for g in range(groups):
            collect(j, g)
        return carry

    lax.fori_loop(0, sources - 1, collect_all, 0)
    for g in range(groups - 1):
        collect(sources - 1, g)
    for i in range(tiles):
        t = lax.rem(own_tile + i, tiles)
        add_from(col, groups - 1, t, own_slot(source_of(sources - 1), col, groups - 1))
        for a in range(a_dev):
            value = prod[t, pl.ds(col * (share * a_dev) + a, share, stride=a_dev), :]
            at = pl.multiple_of(a * width + t * LANES, LANES)
            out_ref[:, pl.ds(at, LANES)] = value.astype(out_ref.dtype)

    sent = (n_col - 1) * groups * tiles
    wait_for(x_tops, 0, n_row - 1, t_send)
    wait_for(inbox, 0, units * (n_row - 1), x_send)
    wait_for(prod.at[0], 0, sent * message, z_send)


def on_device(n_row, n_col, amplitudes, integrals, blocks):
    amplitudes = jnp.swapaxes(amplitudes, 1, 2)
    blocks = blocks.T
    depth, local = integrals.shape
    width = math.isqrt(local * n_row)
    a_dev = width // n_row
    pairs = blocks.shape[1] * OB * OB
    tiles = width // LANES
    share = pairs // n_col
    groups = share * a_dev // LANES
    n_parts = 2
    f32 = jnp.float32
    dma = pltpu.SemaphoreType.DMA
    units = n_col * groups
    slots = (2 * n_col - 3) * groups * tiles
    return pl.pallas_call(
        functools.partial(ladder_kernel, n_row, n_col, a_dev),
        out_shape=pltpu.VMEM((share, local), jnp.bfloat16),
        in_specs=[
            pl.BlockSpec(memory_space=pl.ANY),
            pl.BlockSpec(memory_space=pl.ANY),
            pl.BlockSpec(memory_space=pl.ANY),
        ],
        out_specs=pl.BlockSpec(memory_space=pltpu.VMEM),
        scratch_shapes=[
            pltpu.SMEM(blocks.shape, blocks.dtype),
            pltpu.VMEM(amplitudes.shape, amplitudes.dtype),
            pltpu.VMEM(integrals.shape, integrals.dtype),
            pltpu.VMEM((2 * pairs, depth), f32),
            pltpu.VMEM((tiles, 2 * pairs * a_dev, LANES), f32),
            pltpu.VMEM((units, width, LANES), jnp.int16),
            pltpu.VMEM((units * n_row, a_dev, LANES), jnp.int16),
            pltpu.VMEM((pairs, LANES), f32),
            pltpu.VMEM((units // PACKED, LANES), f32),
            pltpu.VMEM((n_row, units // PACKED, LANES), f32),
            pltpu.VMEM((tiles, PACKED, units // PACKED * LANES // a_dev, LANES), f32),
            pltpu.VMEM((units * tiles, LANES, LANES), jnp.int16),
            pltpu.VMEM((units * tiles, 1, LANES), f32),
            pltpu.VMEM((slots, LANES, LANES), jnp.int16),
            pltpu.VMEM((slots, 1, LANES), f32),
            dma(()),
            dma((4,)),
            dma((n_parts,)),
            dma(()),
            dma((units * tiles,)),
            dma(()),
            dma((tiles,)),
            dma(()),
            dma((slots,)),
        ],
        compiler_params=pltpu.CompilerParams(
            collective_id=0, has_side_effects=True, vmem_limit_bytes=VMEM - 4 * share * local * 2
        ),
    )(blocks, amplitudes, integrals)


def solution(mesh):
    return jax.shard_map(
        functools.partial(on_device, mesh.shape["row"], mesh.shape["col"]),
        mesh=mesh,
        in_specs=(P(None, None, "col"), P("col", "row"), P()),
        out_specs=P("col", "row"),
        check_vma=False,
    )
```

```python
import functools
import math

import jax
import jax.numpy as jnp
from jax import lax
from jax.experimental import pallas as pl
from jax.experimental.pallas import tpu as pltpu
from jax.sharding import PartitionSpec as P

OB = 2
LANES = 128
CODE = 32700.0
TINY = 1e-30
PACKED = 4
ROWS = 8
VMEM = 67043328


def ladder_kernel(
    n_row, n_col, a_dev,
    blocks_hbm, amp_hbm, int_hbm, out_ref,
    blocks, amp, ints, lhs, prod, turned, inbox, peaks, x_top, x_tops, x_wide,
    code_out, top_out, code_in, top_in,
    block_sem, amp_sem, int_sem, x_send, x_recv, t_send, t_recv, z_send, z_recv,
):
    row = lax.axis_index("row")
    col = lax.axis_index("col")
    pairs = lhs.shape[0] // 2
    width = a_dev * n_row
    tiles = width // LANES
    per_tile = LANES // a_dev
    share = pairs // n_col
    groups = share // per_tile
    units = n_col * groups
    occ = amp.shape[2]
    n_parts = int_sem.shape[0]
    part = ints.shape[1] // n_parts

    block_copy = pltpu.make_async_copy(blocks_hbm, blocks, block_sem)
    block_copy.start()
    amp_copies = []
    n_cuts = amp_sem.shape[0]
    planes = amp.shape[0] // n_cuts
    for i in range(n_cuts):
        cut = pl.ds(i * planes, planes if i < n_cuts - 1 else amp.shape[0] - i * planes)
        amp_copies.append(pltpu.make_async_copy(amp_hbm.at[cut], amp.at[cut], amp_sem.at[i]))
        amp_copies[i].start()
    int_copies = []
    for i in range(n_parts):
        cut = pl.ds(i * part, part)
        copy = pltpu.make_async_copy(int_hbm.at[:, cut], ints.at[:, cut], int_sem.at[i])
        int_copies.append(copy)

    barrier = pltpu.get_barrier_semaphore()

    def greet(p, carry):
        pl.semaphore_signal(barrier, inc=1, device_id={"row": lax.rem(row + p, n_row)})
        return carry

    lax.fori_loop(1, n_row, greet, 0)

    def greet_col(p, carry):
        pl.semaphore_signal(barrier, inc=1, device_id={"col": lax.rem(col + p, n_col)})
        return carry

    lax.fori_loop(1, n_col, greet_col, 0)

    amp_copies[0].wait()
    for copy in int_copies:
        copy.start()
    block_copy.wait()
    for copy in amp_copies[1:]:
        copy.wait()
    spot_row = lax.broadcasted_iota(jnp.int32, (ROWS, occ), 0)
    spot_col = lax.broadcasted_iota(jnp.int32, (ROWS, occ), 1)

    def take(spots, plane):
        hit = jnp.zeros((ROWS, occ), jnp.bool_)
        for at, column in spots:
            hit = hit | ((spot_row == at) & (spot_col == column))
        chosen = jnp.where(hit, 1.0, 0.0).astype(amp.dtype)
        return lax.dot_general(
            chosen, amp[plane], (((1,), (1,)), ((), ())), preferred_element_type=jnp.float32
        )

    per_rows = ROWS // (OB * OB)

    def gather(mirrored):
        for tile in range(pairs // ROWS):
            found = jnp.zeros((ROWS, lhs.shape[1]), jnp.float32)
            for k in range(per_rows):
                upper = blocks[0, tile * per_rows + k] * OB
                lower = blocks[1, tile * per_rows + k] * OB
                base = k * OB * OB
                for m in range(OB):
                    if mirrored:
                        found += take([(base + u * OB + m, upper + u) for u in range(OB)], lower + m)
                    else:
                        found += take([(base + m * OB + v, lower + v) for v in range(OB)], upper + m)
            at = (pairs if mirrored else 0) + tile * ROWS
            lhs[at:at + ROWS, :] = found

    gather(True)

    def multiply(i, first, peak):
        block = lhs[first:first + pairs, :].astype(jnp.bfloat16)

        def one(step, peak):
            a = i * (part // width) + step
            panel = ints[:, pl.ds(pl.multiple_of(a * width, width), width)]
            got = jnp.dot(block, panel, preferred_element_type=jnp.float32)
            for t in range(tiles):
                piece = got[:, t * LANES:(t + 1) * LANES]
                prod[t, pl.ds(first * a_dev + a, pairs, stride=a_dev), :] = piece
                if peak is not None:
                    peak = jnp.maximum(peak, jnp.abs(piece))
            return peak

        return lax.fori_loop(0, part // width, one, peak, unroll=16)

    peak = jnp.full((pairs, LANES), TINY, jnp.float32)
    for i in range(n_parts):
        int_copies[i].wait()
        peak = multiply(i, pairs, peak)

    peaks[...] = jnp.broadcast_to(jnp.max(peak, axis=1, keepdims=True), peaks.shape)
    n_rows = x_top.shape[0]
    packed = units // n_rows
    wide = a_dev // packed
    spot = lax.broadcasted_iota(jnp.int32, (n_rows, LANES), 1) // wide
    table = peaks[pl.ds(0, n_rows, stride=packed * per_tile), :]
    for m in range(packed):
        for q in range(per_tile):
            some = peaks[pl.ds(m * per_tile + q, n_rows, stride=packed * per_tile), :]
            table = jnp.where(spot == q * packed + m, some, table)
    x_top[...] = table
    x_tops[row] = table

    pl.semaphore_wait(barrier, n_row + n_col - 2)

    last = n_col - 1
    lower = col < last - col
    from_end = jnp.where(lower, col, last - col)

    def unit(k):
        b = k // groups
        n = last - 1 - from_end
        inner = jnp.where(b < n + 2, n_col - b, b - 1 - n)
        inner = jnp.where(b == 0, 0, jnp.where(b == 1, last, inner))
        d = jnp.where(from_end == 0, last - b, inner)
        return jnp.where(lower, d, last - d), k % groups

    def partner(p):
        if n_row & (n_row - 1):
            return lax.rem(row + p, n_row)
        peer, bit = row, 1
        while bit < n_row:
            if p & bit:
                peer = peer + bit - 2 * bit * ((row // bit) % 2)
            bit *= 2
        return peer

    near = sorted(range(2, min(per_tile, n_row)), key=lambda p: (-bin(p // 2).count('1'), p))
    far = sorted(range(per_tile, n_row), key=lambda p: (-bin(p // 2).count('1'), p))
    own_tile = row // per_tile

    def x_copy(u, p):
        peer = partner(p)
        return pltpu.make_async_remote_copy(
            src_ref=turned.at[u, pl.ds(pl.multiple_of(peer * a_dev, a_dev), a_dev), :],
            dst_ref=inbox.at[u * n_row + row],
            send_sem=x_send,
            recv_sem=x_recv.at[u * tiles + own_tile],
            device_id={"row": peer},
        )

    def top_copy(p):
        return pltpu.make_async_remote_copy(
            src_ref=x_top,
            dst_ref=x_tops.at[row],
            send_sem=t_send,
            recv_sem=t_recv.at[own_tile],
            device_id={"row": partner(p)},
        )

    def wait_for(ref, start, count, sem):
        landed = ref.at[pl.ds(start, count)]
        pltpu.make_async_copy(landed, landed, sem).wait()

    def encode(block, top):
        return jnp.round(block * (CODE / top)).astype(jnp.int32).astype(jnp.int16)

    def decode(code, top):
        return code.astype(jnp.int32).astype(jnp.float32) * (top * (1.0 / CODE))

    def top_of(blocks):
        top = jnp.abs(blocks[0])
        for block in blocks[1:]:
            top = jnp.maximum(top, jnp.abs(block))
        return jnp.maximum(jnp.max(top, axis=0, keepdims=True), TINY)

    def relay_slot(at, d, g):
        return (jnp.where(d < at, d, d - 1) * groups + g) * tiles

    def own_slot(source, d, g):
        at_end = (d == 0) | (d == last)
        which = jnp.where(at_end, source - 1, jnp.where(source < d, 0, 1))
        return ((last + which) * groups + g) * tiles

    def z_copies(d, g, t):
        u = d * groups + g
        straight = ((d == 0) & (col < last)) | ((d == last) & (col > 0))
        to = jnp.where(straight, d, jnp.where(d > col, col + 1, col - 1))
        slot = jnp.where(to == d, own_slot(col, d, g), relay_slot(to, d, g)) + t
        return [
            pltpu.make_async_remote_copy(
                src_ref=src.at[u * tiles + t], dst_ref=dst.at[slot],
                send_sem=z_send, recv_sem=z_recv.at[slot],
                device_id={"col": to},
            )
            for src, dst in ((top_out, top_in), (code_out, code_in))
        ]

    def held(d, g, t):
        start = pl.multiple_of(d * (share * a_dev) + g * LANES, LANES)
        return prod.at[t, pl.ds(start, LANES)]

    message = LANES // 2 + 1

    def add_from(d, g, t, slot):
        at = slot + t
        wait_for(prod.at[0], 0, message, z_recv.at[at])
        here = held(d, g, t)
        here[...] = here[...] + decode(code_in[at], top_in[at])

    def send_on(d, g, t):
        at = (d * groups + g) * tiles + t
        block = held(d, g, t)[...]
        top = top_of([block])
        top_out[at] = top
        code_out[at] = encode(block, top)
        for copy in z_copies(d, g, t):
            copy.start()

    for p in near:
        top_copy(p).start()

    def turn(k, carry):
        d, g = unit(k)
        u = d * groups + g
        start = pl.multiple_of((pairs * a_dev) + u * LANES, LANES)
        for t in range(tiles):
            codes = [
                encode(
                    prod[t, pl.ds(pl.multiple_of(start + q * a_dev, a_dev), a_dev), :],
                    peaks[pl.ds(u * per_tile + q, 1), :],
                )
                for q in range(per_tile)
            ]
            turned[u, t * LANES:(t + 1) * LANES, :] = jnp.concatenate(codes, axis=0).T
        for p in near:
            x_copy(u, p).start()

        @pl.when(k == 0)
        def _():
            for p in far + [1]:
                top_copy(p).start()

        for p in far + [1]:
            x_copy(u, p).start()
        return carry

    lax.fori_loop(0, units // 2, turn, 0, unroll=2)

    gather(False)
    for i in range(n_parts):
        multiply(i, 0, None)

    piece = lax.broadcasted_iota(jnp.int32, (a_dev, LANES), 1) // a_dev

    def combine(k, carry):
        d, g = unit(k)
        u = d * groups + g
        inbox[u * n_row + row] = turned[u, pl.ds(pl.multiple_of(row * a_dev, a_dev), a_dev), :]
        first = jnp.where(d > col, 0, last)
        at_end = (d == 0) | (d == last)
        passes = (col != first) & (jnp.logical_not(at_end) | (jnp.abs(col - first) == 1))
        for i in range(tiles):
            t = lax.rem(own_tile + i, tiles)
            count = per_tile if i else per_tile - 1

            @pl.when(k == 0)
            def _(t=t, count=count):
                wait_for(x_tops, 0, count, t_recv.at[t])
                rows = jnp.concatenate([x_tops[t * per_tile + j] for j in range(per_tile)], axis=0)
                place = lax.broadcasted_iota(jnp.int32, rows.shape, 1) // wide % packed
                for m in range(packed):
                    only = jnp.where(place == m, rows, 0.0)
                    spread = only
                    for v in range(packed):
                        if v != m:
                            spread = spread + pltpu.roll(only, ((v - m) * wide) % LANES, 1)
                    x_wide[t, m] = spread

            wait_for(inbox, u * n_row, count, x_recv.at[u * tiles + t])
            parts = []
            for j in range(per_tile):
                source = t * per_tile + j
                parts.append(decode(inbox[u * n_row + source], x_wide[t, lax.rem(u, packed), pl.ds(j * n_rows + u // packed, 1), :]))
            sums = []
            for q in range(per_tile):
                merged = pltpu.roll(parts[0], (-q * a_dev) % LANES, 1) if q else parts[0]
                for j in range(1, per_tile):
                    shift = ((j - q) * a_dev) % LANES
                    moved = pltpu.roll(parts[j], shift, 1) if shift else parts[j]
                    merged = jnp.where(piece == j, moved, merged)
                sums.append(merged)
            here = held(d, g, t)
            here[...] = here[...] + jnp.concatenate(sums, axis=0)

            @pl.when(d != col)
            def _(t=t):
                @pl.when(passes)
                def _():
                    add_from(d, g, t, relay_slot(col, d, g))

                send_on(d, g, t)

        @pl.when(k < units // 2)
        def _():
            turn(k + units // 2, 0)

        return carry

    lax.fori_loop(0, units, combine, 0)

    at_end = (col == 0) | (col == last)
    sources = jnp.where(at_end, last - 1, 2)

    def source_of(j):
        beside = jnp.where(j == 0, col - 1, col + 1)
        across = jnp.where(col == 0, j + 1, last - 1 - j)
        return jnp.where(at_end, across, beside)

    def collect(j, g):
        for i in range(tiles):
            t = lax.rem(own_tile + i, tiles)
            add_from(col, g, t, own_slot(source_of(j), col, g))

    def collect_all(j, carry):
        for g in range(groups):
            collect(j, g)
        return carry

    lax.fori_loop(0, sources - 1, collect_all, 0)
    for g in range(groups - 1):
        collect(sources - 1, g)
    for i in range(tiles):
        t = lax.rem(own_tile + i, tiles)
        add_from(col, groups - 1, t, own_slot(source_of(sources - 1), col, groups - 1))
        for a in range(a_dev):
            value = prod[t, pl.ds(col * (share * a_dev) + a, share, stride=a_dev), :]
            at = pl.multiple_of(a * width + t * LANES, LANES)
            out_ref[:, pl.ds(at, LANES)] = value.astype(out_ref.dtype)

    sent = (n_col - 1) * groups * tiles
    wait_for(x_tops, 0, n_row - 1, t_send)
    wait_for(inbox, 0, units * (n_row - 1), x_send)
    wait_for(prod.at[0], 0, sent * message, z_send)


def on_device(n_row, n_col, amplitudes, integrals, blocks):
    amplitudes = jnp.swapaxes(amplitudes, 1, 2)
    blocks = blocks.T
    depth, local = integrals.shape
    width = math.isqrt(local * n_row)
    a_dev = width // n_row
    pairs = blocks.shape[1] * OB * OB
    tiles = width // LANES
    share = pairs // n_col
    groups = share * a_dev // LANES
    n_parts = 2
    f32 = jnp.float32
    dma = pltpu.SemaphoreType.DMA
    units = n_col * groups
    slots = (2 * n_col - 3) * groups * tiles
    return pl.pallas_call(
        functools.partial(ladder_kernel, n_row, n_col, a_dev),
        out_shape=pltpu.VMEM((share, local), jnp.bfloat16),
        in_specs=[
            pl.BlockSpec(memory_space=pl.ANY),
            pl.BlockSpec(memory_space=pl.ANY),
            pl.BlockSpec(memory_space=pl.ANY),
        ],
        out_specs=pl.BlockSpec(memory_space=pltpu.VMEM),
        scratch_shapes=[
            pltpu.SMEM(blocks.shape, blocks.dtype),
            pltpu.VMEM(amplitudes.shape, amplitudes.dtype),
            pltpu.VMEM(integrals.shape, integrals.dtype),
            pltpu.VMEM((2 * pairs, depth), f32),
            pltpu.VMEM((tiles, 2 * pairs * a_dev, LANES), f32),
            pltpu.VMEM((units, width, LANES), jnp.int16),
            pltpu.VMEM((units * n_row, a_dev, LANES), jnp.int16),
            pltpu.VMEM((pairs, LANES), f32),
            pltpu.VMEM((units // PACKED, LANES), f32),
            pltpu.VMEM((n_row, units // PACKED, LANES), f32),
            pltpu.VMEM((tiles, PACKED, units // PACKED * LANES // a_dev, LANES), f32),
            pltpu.VMEM((units * tiles, LANES, LANES), jnp.int16),
            pltpu.VMEM((units * tiles, 1, LANES), f32),
            pltpu.VMEM((slots, LANES, LANES), jnp.int16),
            pltpu.VMEM((slots, 1, LANES), f32),
            dma(()),
            dma((4,)),
            dma((n_parts,)),
            dma(()),
            dma((units * tiles,)),
            dma(()),
            dma((tiles,)),
            dma(()),
            dma((slots,)),
        ],
        compiler_params=pltpu.CompilerParams(
            collective_id=0, has_side_effects=True, vmem_limit_bytes=VMEM - 4 * share * local * 2
        ),
    )(blocks, amplitudes, integrals)


def solution(mesh):
    return jax.shard_map(
        functools.partial(on_device, mesh.shape["row"], mesh.shape["col"]),
        mesh=mesh,
        in_specs=(P(None, None, "col"), P("col", "row"), P()),
        out_specs=P("col", "row"),
        check_vma=False,
    )
```

```python
import functools
import math

import jax
import jax.numpy as jnp
from jax import lax
from jax.experimental import pallas as pl
from jax.experimental.pallas import tpu as pltpu
from jax.sharding import PartitionSpec as P

OB = 2
LANES = 128
CODE = 32700.0
TINY = 1e-30
PACKED = 4
ROWS = 8
VMEM = 67043328


def ladder_kernel(
    n_row, n_col, a_dev,
    blocks_hbm, amp_hbm, int_hbm, out_ref,
    blocks, amp, ints, lhs, prod, turned, inbox, peaks, x_top, x_tops, x_wide,
    code_out, top_out, code_in, top_in,
    block_sem, amp_sem, int_sem, x_send, x_recv, t_send, t_recv, z_send, z_recv,
):
    row = lax.axis_index("row")
    col = lax.axis_index("col")
    pairs = lhs.shape[0] // 2
    width = a_dev * n_row
    tiles = width // LANES
    per_tile = LANES // a_dev
    share = pairs // n_col
    groups = share // per_tile
    units = n_col * groups
    occ = amp.shape[2]
    n_parts = int_sem.shape[0]
    part = ints.shape[1] // n_parts

    block_copy = pltpu.make_async_copy(blocks_hbm, blocks, block_sem)
    block_copy.start()
    amp_copies = []
    n_cuts = amp_sem.shape[0]
    planes = amp.shape[0] // n_cuts
    for i in range(n_cuts):
        cut = pl.ds(i * planes, planes if i < n_cuts - 1 else amp.shape[0] - i * planes)
        amp_copies.append(pltpu.make_async_copy(amp_hbm.at[cut], amp.at[cut], amp_sem.at[i]))
        amp_copies[i].start()
    int_copies = []
    for i in range(n_parts):
        cut = pl.ds(i * part, part)
        copy = pltpu.make_async_copy(int_hbm.at[:, cut], ints.at[:, cut], int_sem.at[i])
        int_copies.append(copy)

    barrier = pltpu.get_barrier_semaphore()

    def greet(p, carry):
        pl.semaphore_signal(barrier, inc=1, device_id={"row": lax.rem(row + p, n_row)})
        return carry

    lax.fori_loop(1, n_row, greet, 0)

    def greet_col(p, carry):
        pl.semaphore_signal(barrier, inc=1, device_id={"col": lax.rem(col + p, n_col)})
        return carry

    lax.fori_loop(1, n_col, greet_col, 0)

    amp_copies[0].wait()
    for copy in int_copies:
        copy.start()
    block_copy.wait()
    for copy in amp_copies[1:]:
        copy.wait()
    spot_row = lax.broadcasted_iota(jnp.int32, (ROWS, occ), 0)
    spot_col = lax.broadcasted_iota(jnp.int32, (ROWS, occ), 1)

    def take(spots, plane):
        hit = jnp.zeros((ROWS, occ), jnp.bool_)
        for at, column in spots:
            hit = hit | ((spot_row == at) & (spot_col == column))
        chosen = jnp.where(hit, 1.0, 0.0).astype(amp.dtype)
        return lax.dot_general(
            chosen, amp[plane], (((1,), (1,)), ((), ())), preferred_element_type=jnp.float32
        )

    per_rows = ROWS // (OB * OB)

    def gather(mirrored):
        for tile in range(pairs // ROWS):
            found = jnp.zeros((ROWS, lhs.shape[1]), jnp.float32)
            for k in range(per_rows):
                upper = blocks[0, tile * per_rows + k] * OB
                lower = blocks[1, tile * per_rows + k] * OB
                base = k * OB * OB
                for m in range(OB):
                    if mirrored:
                        found += take([(base + u * OB + m, upper + u) for u in range(OB)], lower + m)
                    else:
                        found += take([(base + m * OB + v, lower + v) for v in range(OB)], upper + m)
            at = (pairs if mirrored else 0) + tile * ROWS
            lhs[at:at + ROWS, :] = found

    gather(True)

    def multiply(i, first, peak):
        block = lhs[first:first + pairs, :].astype(jnp.bfloat16)

        def one(step, peak):
            a = i * (part // width) + step
            panel = ints[:, pl.ds(pl.multiple_of(a * width, width), width)]
            got = jnp.dot(block, panel, preferred_element_type=jnp.float32)
            for t in range(tiles):
                piece = got[:, t * LANES:(t + 1) * LANES]
                prod[t, pl.ds(first * a_dev + a, pairs, stride=a_dev), :] = piece
                if peak is not None:
                    peak = jnp.maximum(peak, jnp.abs(piece))
            return peak

        return lax.fori_loop(0, part // width, one, peak, unroll=16)

    peak = jnp.full((pairs, LANES), TINY, jnp.float32)
    for i in range(n_parts):
        int_copies[i].wait()
        peak = multiply(i, pairs, peak)

    peaks[...] = jnp.broadcast_to(jnp.max(peak, axis=1, keepdims=True), peaks.shape)
    n_rows = x_top.shape[0]
    packed = units // n_rows
    wide = a_dev // packed
    spot = lax.broadcasted_iota(jnp.int32, (n_rows, LANES), 1) // wide
    table = peaks[pl.ds(0, n_rows, stride=packed * per_tile), :]
    for m in range(packed):
        for q in range(per_tile):
            some = peaks[pl.ds(m * per_tile + q, n_rows, stride=packed * per_tile), :]
            table = jnp.where(spot == q * packed + m, some, table)
    x_top[...] = table
    x_tops[row] = table

    pl.semaphore_wait(barrier, n_row + n_col - 2)

    last = n_col - 1
    lower = col < last - col
    from_end = jnp.where(lower, col, last - col)

    def unit(k):
        b = k // groups
        n = last - 1 - from_end
        inner = jnp.where(b < n + 2, n_col - b, b - 1 - n)
        inner = jnp.where(b == 0, 0, jnp.where(b == 1, last, inner))
        d = jnp.where(from_end == 0, last - b, inner)
        return jnp.where(lower, d, last - d), k % groups

    def partner(p):
        if n_row & (n_row - 1):
            return lax.rem(row + p, n_row)
        peer, bit = row, 1
        while bit < n_row:
            if p & bit:
                peer = peer + bit - 2 * bit * ((row // bit) % 2)
            bit *= 2
        return peer

    near = sorted(range(2, min(per_tile, n_row)), key=lambda p: (-bin(p // 2).count('1'), p))
    far = sorted(range(per_tile, n_row), key=lambda p: (bin(p // 2).count('1'), p))
    own_tile = row // per_tile

    def x_copy(u, p):
        peer = partner(p)
        return pltpu.make_async_remote_copy(
            src_ref=turned.at[u, pl.ds(pl.multiple_of(peer * a_dev, a_dev), a_dev), :],
            dst_ref=inbox.at[u * n_row + row],
            send_sem=x_send,
            recv_sem=x_recv.at[u * tiles + own_tile],
            device_id={"row": peer},
        )

    def top_copy(p):
        return pltpu.make_async_remote_copy(
            src_ref=x_top,
            dst_ref=x_tops.at[row],
            send_sem=t_send,
            recv_sem=t_recv.at[own_tile],
            device_id={"row": partner(p)},
        )

    def wait_for(ref, start, count, sem):
        landed = ref.at[pl.ds(start, count)]
        pltpu.make_async_copy(landed, landed, sem).wait()

    def encode(block, top):
        return jnp.round(block * (CODE / top)).astype(jnp.int32).astype(jnp.int16)

    def decode(code, top):
        return code.astype(jnp.int32).astype(jnp.float32) * (top * (1.0 / CODE))

    def top_of(blocks):
        top = jnp.abs(blocks[0])
        for block in blocks[1:]:
            top = jnp.maximum(top, jnp.abs(block))
        return jnp.maximum(jnp.max(top, axis=0, keepdims=True), TINY)

    def relay_slot(at, d, g):
        return (jnp.where(d < at, d, d - 1) * groups + g) * tiles

    def own_slot(source, d, g):
        at_end = (d == 0) | (d == last)
        which = jnp.where(at_end, source - 1, jnp.where(source < d, 0, 1))
        return ((last + which) * groups + g) * tiles

    def z_copies(d, g, t):
        u = d * groups + g
        straight = ((d == 0) & (col < last)) | ((d == last) & (col > 0))
        to = jnp.where(straight, d, jnp.where(d > col, col + 1, col - 1))
        slot = jnp.where(to == d, own_slot(col, d, g), relay_slot(to, d, g)) + t
        return [
            pltpu.make_async_remote_copy(
                src_ref=src.at[u * tiles + t], dst_ref=dst.at[slot],
                send_sem=z_send, recv_sem=z_recv.at[slot],
                device_id={"col": to},
            )
            for src, dst in ((top_out, top_in), (code_out, code_in))
        ]

    def held(d, g, t):
        start = pl.multiple_of(d * (share * a_dev) + g * LANES, LANES)
        return prod.at[t, pl.ds(start, LANES)]

    message = LANES // 2 + 1

    def add_from(d, g, t, slot):
        at = slot + t
        wait_for(prod.at[0], 0, message, z_recv.at[at])
        here = held(d, g, t)
        here[...] = here[...] + decode(code_in[at], top_in[at])

    def send_on(d, g, t):
        at = (d * groups + g) * tiles + t
        block = held(d, g, t)[...]
        top = top_of([block])
        top_out[at] = top
        code_out[at] = encode(block, top)
        for copy in z_copies(d, g, t):
            copy.start()

    for p in near:
        top_copy(p).start()

    def turn(k, carry):
        d, g = unit(k)
        u = d * groups + g
        start = pl.multiple_of((pairs * a_dev) + u * LANES, LANES)
        for t in range(tiles):
            codes = [
                encode(
                    prod[t, pl.ds(pl.multiple_of(start + q * a_dev, a_dev), a_dev), :],
                    peaks[pl.ds(u * per_tile + q, 1), :],
                )
                for q in range(per_tile)
            ]
            turned[u, t * LANES:(t + 1) * LANES, :] = jnp.concatenate(codes, axis=0).T
        for p in near:
            x_copy(u, p).start()

        @pl.when(k == 0)
        def _():
            for p in far + [1]:
                top_copy(p).start()

        for p in far + [1]:
            x_copy(u, p).start()
        return carry

    lax.fori_loop(0, units // 2, turn, 0, unroll=2)

    gather(False)
    for i in range(n_parts):
        multiply(i, 0, None)

    piece = lax.broadcasted_iota(jnp.int32, (a_dev, LANES), 1) // a_dev

    def combine(k, carry):
        d, g = unit(k)
        u = d * groups + g
        inbox[u * n_row + row] = turned[u, pl.ds(pl.multiple_of(row * a_dev, a_dev), a_dev), :]
        first = jnp.where(d > col, 0, last)
        at_end = (d == 0) | (d == last)
        passes = (col != first) & (jnp.logical_not(at_end) | (jnp.abs(col - first) == 1))
        for i in range(tiles):
            t = lax.rem(own_tile + i, tiles)
            count = per_tile if i else per_tile - 1

            @pl.when(k == 0)
            def _(t=t, count=count):
                wait_for(x_tops, 0, count, t_recv.at[t])
                rows = jnp.concatenate([x_tops[t * per_tile + j] for j in range(per_tile)], axis=0)
                place = lax.broadcasted_iota(jnp.int32, rows.shape, 1) // wide % packed
                for m in range(packed):
                    only = jnp.where(place == m, rows, 0.0)
                    spread = only
                    for v in range(packed):
                        if v != m:
                            spread = spread + pltpu.roll(only, ((v - m) * wide) % LANES, 1)
                    x_wide[t, m] = spread

            wait_for(inbox, u * n_row, count, x_recv.at[u * tiles + t])
            parts = []
            for j in range(per_tile):
                source = t * per_tile + j
                parts.append(decode(inbox[u * n_row + source], x_wide[t, lax.rem(u, packed), pl.ds(j * n_rows + u // packed, 1), :]))
            sums = []
            for q in range(per_tile):
                merged = pltpu.roll(parts[0], (-q * a_dev) % LANES, 1) if q else parts[0]
                for j in range(1, per_tile):
                    shift = ((j - q) * a_dev) % LANES
                    moved = pltpu.roll(parts[j], shift, 1) if shift else parts[j]
                    merged = jnp.where(piece == j, moved, merged)
                sums.append(merged)
            here = held(d, g, t)
            here[...] = here[...] + jnp.concatenate(sums, axis=0)

            @pl.when(d != col)
            def _(t=t):
                @pl.when(passes)
                def _():
                    add_from(d, g, t, relay_slot(col, d, g))

                send_on(d, g, t)

        @pl.when(k < units // 2)
        def _():
            turn(k + units // 2, 0)

        return carry

    lax.fori_loop(0, units, combine, 0)

    at_end = (col == 0) | (col == last)
    sources = jnp.where(at_end, last - 1, 2)

    def source_of(j):
        beside = jnp.where(j == 0, col - 1, col + 1)
        across = jnp.where(col == 0, j + 1, last - 1 - j)
        return jnp.where(at_end, across, beside)

    def collect(j, g):
        for i in range(tiles):
            t = lax.rem(own_tile + i, tiles)
            add_from(col, g, t, own_slot(source_of(j), col, g))

    def collect_all(j, carry):
        for g in range(groups):
            collect(j, g)
        return carry

    lax.fori_loop(0, sources - 1, collect_all, 0)
    for g in range(groups - 1):
        collect(sources - 1, g)
    for i in range(tiles):
        t = lax.rem(own_tile + i, tiles)
        add_from(col, groups - 1, t, own_slot(source_of(sources - 1), col, groups - 1))
        for a in range(a_dev):
            value = prod[t, pl.ds(col * (share * a_dev) + a, share, stride=a_dev), :]
            at = pl.multiple_of(a * width + t * LANES, LANES)
            out_ref[:, pl.ds(at, LANES)] = value.astype(out_ref.dtype)

    sent = (n_col - 1) * groups * tiles
    wait_for(x_tops, 0, n_row - 1, t_send)
    wait_for(inbox, 0, units * (n_row - 1), x_send)
    wait_for(prod.at[0], 0, sent * message, z_send)


def on_device(n_row, n_col, amplitudes, integrals, blocks):
    amplitudes = jnp.swapaxes(amplitudes, 1, 2)
    blocks = blocks.T
    depth, local = integrals.shape
    width = math.isqrt(local * n_row)
    a_dev = width // n_row
    pairs = blocks.shape[1] * OB * OB
    tiles = width // LANES
    share = pairs // n_col
    groups = share * a_dev // LANES
    n_parts = 2
    f32 = jnp.float32
    dma = pltpu.SemaphoreType.DMA
    units = n_col * groups
    slots = (2 * n_col - 3) * groups * tiles
    return pl.pallas_call(
        functools.partial(ladder_kernel, n_row, n_col, a_dev),
        out_shape=pltpu.VMEM((share, local), jnp.bfloat16),
        in_specs=[
            pl.BlockSpec(memory_space=pl.ANY),
            pl.BlockSpec(memory_space=pl.ANY),
            pl.BlockSpec(memory_space=pl.ANY),
        ],
        out_specs=pl.BlockSpec(memory_space=pltpu.VMEM),
        scratch_shapes=[
            pltpu.SMEM(blocks.shape, blocks.dtype),
            pltpu.VMEM(amplitudes.shape, amplitudes.dtype),
            pltpu.VMEM(integrals.shape, integrals.dtype),
            pltpu.VMEM((2 * pairs, depth), f32),
            pltpu.VMEM((tiles, 2 * pairs * a_dev, LANES), f32),
            pltpu.VMEM((units, width, LANES), jnp.int16),
            pltpu.VMEM((units * n_row, a_dev, LANES), jnp.int16),
            pltpu.VMEM((pairs, LANES), f32),
            pltpu.VMEM((units // PACKED, LANES), f32),
            pltpu.VMEM((n_row, units // PACKED, LANES), f32),
            pltpu.VMEM((tiles, PACKED, units // PACKED * LANES // a_dev, LANES), f32),
            pltpu.VMEM((units * tiles, LANES, LANES), jnp.int16),
            pltpu.VMEM((units * tiles, 1, LANES), f32),
            pltpu.VMEM((slots, LANES, LANES), jnp.int16),
            pltpu.VMEM((slots, 1, LANES), f32),
            dma(()),
            dma((4,)),
            dma((n_parts,)),
            dma(()),
            dma((units * tiles,)),
            dma(()),
            dma((tiles,)),
            dma(()),
            dma((slots,)),
        ],
        compiler_params=pltpu.CompilerParams(
            collective_id=0, has_side_effects=True, vmem_limit_bytes=VMEM - 4 * share * local * 2
        ),
    )(blocks, amplitudes, integrals)


def solution(mesh):
    return jax.shard_map(
        functools.partial(on_device, mesh.shape["row"], mesh.shape["col"]),
        mesh=mesh,
        in_specs=(P(None, None, "col"), P("col", "row"), P()),
        out_specs=P("col", "row"),
        check_vma=False,
    )
```

```python
import functools
import math

import jax
import jax.numpy as jnp
from jax import lax
from jax.experimental import pallas as pl
from jax.experimental.pallas import tpu as pltpu
from jax.sharding import PartitionSpec as P

OB = 2
LANES = 128
CODE = 32700.0
TINY = 1e-30
PACKED = 4
ROWS = 8
VMEM = 67043328


def ladder_kernel(
    n_row, n_col, a_dev,
    blocks_hbm, amp_hbm, int_hbm, out_ref,
    blocks, amp, ints, lhs, prod, turned, inbox, peaks, x_top, x_tops, x_wide,
    code_out, top_out, code_in, top_in,
    block_sem, amp_sem, int_sem, x_send, x_recv, t_send, t_recv, z_send, z_recv,
):
    row = lax.axis_index("row")
    col = lax.axis_index("col")
    pairs = lhs.shape[0] // 2
    width = a_dev * n_row
    tiles = width // LANES
    per_tile = LANES // a_dev
    share = pairs // n_col
    groups = share // per_tile
    units = n_col * groups
    occ = amp.shape[2]
    n_parts = int_sem.shape[0]
    part = ints.shape[1] // n_parts

    block_copy = pltpu.make_async_copy(blocks_hbm, blocks, block_sem)
    block_copy.start()
    amp_copies = []
    n_cuts = amp_sem.shape[0]
    planes = amp.shape[0] // n_cuts
    for i in range(n_cuts):
        cut = pl.ds(i * planes, planes if i < n_cuts - 1 else amp.shape[0] - i * planes)
        amp_copies.append(pltpu.make_async_copy(amp_hbm.at[cut], amp.at[cut], amp_sem.at[i]))
        amp_copies[i].start()
    int_copies = []
    for i in range(n_parts):
        cut = pl.ds(i * part, part)
        copy = pltpu.make_async_copy(int_hbm.at[:, cut], ints.at[:, cut], int_sem.at[i])
        int_copies.append(copy)

    barrier = pltpu.get_barrier_semaphore()

    def greet(p, carry):
        pl.semaphore_signal(barrier, inc=1, device_id={"row": lax.rem(row + p, n_row)})
        return carry

    lax.fori_loop(1, n_row, greet, 0)

    def greet_col(p, carry):
        pl.semaphore_signal(barrier, inc=1, device_id={"col": lax.rem(col + p, n_col)})
        return carry

    lax.fori_loop(1, n_col, greet_col, 0)

    amp_copies[0].wait()
    for copy in int_copies:
        copy.start()
    block_copy.wait()
    for copy in amp_copies[1:]:
        copy.wait()
    spot_row = lax.broadcasted_iota(jnp.int32, (ROWS, occ), 0)
    spot_col = lax.broadcasted_iota(jnp.int32, (ROWS, occ), 1)

    def take(spots, plane):
        hit = jnp.zeros((ROWS, occ), jnp.bool_)
        for at, column in spots:
            hit = hit | ((spot_row == at) & (spot_col == column))
        chosen = jnp.where(hit, 1.0, 0.0).astype(amp.dtype)
        return lax.dot_general(
            chosen, amp[plane], (((1,), (1,)), ((), ())), preferred_element_type=jnp.float32
        )

    per_rows = ROWS // (OB * OB)

    def gather(mirrored):
        for tile in range(pairs // ROWS):
            found = jnp.zeros((ROWS, lhs.shape[1]), jnp.float32)
            for k in range(per_rows):
                upper = blocks[0, tile * per_rows + k] * OB
                lower = blocks[1, tile * per_rows + k] * OB
                base = k * OB * OB
                for m in range(OB):
                    if mirrored:
                        found += take([(base + u * OB + m, upper + u) for u in range(OB)], lower + m)
                    else:
                        found += take([(base + m * OB + v, lower + v) for v in range(OB)], upper + m)
            at = (pairs if mirrored else 0) + tile * ROWS
            lhs[at:at + ROWS, :] = found

    gather(True)

    def multiply(i, first, peak):
        block = lhs[first:first + pairs, :].astype(jnp.bfloat16)

        def one(step, peak):
            a = i * (part // width) + step
            panel = ints[:, pl.ds(pl.multiple_of(a * width, width), width)]
            got = jnp.dot(block, panel, preferred_element_type=jnp.float32)
            for t in range(tiles):
                piece = got[:, t * LANES:(t + 1) * LANES]
                prod[t, pl.ds(first * a_dev + a, pairs, stride=a_dev), :] = piece
                if peak is not None:
                    peak = jnp.maximum(peak, jnp.abs(piece))
            return peak

        return lax.fori_loop(0, part // width, one, peak, unroll=16)

    peak = jnp.full((pairs, LANES), TINY, jnp.float32)
    for i in range(n_parts):
        int_copies[i].wait()
        peak = multiply(i, pairs, peak)

    peaks[...] = jnp.broadcast_to(jnp.max(peak, axis=1, keepdims=True), peaks.shape)
    n_rows = x_top.shape[0]
    packed = units // n_rows
    wide = a_dev // packed
    spot = lax.broadcasted_iota(jnp.int32, (n_rows, LANES), 1) // wide
    table = peaks[pl.ds(0, n_rows, stride=packed * per_tile), :]
    for m in range(packed):
        for q in range(per_tile):
            some = peaks[pl.ds(m * per_tile + q, n_rows, stride=packed * per_tile), :]
            table = jnp.where(spot == q * packed + m, some, table)
    x_top[...] = table
    x_tops[row] = table

    pl.semaphore_wait(barrier, n_row + n_col - 2)

    last = n_col - 1
    lower = col < last - col
    from_end = jnp.where(lower, col, last - col)

    def unit(k):
        b = k // groups
        n = last - 1 - from_end
        inner = jnp.where(b < n + 2, n_col - b, b - 1 - n)
        inner = jnp.where(b == 0, 0, jnp.where(b == 1, last, inner))
        d = jnp.where(from_end == 0, last - b, inner)
        return jnp.where(lower, d, last - d), k % groups

    def partner(p):
        if n_row & (n_row - 1):
            return lax.rem(row + p, n_row)
        peer, bit = row, 1
        while bit < n_row:
            if p & bit:
                peer = peer + bit - 2 * bit * ((row // bit) % 2)
            bit *= 2
        return peer

    near = sorted(range(2, min(per_tile, n_row)), key=lambda p: (-bin(p // 2).count('1'), p))
    far = sorted(range(per_tile, n_row), key=lambda p: (bin(p // 2).count('1'), p))
    own_tile = row // per_tile

    def x_copy(u, p):
        peer = partner(p)
        return pltpu.make_async_remote_copy(
            src_ref=turned.at[u, pl.ds(pl.multiple_of(peer * a_dev, a_dev), a_dev), :],
            dst_ref=inbox.at[u * n_row + row],
            send_sem=x_send,
            recv_sem=x_recv.at[u * tiles + own_tile],
            device_id={"row": peer},
        )

    def top_copy(p):
        return pltpu.make_async_remote_copy(
            src_ref=x_top,
            dst_ref=x_tops.at[row],
            send_sem=t_send,
            recv_sem=t_recv.at[own_tile],
            device_id={"row": partner(p)},
        )

    def wait_for(ref, start, count, sem):
        landed = ref.at[pl.ds(start, count)]
        pltpu.make_async_copy(landed, landed, sem).wait()

    def encode(block, top):
        return jnp.round(block * (CODE / top)).astype(jnp.int32).astype(jnp.int16)

    def decode(code, top):
        return code.astype(jnp.int32).astype(jnp.float32) * (top * (1.0 / CODE))

    def top_of(blocks):
        top = jnp.abs(blocks[0])
        for block in blocks[1:]:
            top = jnp.maximum(top, jnp.abs(block))
        return jnp.maximum(jnp.max(top, axis=0, keepdims=True), TINY)

    def relay_slot(at, d, g):
        return (jnp.where(d < at, d, d - 1) * groups + g) * tiles

    def own_slot(source, d, g):
        at_end = (d == 0) | (d == last)
        which = jnp.where(at_end, source - 1, jnp.where(source < d, 0, 1))
        return ((last + which) * groups + g) * tiles

    def z_copies(d, g, t):
        u = d * groups + g
        straight = ((d == 0) & (col < last)) | ((d == last) & (col > 0))
        to = jnp.where(straight, d, jnp.where(d > col, col + 1, col - 1))
        slot = jnp.where(to == d, own_slot(col, d, g), relay_slot(to, d, g)) + t
        return [
            pltpu.make_async_remote_copy(
                src_ref=src.at[u * tiles + t], dst_ref=dst.at[slot],
                send_sem=z_send, recv_sem=z_recv.at[slot],
                device_id={"col": to},
            )
            for src, dst in ((top_out, top_in), (code_out, code_in))
        ]

    def held(d, g, t):
        start = pl.multiple_of(d * (share * a_dev) + g * LANES, LANES)
        return prod.at[t, pl.ds(start, LANES)]

    message = LANES // 2 + 1

    def add_from(d, g, t, slot):
        at = slot + t
        wait_for(prod.at[0], 0, message, z_recv.at[at])
        here = held(d, g, t)
        here[...] = here[...] + decode(code_in[at], top_in[at])

    def send_on(d, g, t):
        at = (d * groups + g) * tiles + t
        block = held(d, g, t)[...]
        top = top_of([block])
        top_out[at] = top
        code_out[at] = encode(block, top)
        for copy in z_copies(d, g, t):
            copy.start()

    for p in near:
        top_copy(p).start()

    def turn(k, carry):
        d, g = unit(k)
        u = d * groups + g
        start = pl.multiple_of((pairs * a_dev) + u * LANES, LANES)
        for t in range(tiles):
            codes = [
                encode(
                    prod[t, pl.ds(pl.multiple_of(start + q * a_dev, a_dev), a_dev), :],
                    peaks[pl.ds(u * per_tile + q, 1), :],
                )
                for q in range(per_tile)
            ]
            turned[u, t * LANES:(t + 1) * LANES, :] = jnp.concatenate(codes, axis=0).T
        for p in near:
            x_copy(u, p).start()

        @pl.when(k == 0)
        def _():
            for p in far + [1]:
                top_copy(p).start()

        for p in far + [1]:
            x_copy(u, p).start()
        return carry

    lax.fori_loop(0, units // 2, turn, 0, unroll=2)

    gather(False)
    for i in range(n_parts):
        multiply(i, 0, None)

    piece = lax.broadcasted_iota(jnp.int32, (a_dev, LANES), 1) // a_dev

    def combine(k, carry):
        d, g = unit(k)
        u = d * groups + g
        inbox[u * n_row + row] = turned[u, pl.ds(pl.multiple_of(row * a_dev, a_dev), a_dev), :]
        first = jnp.where(d > col, 0, last)
        at_end = (d == 0) | (d == last)
        passes = (col != first) & (jnp.logical_not(at_end) | (jnp.abs(col - first) == 1))
        for i in range(tiles):
            t = lax.rem(own_tile + i, tiles)
            count = per_tile if i else per_tile - 1

            @pl.when(k == 0)
            def _(t=t, count=count):
                wait_for(x_tops, 0, count, t_recv.at[t])
                rows = jnp.concatenate([x_tops[t * per_tile + j] for j in range(per_tile)], axis=0)
                place = lax.broadcasted_iota(jnp.int32, rows.shape, 1) // wide % packed
                for m in range(packed):
                    only = jnp.where(place == m, rows, 0.0)
                    spread = only
                    for v in range(packed):
                        if v != m:
                            spread = spread + pltpu.roll(only, ((v - m) * wide) % LANES, 1)
                    x_wide[t, m] = spread

            wait_for(inbox, u * n_row, count, x_recv.at[u * tiles + t])
            parts = []
            for j in range(per_tile):
                source = t * per_tile + j
                parts.append(decode(inbox[u * n_row + source], x_wide[t, lax.rem(u, packed), pl.ds(j * n_rows + u // packed, 1), :]))
            sums = []
            for q in range(per_tile):
                merged = pltpu.roll(parts[0], (-q * a_dev) % LANES, 1) if q else parts[0]
                for j in range(1, per_tile):
                    shift = ((j - q) * a_dev) % LANES
                    moved = pltpu.roll(parts[j], shift, 1) if shift else parts[j]
                    merged = jnp.where(piece == j, moved, merged)
                sums.append(merged)
            here = held(d, g, t)
            here[...] = here[...] + jnp.concatenate(sums, axis=0)

            @pl.when(d != col)
            def _(t=t):
                @pl.when(passes)
                def _():
                    add_from(d, g, t, relay_slot(col, d, g))

                send_on(d, g, t)

        @pl.when(k < units // 2)
        def _():
            turn(k + units // 2, 0)

        return carry

    lax.fori_loop(0, units, combine, 0)

    at_end = (col == 0) | (col == last)
    sources = jnp.where(at_end, last - 1, 2)

    def source_of(j):
        beside = jnp.where(j == 0, col - 1, col + 1)
        across = jnp.where(col == 0, j + 1, last - 1 - j)
        return jnp.where(at_end, across, beside)

    def collect(j, g):
        for i in range(tiles):
            t = lax.rem(own_tile + i, tiles)
            add_from(col, g, t, own_slot(source_of(j), col, g))

    def collect_all(j, carry):
        for g in range(groups):
            collect(j, g)
        return carry

    lax.fori_loop(0, sources - 1, collect_all, 0)
    for g in range(groups - 1):
        collect(sources - 1, g)
    for i in range(tiles):
        t = lax.rem(own_tile + i, tiles)
        add_from(col, groups - 1, t, own_slot(source_of(sources - 1), col, groups - 1))
        for a in range(a_dev):
            value = prod[t, pl.ds(col * (share * a_dev) + a, share, stride=a_dev), :]
            at = pl.multiple_of(a * width + t * LANES, LANES)
            out_ref[:, pl.ds(at, LANES)] = value.astype(out_ref.dtype)

    sent = (n_col - 1) * groups * tiles
    wait_for(x_tops, 0, n_row - 1, t_send)
    wait_for(inbox, 0, units * (n_row - 1), x_send)
    wait_for(prod.at[0], 0, sent * message, z_send)


def on_device(n_row, n_col, amplitudes, integrals, blocks):
    amplitudes = jnp.swapaxes(amplitudes, 1, 2)
    blocks = blocks.T
    depth, local = integrals.shape
    width = math.isqrt(local * n_row)
    a_dev = width // n_row
    pairs = blocks.shape[1] * OB * OB
    tiles = width // LANES
    share = pairs // n_col
    groups = share * a_dev // LANES
    n_parts = 2
    f32 = jnp.float32
    dma = pltpu.SemaphoreType.DMA
    units = n_col * groups
    slots = (2 * n_col - 3) * groups * tiles
    return pl.pallas_call(
        functools.partial(ladder_kernel, n_row, n_col, a_dev),
        out_shape=pltpu.VMEM((share, local), jnp.bfloat16),
        in_specs=[
            pl.BlockSpec(memory_space=pl.ANY),
            pl.BlockSpec(memory_space=pl.ANY),
            pl.BlockSpec(memory_space=pl.ANY),
        ],
        out_specs=pl.BlockSpec(memory_space=pltpu.VMEM),
        scratch_shapes=[
            pltpu.SMEM(blocks.shape, blocks.dtype),
            pltpu.VMEM(amplitudes.shape, amplitudes.dtype),
            pltpu.VMEM(integrals.shape, integrals.dtype),
            pltpu.VMEM((2 * pairs, depth), f32),
            pltpu.VMEM((tiles, 2 * pairs * a_dev, LANES), f32),
            pltpu.VMEM((units, width, LANES), jnp.int16),
            pltpu.VMEM((units * n_row, a_dev, LANES), jnp.int16),
            pltpu.VMEM((pairs, LANES), f32),
            pltpu.VMEM((units // PACKED, LANES), f32),
            pltpu.VMEM((n_row, units // PACKED, LANES), f32),
            pltpu.VMEM((tiles, PACKED, units // PACKED * LANES // a_dev, LANES), f32),
            pltpu.VMEM((units * tiles, LANES, LANES), jnp.int16),
            pltpu.VMEM((units * tiles, 1, LANES), f32),
            pltpu.VMEM((slots, LANES, LANES), jnp.int16),
            pltpu.VMEM((slots, 1, LANES), f32),
            dma(()),
            dma((2,)),
            dma((n_parts,)),
            dma(()),
            dma((units * tiles,)),
            dma(()),
            dma((tiles,)),
            dma(()),
            dma((slots,)),
        ],
        compiler_params=pltpu.CompilerParams(
            collective_id=0, has_side_effects=True, vmem_limit_bytes=VMEM - 4 * share * local * 2
        ),
    )(blocks, amplitudes, integrals)


def solution(mesh):
    return jax.shard_map(
        functools.partial(on_device, mesh.shape["row"], mesh.shape["col"]),
        mesh=mesh,
        in_specs=(P(None, None, "col"), P("col", "row"), P()),
        out_specs=P("col", "row"),
        check_vma=False,
    )
```
